32 devices in a mesh: fsdp: 8 (over y, x, core), tensor: 4 (over z).
Axes of the slice: x: 2, y: 2, z: 4, core: 2. Of those that a mesh axis runs over, the one named last changes fastest.
Arguments:
- tokens: bfloat16 [2, 8, 1024, 768], P(None, 'fsdp', 'tensor'), may hold values from -6 to 6
- lengths: int32 [2, 8], P(None, 'fsdp'), may hold values from 256 to 1024, as said below
- cotangent: bfloat16 [2, 8, 1024, 768], P(None, 'fsdp', 'tensor'), may hold values from -6 to 6
- query_proj: bfloat16 [768, 768], P('fsdp', 'tensor'), may hold values from -0.3125 to 0.3125
- key_proj: bfloat16 [768, 768], P('fsdp', 'tensor'), may hold values from -0.3125 to 0.3125
- value_proj: bfloat16 [768, 768], P('fsdp', 'tensor'), may hold values from -0.21875 to 0.21875
- output_proj: bfloat16 [768, 768], P('tensor', 'fsdp'), may hold values from -1.25 to 1.25
- expand_proj: bfloat16 [768, 3072], P('fsdp', 'tensor'), may hold values from -0.21875 to 0.21875
- shrink_proj: bfloat16 [3072, 768], P('tensor', 'fsdp'), may hold values from -0.109375 to 0.109375
- query_bias: bfloat16 [768], P(('tensor', 'fsdp')), may hold values from -3 to 3
- value_bias: bfloat16 [768], P(('tensor', 'fsdp')), may hold values from -3 to 3
- expand_bias: bfloat16 [3072], P(('tensor', 'fsdp')), may hold values from -3 to 3
- output_bias: bfloat16 [768], P('fsdp'), may hold values from -3 to 3
- attn_gain: bfloat16 [768], P('fsdp'), may hold values from 0.25 to 1.75
- attn_shift: bfloat16 [768], P('fsdp'), may hold values from -2 to 2
- shrink_bias: bfloat16 [768], P('fsdp'), may hold values from -3 to 3
- ffn_gain: bfloat16 [768], P('fsdp'), may hold values from 0.25 to 1.75
- ffn_shift: bfloat16 [768], P('fsdp'), may hold values from -2 to 2
Outputs:
- layer_out: bfloat16 [2, 8, 1024, 768], P(None, 'fsdp', 'tensor')
- input_grad: float32 [2, 8, 1024, 768], P(None, 'fsdp', 'tensor')
- grad_query: float32 [768, 768], P('fsdp', 'tensor')
- grad_key: float32 [768, 768], P('fsdp', 'tensor')
- grad_value: float32 [768, 768], P('fsdp', 'tensor')
- grad_output: float32 [768, 768], P('tensor', 'fsdp')
- grad_expand: float32 [768, 3072], P('fsdp', 'tensor')
- grad_shrink: float32 [3072, 768], P('tensor', 'fsdp')
- bgrad_query: float32 [768], P(('tensor', 'fsdp'))
- bgrad_value: float32 [768], P(('tensor', 'fsdp'))
- bgrad_expand: float32 [3072], P(('tensor', 'fsdp'))
- bgrad_output: float32 [768], P(('fsdp', 'tensor'))
- ggrad_attn: float32 [768], P(('fsdp', 'tensor'))
- sgrad_attn: float32 [768], P(('fsdp', 'tensor'))
- bgrad_shrink: float32 [768], P(('fsdp', 'tensor'))
- ggrad_ffn: float32 [768], P(('fsdp', 'tensor'))
- sgrad_ffn: float32 [768], P(('fsdp', 'tensor'))
The draws below stay inside these ranges and needn't reach their ends.
Inputs may be any that keep to these rules, and one draw needn't show every extreme that they name: Sequence (m, s) holds live tokens in its first lengths[m, s] slots and padding after them. Some sequence fills all 1024 slots and some has exactly 256.
All inputs are finite; a program needn't handle non-finite values.
Results may differ from the reference program's by a relative error of at most 0.015.
Values may be sent and summed in bfloat16 or wider, within the bound.
No kernel may reach another device: no remote copies, remote signals or barrier semaphores. Data moves between devices by JAX's collectives and lax.ppermute only.
A program may use at most 128 MiB of HBM per device.

```python
import jax
import jax.numpy as jnp
from jax import lax

D = 768
HEADS = 12
HD = 64
FF = 3072
SLOTS = 1024
LMIN = 256
MICRO = 2
SEQS = 8


def draw_lengths(key, part):
    number = MICRO * SEQS
    first, second, third = jax.random.split(key, 3)
    drawn = jax.random.randint(first, (number,), LMIN, SLOTS + 1)
    longest = jax.random.randint(second, (), 0, number)
    shortest = (longest + 1 + jax.random.randint(third, (), 0, number - 1)) % number
    places = jnp.arange(number)
    drawn = jnp.where(places == longest, SLOTS, drawn)
    drawn = jnp.where(places == shortest, LMIN, drawn)
    return drawn.reshape(MICRO, SEQS).astype(jnp.int32)


def with_spikes(values, own_key, source, target, shards_of, factor):
    owner, partner = [(jnp.arange(values.shape[axis_at]) // (values.shape[axis_at] // shards_of)).reshape([-1 if axis == axis_at else 1 for axis in range(values.ndim)]) for axis_at in (source, target)]
    chosen = jax.random.permutation(own_key, shards_of)[partner]
    strong = (owner == chosen) | (owner == (partner + shards_of // 2) % shards_of)
    return jnp.where(strong, factor * values, values)


def block_levels(stream_key, extent, cuts, low, largest):
    factor_of = 1.0
    for position, parts in cuts:
        draws = jax.random.uniform(jax.random.fold_in(jax.random.fold_in(stream_key, 6), position), (parts,), jnp.float32, low / len(cuts), largest / len(cuts))
        factor_of = factor_of * jnp.repeat(jnp.exp(draws), extent[position] // parts).reshape((-1,) + (1,) * (len(extent) - 1 - position))
    return factor_of


def normal_values(key, shape, scale, bound, cuts=(), dtype=jnp.bfloat16):
    values = scale * jax.random.normal(key, shape, jnp.float32)
    if cuts:
        values = values * block_levels(key, shape, cuts, -0.22, 0.18)
    return jnp.clip(values, -bound, bound).astype(dtype)


def gaussian_with(stream_key, shape, deviation, reach, pieces, heavy, held_as=jnp.bfloat16):
    array = deviation * jax.random.normal(stream_key, shape, jnp.float32)
    if pieces:
        array = array * block_levels(stream_key, shape, pieces, -0.22, 0.18)
    return jnp.clip(with_spikes(array, jax.random.fold_in(stream_key, 3), *heavy), -reach, reach).astype(held_as)


def setup_inputs(seed: int = 0) -> dict:
    key_list = jax.random.split(jax.random.key(seed), 19)
    return {
        "tokens": normal_values(key_list[0], (MICRO, SEQS, SLOTS, D), 1.0, 6.0, ((1, 8), (2, 4))),
        "lengths": draw_lengths(jax.random.fold_in(key_list[18], 71), 0),
        "cotangent": gaussian_with(key_list[2], (MICRO, SEQS, SLOTS, D), 1.0, 6.0, ((1, 8), (2, 4)), (1, 3, 8, 2.0)),
        "query_proj": normal_values(key_list[3], (D, D), (D // 2) ** -0.5, 0.3125, ((0, 8), (1, 4))),
        "key_proj": normal_values(key_list[4], (D, D), (D // 2) ** -0.5, 0.3125, ((0, 8), (1, 4))),
        "value_proj": normal_values(key_list[5], (D, D), D ** -0.5, 0.21875, ((0, 8), (1, 4))),
        "output_proj": normal_values(key_list[6], (D, D), (D // 32) ** -0.5, 1.25, ((0, 4), (1, 8))),
        "expand_proj": normal_values(key_list[7], (D, FF), D ** -0.5, 0.21875, ((0, 8), (1, 4))),
        "shrink_proj": normal_values(key_list[8], (FF, D), FF ** -0.5, 0.109375, ((0, 4), (1, 8))),
        "query_bias": normal_values(key_list[9], (D,), 0.5, 3.0, ((0, 32),)),
        "value_bias": normal_values(key_list[10], (D,), 0.5, 3.0, ((0, 32),)),
        "expand_bias": normal_values(key_list[11], (FF,), 0.5, 3.0, ((0, 32),)),
        "output_bias": normal_values(key_list[12], (D,), 0.5, 3.0, ((0, 8),)),
        "attn_gain": jnp.clip(1.0 + 0.15 * jax.random.normal(key_list[13], (D,), jnp.float32), 0.25, 1.75).astype(jnp.bfloat16),
        "attn_shift": normal_values(key_list[14], (D,), 0.3, 2.0, ((0, 8),)),
        "shrink_bias": normal_values(key_list[15], (D,), 0.5, 3.0, ((0, 8),)),
        "ffn_gain": jnp.clip(1.0 + 0.15 * jax.random.normal(key_list[16], (D,), jnp.float32), 0.25, 1.75).astype(jnp.bfloat16),
        "ffn_shift": normal_values(key_list[17], (D,), 0.3, 2.0, ((0, 8),)),
    }


@jax.custom_vjp
def low(v):
    return lax.optimization_barrier(v.astype(jnp.bfloat16)).astype(jnp.float32)

@jax.custom_vjp
def low_back(v):
    return v

def low_keep(v):
    return (low(v), None)

def low_pass(kept, grad):
    return (grad,)

def back_keep(v):
    return (v, None)

def back_low(kept, grad):
    return (low(grad),)
low.defvjp(low_keep, low_pass)
low_back.defvjp(back_keep, back_low)
EPS = 1e-05
NEG = -1000000000.0

def hdot(left, right):
    return jnp.dot(left, right, precision=lax.Precision.HIGHEST, preferred_element_type=jnp.float32)

def normed_rows(summed, gain, shift):
    center = summed - lax.optimization_barrier(jnp.mean(summed, axis=-1, keepdims=True))
    spread = lax.optimization_barrier(jnp.mean(center * center, axis=-1, keepdims=True))
    return center * lax.rsqrt(spread + EPS) * gain + shift

def layer(params, rows, length):
    query_proj, key_proj, value_proj, output_proj, expand_proj, shrink_proj, query_bias, value_bias, expand_bias, output_bias, attn_gain, attn_shift, shrink_bias, ffn_gain, ffn_shift = params
    live = jnp.arange(SLOTS) < length
    query = low(low_back(hdot(rows, query_proj)) + query_bias).reshape(SLOTS, HEADS, HD)
    keys = low(low_back(hdot(rows, key_proj))).reshape(SLOTS, HEADS, HD)
    values = low(low_back(hdot(rows, value_proj)) + value_bias).reshape(SLOTS, HEADS, HD)
    scores = low_back(jnp.einsum('qhd,khd->hqk', query, keys, precision=lax.Precision.HIGHEST) * 0.125)
    scores = jnp.where(live[None, None, :], scores, NEG)
    probs = low(jax.nn.softmax(scores, axis=-1))
    attended = jnp.einsum('hqk,khd->qhd', probs, values, precision=lax.Precision.HIGHEST).reshape(SLOTS, D)
    attended = low(low_back(attended))
    first_sum = rows + low_back(hdot(attended, output_proj)) + output_bias
    normed = normed_rows(first_sum, attn_gain, attn_shift)
    upper = low_back(hdot(low(normed), expand_proj)) + expand_bias
    active = low(jax.nn.gelu(upper, approximate=False))
    second_sum = normed + low_back(hdot(active, shrink_proj)) + shrink_bias
    return normed_rows(second_sum, ffn_gain, ffn_shift)

def reference(tokens, lengths, cotangent, query_proj, key_proj, value_proj, output_proj, expand_proj, shrink_proj, query_bias, value_bias, expand_bias, output_bias, attn_gain, attn_shift, shrink_bias, ffn_gain, ffn_shift):
    params = tuple((p.astype(jnp.float32) for p in (query_proj, key_proj, value_proj, output_proj, expand_proj, shrink_proj, query_bias, value_bias, expand_bias, output_bias, attn_gain, attn_shift, shrink_bias, ffn_gain, ffn_shift)))
    inputs = tokens.reshape(MICRO * SEQS, SLOTS, D).astype(jnp.float32)
    arriving = cotangent.reshape(MICRO * SEQS, SLOTS, D).astype(jnp.float32)
    counts = lengths.reshape(MICRO * SEQS).astype(jnp.int32)

    def one_sequence(totals, item):
        rows, incoming, length = item
        result, pull = jax.vjp(lambda weights, values: layer(weights, values, length), params, rows)
        live = (jnp.arange(SLOTS) < length).astype(jnp.float32)
        grads, rows_grad = pull(incoming * live[:, None])
        totals = jax.tree.map(jnp.add, totals, grads)
        return (totals, (result.astype(jnp.bfloat16), rows_grad))
    zeros = jax.tree.map(jnp.zeros_like, params)
    totals, (results, rows_grads) = lax.scan(one_sequence, zeros, (inputs, arriving, counts))
    layer_out = results.reshape(MICRO, SEQS, SLOTS, D)
    input_grad = rows_grads.reshape(MICRO, SEQS, SLOTS, D)
    return (layer_out, input_grad, totals[0], totals[1], totals[2], totals[3], totals[4], totals[5], totals[6], totals[7], totals[8], totals[9], totals[10], totals[11], totals[12], totals[13], totals[14])
```

```python
import jax
import jax.numpy as jnp
from jax import lax
from jax.sharding import PartitionSpec as P

HD = 64
EPS = 1e-05
NEG = -1000000000.0
ROOT_HALF = 0.7071067811865476
DENSITY = 0.3989422804014327
BOTH = ("fsdp", "tensor")
LOW = jnp.bfloat16
FULL = jnp.float32


def contract(left, right, form):
    return jnp.einsum(form, left, right, preferred_element_type=FULL)


def normalize(summed):
    center = summed - jnp.mean(summed, axis=-1, keepdims=True)
    spread = jnp.mean(center * center, axis=-1, keepdims=True)
    inv_scale = lax.rsqrt(spread + EPS)
    return (center * inv_scale, inv_scale)


def norm_back(grad, gain, unit, inv_scale):
    scaled = grad * gain
    return inv_scale * (
        scaled
        - jnp.mean(scaled, axis=-1, keepdims=True)
        - unit * jnp.mean(scaled * unit, axis=-1, keepdims=True)
    )


def pick(value, where, own, axis):
    return jnp.concatenate(
        [
            lax.dynamic_slice_in_dim(value, where[n ^ own], 1, axis)
            for n in range(value.shape[axis])
        ],
        axis=axis,
    )


class Plan:
    def __init__(self):
        self.parts = lax.axis_size("tensor")
        self.owners = lax.axis_size("fsdp")
        self.place = lax.axis_index("tensor")
        self.owner = lax.axis_index("fsdp")
        self.core = self.owner % 2
        self.outer = self.owner // 2
        self.outers = self.owners // 2
        self.bits = [1 << n for n in range((self.outers - 1).bit_length())]

    def swap(self, value, bit):
        return lax.ppermute(value, "fsdp", [(n, n ^ bit) for n in range(self.owners)])

    def turn(self, value, by):
        n = self.parts
        return lax.ppermute(value, "tensor", [(i, (i + by) % n) for i in range(n)])

    def trade(self, turn, back):
        pairs = []
        half = self.parts // 2
        for owner in range(self.owners):
            for place in range(self.parts):
                micro = (place + turn) % 2
                there = (owner - owner % 2 + place // half) * self.parts + 2 * micro + owner % 2
                here = owner * self.parts + place
                pairs.append((there, here) if back else (here, there))
        return pairs

    def collect(self, value):
        return [
            lax.ppermute(
                lax.dynamic_index_in_dim(value, (self.place + turn) % 2, 0, False),
                BOTH,
                self.trade(turn, False),
            )
            for turn in range(2)
        ]

    def release(self, blocks):
        first, second = [
            lax.ppermute(block, BOTH, self.trade(turn, True)) for turn, block in enumerate(blocks)
        ]
        even = self.place % 2 == 0
        return jnp.stack([jnp.where(even, first, second), jnp.where(even, second, first)])

    def gather(self, shard):
        slices = [shard] + [self.turn(shard, by) for by in range(1, self.parts)]
        half = self.parts // 2
        whole = []
        for lot, bits in ((slices[:half], self.bits), (slices[half:], self.bits[::-1])):
            held = jnp.stack(lot)[None]
            order = [0]
            for bit in bits:
                held = jnp.concatenate([held, self.swap(held, 2 * bit)])
                order = order + [n ^ bit for n in order]
            other = self.swap(held, 1)
            where = jnp.array([order.index(n) for n in range(self.outers)])
            mine, other = pick(held, where, self.outer, 0), pick(other, where, self.outer, 0)
            first = jnp.where(self.core == 0, mine, other)
            second = jnp.where(self.core == 0, other, mine)
            joined = jnp.stack([first, second], axis=1)
            for n in range(half):
                whole.append(joined[:, :, n].reshape(-1, shard.shape[1]))
        return whole

    def reduce(self, terms):
        half = self.parts // 2
        rows = terms[0].shape[0] // self.owners
        total = None
        for first, bits in ((0, self.bits), (half, self.bits[::-1])):
            lot = jnp.stack([t.reshape(self.outers, 2, rows, -1) for t in terms[first : first + half]])
            lot = pick(lot, jnp.arange(self.outers), self.outer, 1)
            away = lax.dynamic_index_in_dim(lot, 1 - self.core, 2, False)
            kept = lax.dynamic_index_in_dim(lot, self.core, 2, False)
            kept = kept + self.swap(away.astype(LOW), 1).astype(FULL)
            names = list(range(self.outers))
            for bit in bits:
                stay = [i for i, n in enumerate(names) if not n & bit]
                leave = [names.index(names[i] ^ bit) for i in stay]
                away = jnp.concatenate([kept[:, i : i + 1] for i in leave], axis=1)
                here = jnp.concatenate([kept[:, i : i + 1] for i in stay], axis=1)
                kept = here + self.swap(away.astype(LOW), 2 * bit).astype(FULL)
                names = [names[i] for i in stay]
            kept = kept[:, 0]
            for n in range(half):
                by = first + n
                term = kept[n] if by == 0 else self.turn(kept[n].astype(LOW), -by).astype(FULL)
                total = term if total is None else total + term
        return total


def head_blocks(width):
    return width // HD


def attend_forward(query, keys, values, live):
    rows, width = query.shape
    heads = head_blocks(width)
    q = query.reshape(rows, heads, HD)
    k = keys.reshape(-1, heads, HD)
    v = values.reshape(-1, heads, HD)
    scores = contract(q, k, "qhd,khd->hqk") * 0.125
    scores = jnp.where(live[None, None, :], scores, NEG)
    top = jnp.max(scores, axis=-1, keepdims=True)
    raised = jnp.exp(scores - top)
    denom = jnp.sum(raised, axis=-1, keepdims=True)
    probs_low = (raised / denom).astype(LOW)
    attended = contract(probs_low, v, "hqk,khd->qhd").astype(LOW)
    return (attended.reshape(rows, width), top + jnp.log(denom))


def attend_backward(query, keys, values, live, log_total, grad):
    rows, width = query.shape
    heads = head_blocks(width)
    q = query.reshape(rows, heads, HD)
    g = grad.reshape(rows, heads, HD)
    k = keys.reshape(-1, heads, HD)
    v = values.reshape(-1, heads, HD)
    scores = contract(q, k, "qhd,khd->hqk") * 0.125
    scores = jnp.where(live[None, None, :], scores, NEG)
    probs = jnp.exp(scores - log_total)
    prob_grad = contract(g, v, "qhd,khd->hqk")
    inner = jnp.sum(probs * prob_grad, axis=-1, keepdims=True)
    score_grad = (probs * (prob_grad - inner)).astype(LOW)
    query_grad = contract(score_grad, k, "hqk,khd->qhd") * 0.125
    key_grad = contract(score_grad, q, "hqk,qhd->khd") * 0.125
    value_grad = contract(probs.astype(LOW), g, "hqk,qhd->khd")
    return (
        query_grad.reshape(rows, width),
        key_grad.reshape(-1, width),
        value_grad.reshape(-1, width),
    )


def column(vector, rows):
    return jnp.pad(vector, (0, rows - vector.shape[0]))[:, None]


def shards(
    tokens, lengths, cotangent, query_proj, key_proj, value_proj, output_proj, expand_proj,
    shrink_proj, query_bias, value_bias, expand_bias, output_bias, attn_gain, attn_shift,
    shrink_bias, ffn_gain, ffn_shift,
):
    plan = Plan()
    parts = plan.parts
    rows, width = query_proj.shape
    hidden = expand_proj.shape[1]
    few = query_bias.shape[0]
    block = tokens.shape[2]

    head_biases = jnp.concatenate([query_bias, value_bias])
    smalls = [output_bias, attn_gain, attn_shift, shrink_bias, ffn_gain, ffn_shift, expand_bias]
    pack_one = jnp.concatenate(
        [query_proj, key_proj, value_proj]
        + [column(v, rows) for v in smalls]
        + [column(head_biases, rows)],
        axis=1,
    )
    pack_two = jnp.concatenate([output_proj.T, expand_proj, shrink_proj.T], axis=1)
    ones = plan.gather(pack_one)
    own_tokens = plan.collect(tokens[:, 0])
    twos = plan.gather(pack_two)
    three = 3 * width
    wide = [w[:, three : three + 6].astype(FULL).T for w in ones[:1]][0]
    output_b, gain_one, shift_one, shrink_b, gain_two, shift_two = [wide[n] for n in range(6)]
    expand_b = [w[:, three + 6].astype(FULL) for w in ones]
    query_b, value_b = [], []
    for w in ones:
        both = w[:, three + 7].astype(FULL).reshape(plan.owners, rows)
        query_b.append(both[:, :few].reshape(width))
        value_b.append(both[:, few : 2 * few].reshape(width))
    qkv_w = [w[:, :three] for w in ones]
    output_w = jnp.concatenate([w[:, :width] for w in twos], axis=1)
    expand_w = [w[:, width : width + hidden] for w in twos]
    shrink_w = [w[:, width + hidden :] for w in twos]

    micro, parity = plan.place // 2, plan.place % 2
    other_lengths = plan.swap(lengths, 1)
    mine = jnp.where(parity == plan.core, lengths, other_lengths)[:, 0]
    length = lax.dynamic_index_in_dim(mine, micro, 0, False)

    def slots_of(core):
        return jnp.concatenate(
            [block * (2 * core + (micro + n) % 2) + jnp.arange(block) for n in range(2)]
        )

    row_slots = slots_of(plan.core)
    live_rows = (row_slots < length).astype(FULL)[:, None]
    live = jnp.concatenate([row_slots, slots_of(1 - plan.core)]) < length

    x = jnp.concatenate(own_tokens)
    query, keys, values = [], [], []
    for n in range(parts):
        y = contract(x, qkv_w[n], "rd,dk->rk")
        query.append((y[:, :width] + query_b[n]).astype(LOW))
        keys.append(y[:, width : 2 * width].astype(LOW))
        values.append((y[:, 2 * width :] + value_b[n]).astype(LOW))
    other = plan.swap(jnp.concatenate(keys + values, axis=1), 1)
    full = parts * width
    attended, logs = [], []
    for n in range(parts):
        keys[n] = jnp.concatenate([keys[n], other[:, n * width : (n + 1) * width]])
        values[n] = jnp.concatenate([values[n], other[:, full + n * width : full + (n + 1) * width]])
        a, log_total = attend_forward(query[n], keys[n], values[n], live)
        attended.append(a)
        logs.append(log_total)
    attended_all = jnp.concatenate(attended, axis=1)
    attn = contract(attended_all, output_w, "rk,dk->rd")
    first_sum = x.astype(FULL) + attn + output_b
    first_unit, first_scale = normalize(first_sum)
    normed = first_unit * gain_one + shift_one
    ffn_in = normed.astype(LOW)
    active, slope = [], []
    ffn = 0.0
    for n in range(parts):
        upper = contract(ffn_in, expand_w[n], "rd,dk->rk") + expand_b[n]
        below = 0.5 * (1.0 + lax.erf(upper * ROOT_HALF))
        active.append((upper * below).astype(LOW))
        slope.append(below + upper * jnp.exp(-0.5 * upper * upper) * DENSITY)
        ffn = ffn + contract(active[n], shrink_w[n], "rk,dk->rd")
    second_sum = normed + ffn + shrink_b
    second_unit, second_scale = normalize(second_sum)
    layer_rows = (second_unit * gain_two + shift_two).astype(LOW)
    layer_out = plan.release([layer_rows[:block], layer_rows[block:]])

    cot = jnp.concatenate(plan.collect(cotangent[:, 0]))
    out_grad = cot.astype(FULL) * live_rows
    grad_gain_two = jnp.sum(out_grad * second_unit, axis=0)
    grad_shift_two = jnp.sum(out_grad, axis=0)
    second_grad = norm_back(out_grad, gain_two, second_unit, second_scale)
    grad_shrink_b = jnp.sum(second_grad, axis=0)
    second_low = second_grad.astype(LOW)
    grad_two, grad_expand_b = [], []
    normed_grad = second_grad
    upper_low = []
    for n in range(parts):
        upper_grad = contract(second_low, shrink_w[n], "rd,dk->rk") * slope[n]
        grad_expand_b.append(jnp.sum(upper_grad, axis=0))
        upper_low.append(upper_grad.astype(LOW))
        normed_grad = normed_grad + contract(upper_low[n], expand_w[n], "rk,dk->rd")
    grad_gain_one = jnp.sum(normed_grad * first_unit, axis=0)
    grad_shift_one = jnp.sum(normed_grad, axis=0)
    first_grad = norm_back(normed_grad, gain_one, first_unit, first_scale)
    grad_output_b = jnp.sum(first_grad, axis=0)
    first_low = first_grad.astype(LOW)
    for n in range(parts):
        grad_two.append(
            jnp.concatenate(
                [
                    contract(first_low, attended[n], "rd,rk->dk"),
                    contract(ffn_in, upper_low[n], "rd,rk->dk"),
                    contract(second_low, active[n], "rd,rk->dk"),
                ],
                axis=1,
            )
        )
    sums_two = plan.reduce(grad_two)
    attended_grad = contract(first_low, output_w, "rd,dk->rk").astype(LOW)
    query_grad, key_grad, value_grad = [], [], []
    for n in range(parts):
        q, k, v = attend_backward(
            query[n], keys[n], values[n], live, logs[n], attended_grad[:, n * width : (n + 1) * width]
        )
        query_grad.append(q)
        key_grad.append(k)
        value_grad.append(v)
    here = 2 * block
    away = jnp.concatenate([g[here:] for g in key_grad + value_grad], axis=1).astype(LOW)
    added = plan.swap(away, 1).astype(FULL)
    grad_one = []
    rows_grad = first_grad
    vectors = [grad_output_b, grad_gain_one, grad_shift_one, grad_shrink_b, grad_gain_two, grad_shift_two]
    for n in range(parts):
        k = key_grad[n][:here] + added[:, n * width : (n + 1) * width]
        v = value_grad[n][:here] + added[:, full + n * width : full + (n + 1) * width]
        low = jnp.concatenate([query_grad[n], k, v], axis=1).astype(LOW)
        rows_grad = rows_grad + contract(low, qkv_w[n], "rk,dk->rd")
        biases = jnp.concatenate(
            [jnp.sum(g, axis=0).reshape(plan.owners, few) for g in (query_grad[n], v)], axis=1
        )
        biases = jnp.pad(biases, ((0, 0), (0, rows - 2 * few))).reshape(-1)
        cols = jnp.stack(vectors + [grad_expand_b[n], biases], axis=1)
        grad_one.append(jnp.concatenate([contract(x, low, "rd,rk->dk"), cols], axis=1))
    input_low = rows_grad.astype(LOW)
    input_grad = plan.release([input_low[:block], input_low[block:]]).astype(FULL)
    sums_one = plan.reduce(grad_one)
    quarter = rows // parts
    own = lax.dynamic_slice_in_dim(sums_one[:, three : three + 6], plan.place * quarter, quarter, 0)
    return (
        layer_out[:, None],
        input_grad[:, None],
        sums_one[:, :width],
        sums_one[:, width : 2 * width],
        sums_one[:, 2 * width : three],
        sums_two[:, :width].T,
        sums_two[:, width : width + hidden],
        sums_two[:, width + hidden :].T,
        sums_one[:few, three + 7],
        sums_one[few : 2 * few, three + 7],
        sums_one[:, three + 6],
        own[:, 0],
        own[:, 1],
        own[:, 2],
        own[:, 3],
        own[:, 4],
        own[:, 5],
    )


def solution(mesh):
    rows = P(None, "fsdp", "tensor", None)
    split = P("fsdp", "tensor")
    turned = P("tensor", "fsdp")
    heads = P(("tensor", "fsdp"))
    model = P("fsdp")
    spread = P(("fsdp", "tensor"))
    return jax.shard_map(
        shards,
        mesh=mesh,
        in_specs=(rows, P(None, "fsdp"), rows, split, split, split, turned, split, turned)
        + (heads,) * 3
        + (model,) * 6,
        out_specs=(rows, rows, split, split, split, turned, split, turned)
        + (heads,) * 3
        + (spread,) * 6,
        check_vma=False,
    )
```

```python
import functools
import math

import jax
import jax.numpy as jnp
from jax import lax
from jax.experimental import pallas as pl
from jax.experimental.pallas import tpu as pltpu
from jax.sharding import PartitionSpec as P

HD = 64
EPS = 1e-05
DEAD = -8000000000.0
ROOT_HALF = 0.7071067811865476
DENSITY = 0.3989422804014327
LOG2E = 1.4426950408889634
SCALE2 = 0.125 * LOG2E
BOTH = ("fsdp", "tensor")
LOW = jnp.bfloat16
FULL = jnp.float32
LANES = 128
CHUNK = 256
QUERIES = 256
ROWS = 128
MIB = 1 << 20
NT = (((1,), (1,)), ((), ()))
SMALL = 64

IN_VMEM = pl.BlockSpec(memory_space=pltpu.VMEM)
IN_SMEM = pl.BlockSpec(memory_space=pltpu.SMEM)
ANYWHERE = pl.BlockSpec(memory_space=pl.ANY)


def shape(dims, dtype):
    return jax.ShapeDtypeStruct(dims, dtype)


def fixed(dims):
    return pl.BlockSpec(dims, lambda i: (0,) * len(dims))


def params(grid=0, vmem=56):
    return pltpu.CompilerParams(
        vmem_limit_bytes=vmem * MIB, dimension_semantics=("arbitrary",) * grid if grid else None
    )


def cost(flops, touched, exps=0):
    return pl.CostEstimate(flops=int(flops), bytes_accessed=int(touched), transcendentals=int(exps))


def mm(left, right):
    return jnp.dot(left, right, preferred_element_type=FULL)


def mm_nt(left, right):
    return lax.dot_general(left, right, NT, preferred_element_type=FULL)


def flip(value):
    return value.astype(FULL).T.astype(value.dtype)


class Blocks:
    def __init__(self, arrays, slices, table_rows):
        self.arrays, self.slices, self.table_rows = arrays, slices, table_rows

    def count(self):
        return sum(a.shape[0] * a.shape[1] for a in self.arrays)

    def width(self):
        return self.arrays[0].shape[3]

    def copies(self, table, refs, scratch, sems):
        found = {}
        at = 0
        for ref, slices, row in zip(refs, self.slices, self.table_rows):
            n, _, rows, _ = ref.shape
            for place, s in enumerate(slices):
                for i in range(n):
                    start = pl.multiple_of(table[row, i], 16) if n > 1 else 0
                    found.setdefault(s, []).append(
                        pltpu.make_async_copy(
                            ref.at[i, place], scratch.at[s, pl.ds(start, rows), :], sems.at[at]
                        )
                    )
                    at += 1
        return found


def begin(copies):
    for group in copies.values():
        for copy in group:
            copy.start()


def finish(group):
    for copy in group:
        copy.wait()


def project_kernel(blocks, rows_few, table, x_ref, pick_ref, *rest):
    n = len(blocks.arrays)
    refs, (q_ref, kv_ref, small_ref, w, sems) = rest[:n], rest[n:]
    copies = blocks.copies(table, refs, w, sems)
    begin(copies)
    parts = len(copies)
    third = q_ref.shape[1] // parts
    base = 3 * third // LANES * LANES
    skip = 3 * third - base
    small_ref[...] = jnp.zeros_like(small_ref)
    queries, keys, values = [], [], []
    for s in range(parts):
        finish(copies[s])
        turned = w[s, :, base:].astype(FULL).T
        few = turned[skip : skip + 8]
        if s == 0:
            small_ref[0:8] = few
        small_ref[8 + s : 9 + s] = few[6:7]
        bias = mm(few.astype(LOW), pick_ref[...])[7:8]
        y = mm(x_ref[...], w[s])
        queries.append(y[:, :third] + bias[:, :third])
        keys.append(y[:, third : 2 * third])
        values.append(y[:, 2 * third : 3 * third] + bias[:, third:])
    q_ref[...] = jnp.concatenate(queries, axis=1).astype(LOW)
    width = q_ref.shape[1]
    kv_ref[:, :width] = jnp.concatenate(keys, axis=1).astype(LOW)
    kv_ref[:, width:] = jnp.concatenate(values, axis=1).astype(LOW)


def attend_kernel(q_ref, ko, ke, vo, ve, xk_ref, xq_ref, att_ref, lse_ref):
    pair = pl.program_id(0)
    k = jnp.concatenate([ko[...], ke[...]], axis=0)
    v_t = flip(jnp.concatenate([vo[...], ve[...]], axis=0))
    q = q_ref[...]
    rows = q.shape[0]
    ones = jnp.ones((16, k.shape[0]), LOW)
    outs = []
    for h in range(2):
        side = slice(HD * h, HD * h + HD)
        kh = jnp.concatenate([k[:, side], xk_ref[...]], axis=1)
        qh = jnp.concatenate([q[:, side], xq_ref[...]], axis=1)
        vt = jnp.concatenate([v_t[side], ones], axis=0)
        got = []
        for start in range(0, rows, QUERIES):
            span = slice(start, start + QUERIES)
            scores = mm_nt(kh, qh[span])
            top = jnp.max(scores, axis=0, keepdims=True)
            raised = jnp.exp2((scores - top) * SCALE2).astype(LOW)
            o = mm(vt, raised)
            denom = o[HD : HD + 1]
            got.append(o[:HD] * (1.0 / denom))
            lse_ref[pl.ds(2 * pair + h, 1), span] = top * SCALE2 + jnp.log2(denom)
        outs.append(jnp.concatenate(got, axis=1))
    att_ref[...] = jnp.concatenate(outs, axis=0).T.astype(LOW)


def attend_back_kernel(
    first, q_ref, g_ref, att_ref, ko, ke, vo, ve, xk_ref, xq_ref, lse_ref,
    dq_ref, sum_ref, dk_ref, dv_ref, ak_ref, av_ref,
):
    pair = pl.program_id(0) + first
    k = jnp.concatenate([ko[...], ke[...]], axis=0)
    v = jnp.concatenate([vo[...], ve[...]], axis=0)
    k_t = flip(k)
    q, g = q_ref[...], g_ref[...]
    rows = q.shape[0]
    product = (g.astype(FULL) * att_ref[...].astype(FULL)).T
    dqs, dks, dvs = [], [], []
    for h in range(2):
        side = slice(HD * h, HD * h + HD)
        kh = jnp.concatenate([k[:, side], xk_ref[...]], axis=1)
        qh = jnp.concatenate([q[:, side], xq_ref[...]], axis=1)
        inner = jnp.sum(product[side], axis=0, keepdims=True)
        lse = lse_ref[pl.ds(2 * pair + h, 1), :]
        vh, gh, qs = v[:, side], g[:, side], q[:, side]
        dk = dv = None
        got = []
        for start in range(0, rows, QUERIES):
            span = slice(start, start + QUERIES)
            probs = jnp.exp2(mm_nt(kh, qh[span]) * SCALE2 - lse[:, span])
            prob_grad = mm_nt(vh, gh[span])
            score_grad = (probs * (prob_grad - inner[:, span])).astype(LOW)
            more_v = mm(probs.astype(LOW), gh[span])
            more_k = mm(score_grad, qs[span])
            dv = more_v if dv is None else dv + more_v
            dk = more_k if dk is None else dk + more_k
            got.append(mm(k_t[side], score_grad))
        dqs.append(jnp.concatenate(got, axis=1))
        dks.append(dk)
        dvs.append(dv)
    dq = jnp.concatenate(dqs, axis=0).T * 0.125
    dq_ref[...] = dq.astype(LOW)
    sum_ref[...] = jnp.broadcast_to(jnp.sum(dq, axis=0, keepdims=True), sum_ref.shape)
    dk = jnp.concatenate(dks, axis=1) * 0.125
    dv = jnp.concatenate(dvs, axis=1)
    dk_ref[...] = dk[:rows]
    dv_ref[...] = dv[:rows]
    ak_ref[...] = dk[rows:].astype(LOW)
    av_ref[...] = dv[rows:].astype(LOW)


def means(value):
    return jnp.mean(value, axis=-1, keepdims=True)


def normalize(summed):
    center = summed - means(summed)
    inv = lax.rsqrt(means(center * center) + EPS)
    return center * inv, inv


def norm_back(grad, gain, unit, inv):
    scaled = grad * gain
    return inv * (scaled - means(scaled) - unit * means(scaled * unit))


def total(value):
    return jnp.sum(value, axis=0, keepdims=True)


def expand_kernel(blocks, table, x_ref, att_ref, small_ref, *rest):
    n = len(blocks.arrays)
    refs = rest[:n]
    normed_ref, unit_ref, inv_ref, low_ref, act_ref, slope_ref, w, attn, sems = rest[n:]
    copies = blocks.copies(table, refs, w, sems)
    parts = len(copies)
    step = pl.program_id(0)
    hidden = x_ref.shape[1]
    width = hidden // parts

    @pl.when(step == 0)
    def _():
        begin(copies)
        for s in range(parts):
            finish(copies[s])
        value = None
        for s in range(parts):
            more = mm_nt(att_ref[:, width * s : width * s + width], w[s, :, hidden : hidden + width])
            value = more if value is None else value + more
        attn[...] = value

        @pl.loop(0, x_ref.shape[0] // ROWS)
        def _(i):
            span = pl.ds(pl.multiple_of(i * ROWS, ROWS), ROWS)
            summed = x_ref[span].astype(FULL) + attn[span] + small_ref[0:1]
            unit, inv = normalize(summed)
            normed = unit * small_ref[1:2] + small_ref[2:3]
            normed_ref[span] = normed
            unit_ref[span] = unit
            inv_ref[span] = jnp.broadcast_to(inv, (ROWS, LANES))
            low_ref[span] = normed.astype(LOW)

    per = hidden // CHUNK
    s, lanes = step // per, pl.ds(pl.multiple_of(step % per * CHUNK, CHUNK), CHUNK)
    bias = small_ref[pl.ds(8 + s, 1), lanes]
    upper = mm(low_ref[...], w[s, :, lanes]) + bias
    below = 0.5 * (1.0 + lax.erf(upper * ROOT_HALF))
    act_ref[...] = (upper * below).astype(LOW)
    slope_ref[...] = (below + upper * jnp.exp(-0.5 * upper * upper) * DENSITY).astype(LOW)


def shrink_kernel(blocks, table, act_ref, normed_ref, small_ref, cot_ref, live_ref, *rest):
    n = len(blocks.arrays)
    refs = rest[:n]
    out_ref, grad_ref, low_ref, vec_ref, w, acc, sems = rest[n:]
    copies = blocks.copies(table, refs, w, sems)
    step = pl.program_id(0)
    hidden = normed_ref.shape[1]
    per = hidden // CHUNK
    s, lanes = step // per, pl.ds(pl.multiple_of(step % per * CHUNK, CHUNK), CHUNK)

    @pl.when(step == 0)
    def _():
        begin(copies)

    for part, group in copies.items():

        @pl.when(step == part * per)
        def _(group=group):
            finish(group)

    more = mm_nt(act_ref[...], w[s, :, lanes])

    @pl.when(step == 0)
    def _():
        acc[...] = more

    @pl.when(step > 0)
    def _():
        acc[...] += more

    @pl.when(step == pl.num_programs(0) - 1)
    def _():
        vec_ref[...] = jnp.zeros_like(vec_ref)

        @pl.loop(0, normed_ref.shape[0] // ROWS)
        def _(i):
            span = pl.ds(pl.multiple_of(i * ROWS, ROWS), ROWS)
            summed = normed_ref[span] + acc[span] + small_ref[3:4]
            unit, inv = normalize(summed)
            out_ref[span] = (unit * small_ref[4:5] + small_ref[5:6]).astype(LOW)
            arriving = cot_ref[span].astype(FULL) * live_ref[span, 0:1]
            grad = norm_back(arriving, small_ref[4:5], unit, inv)
            grad_ref[span] = grad
            low_ref[span] = grad.astype(LOW)
            vec_ref[0:1] += total(grad)
            vec_ref[1:2] += total(arriving * unit)
            vec_ref[2:3] += total(arriving)


class Exits:
    def __init__(self, flat, outers, rows, table_rows):
        self.flat, self.outers, self.rows, self.table_rows = flat, outers, rows, table_rows

    def shapes(self, slices, width):
        dims = (self.outers, slices, self.rows, width)
        if self.flat:
            return [shape((slices, 2 * self.outers * self.rows, width), LOW)]
        return [shape(dims, LOW)] * 2

    def emit(self, table, value_ref, refs, s, lanes):
        if self.flat:
            refs[0][s, :, lanes] = value_ref[...].astype(LOW)
            return
        for ref, row in zip(refs, self.table_rows):
            for i in range(self.outers):
                start = pl.multiple_of(table[row, i], 8)
                ref[i, s, :, lanes] = value_ref[pl.ds(start, self.rows), :].astype(LOW)


def shrink_grad_kernel(exits, table, low_ref, act_ref, *rest):
    outs, (turned, stage) = rest[:-2], rest[-2:]

    @pl.when(pl.program_id(0) == 0)
    def _():
        turned[...] = flip(low_ref[...])

    stage[...] = mm(turned[...], act_ref[...])
    exits.emit(table, stage, outs, 0, slice(None))


def middle_kernel(
    ups, downs, exits, table, low_ref, normed_low_ref, slope_ref, grad_ref, unit_ref, inv_ref,
    small_ref, att_ref, *rest,
):
    n, m = len(ups.arrays), len(downs.arrays)
    up_refs, down_refs, rest = rest[:n], rest[n : n + m], rest[n + m :]
    first_ref, first_low_ref, att_grad_ref, vec_ref, expand_ref = rest[:5]
    outs = rest[5:-8]
    up_w, down_w, up_sems, down_sems, turned, acc, stage, stage_o = rest[-8:]
    up_copies = ups.copies(table, up_refs, up_w, up_sems)
    down_copies = downs.copies(table, down_refs, down_w, down_sems)
    parts = len(up_copies)
    step = pl.program_id(0)
    hidden = unit_ref.shape[1]
    width = hidden // parts
    per = hidden // CHUNK
    s, lanes = step // per, pl.ds(pl.multiple_of(step % per * CHUNK, CHUNK), CHUNK)

    @pl.when(step == 0)
    def _():
        for part in range(parts):
            begin({0: down_copies[part], 1: up_copies[part]})
        turned[...] = flip(normed_low_ref[...])
        expand_ref[...] = jnp.zeros_like(expand_ref)

    for part in range(parts):

        @pl.when(step == part * per)
        def _(part=part):
            finish(down_copies[part])
            finish(up_copies[part])

    upper_grad = mm(low_ref[...], down_w[s, :, lanes]) * slope_ref[...].astype(FULL)
    expand_ref[pl.ds(s, 1), lanes] = total(upper_grad)
    upper_low = upper_grad.astype(LOW)
    stage[...] = mm(turned[...], upper_low)
    exits.emit(table, stage, outs, s, lanes)
    more = mm_nt(upper_low, up_w[s, :, lanes])

    @pl.when(step == 0)
    def _():
        acc[...] = more

    @pl.when(step > 0)
    def _():
        acc[...] += more

    @pl.when(step == pl.num_programs(0) - 1)
    def _():
        vec_ref[...] = jnp.zeros_like(vec_ref)

        @pl.loop(0, unit_ref.shape[0] // ROWS)
        def _(i):
            span = pl.ds(pl.multiple_of(i * ROWS, ROWS), ROWS)
            grad = acc[span] + grad_ref[span]
            unit = unit_ref[span]
            first = norm_back(grad, small_ref[1:2], unit, inv_ref[span, 0:1])
            first_ref[span] = first
            first_low_ref[span] = first.astype(LOW)
            vec_ref[0:1] += total(first)
            vec_ref[1:2] += total(grad * unit)
            vec_ref[2:3] += total(grad)

        turned[...] = flip(first_low_ref[...])
        grads = []
        for part in range(parts):
            o = up_w[part, :, hidden : hidden + width]
            grads.append(mm(first_low_ref[...], o))
            stage_o[...] = mm(turned[...], att_ref[:, width * part : width * part + width])
            exits.emit(table, stage_o, outs, part, slice(hidden, hidden + width))
        att_grad_ref[...] = jnp.concatenate(grads, axis=1).astype(LOW)


def input_kernel(
    blocks, exits, slices, table, x_ref, dq_ref, dqs_ref, dk_ref, dv_ref, add_ref, sofar_ref,
    one_ref, two_ref, expand_ref, pick_ref, *rest,
):
    n = len(blocks.arrays)
    refs, rest = rest[:n], rest[n:]
    grad_ref, outs = rest[0], rest[1:-4]
    w, vecs, stage, sems = rest[-4:]
    copies = blocks.copies(table, refs, w, sems)
    begin(copies)
    turned = flip(x_ref[...])
    rows = x_ref.shape[0]
    wide = dq_ref.shape[1]
    width = wide // len(slices)
    dq = dq_ref[...]
    dk = (dk_ref[...] + add_ref[:, :wide].astype(FULL)).astype(LOW)
    dv_full = dv_ref[...] + add_ref[:, wide:].astype(FULL)
    dv = dv_full.astype(LOW)
    dvs = total(dv_full)
    base = 3 * width // LANES * LANES
    skip = 3 * width - base
    vecs[...] = jnp.zeros_like(vecs)
    vecs[skip : skip + 3] = one_ref[0:3]
    vecs[skip + 3 : skip + 6] = two_ref[0:3]
    grad = sofar_ref[...]
    for i, s in enumerate(slices):
        side = slice(width * i, width * i + width)
        low = jnp.concatenate([dq[:, side], dk[:, side], dv[:, side], jnp.zeros((rows, SMALL), LOW)], axis=1)
        stage[...] = mm(turned, low)
        sums = jnp.concatenate([dqs_ref[:, side], jnp.broadcast_to(dvs[:, side], (8, width))], axis=1)
        high = sums.astype(LOW)
        rest_of = (sums - high.astype(FULL)).astype(LOW)
        heads = mm_nt(high, pick_ref[...]) + mm_nt(rest_of, pick_ref[...])
        vecs[skip + 6 : skip + 7] = expand_ref[s : s + 1]
        vecs[skip + 7 : skip + 8] = heads[0:1]
        stage[:, base:] += vecs[...].T
        exits.emit(table, stage, outs, i, slice(None))
        finish(copies[s])
        grad = grad + mm_nt(low, w[s])
    grad_ref[...] = grad.astype(grad_ref.dtype)


class Plan:
    def __init__(self, rows):
        self.parts = lax.axis_size("tensor")
        self.owners = lax.axis_size("fsdp")
        self.place = lax.axis_index("tensor")
        self.owner = lax.axis_index("fsdp")
        self.core = self.owner % 2
        self.outer = self.owner // 2
        self.outers = self.owners // 2
        self.rows = rows
        self.flat = rows % 16 != 0
        self.bits = [1 << n for n in range((self.outers - 1).bit_length())]
        rising = list(range(self.outers))
        falling = [0]
        for bit in self.bits[::-1]:
            falling = falling + [n ^ bit for n in falling]
        self.orders = (rising, falling)
        own = jnp.array([rising, rising, falling, falling], jnp.int32) ^ self.outer
        core = jnp.array([0, 1, 0, 1], jnp.int32)[:, None] ^ self.core
        self.table = ((own * 2 + core) * rows).astype(jnp.int32)

    def swap(self, value, bit):
        return lax.ppermute(value, "fsdp", [(n, n ^ bit) for n in range(self.owners)])

    def turn(self, value, by):
        n = self.parts
        return lax.ppermute(value, "tensor", [(i, (i + by) % n) for i in range(n)])

    def trade(self, turn, back):
        pairs = []
        half = self.parts // 2
        for owner in range(self.owners):
            for place in range(self.parts):
                micro = (place + turn) % 2
                there = (owner - owner % 2 + place // half) * self.parts + 2 * micro + owner % 2
                here = owner * self.parts + place
                pairs.append((there, here) if back else (here, there))
        return pairs

    def collect(self, value):
        return [
            lax.ppermute(
                lax.dynamic_index_in_dim(value, (self.place + turn) % 2, 0, False),
                BOTH,
                self.trade(turn, False),
            )
            for turn in range(2)
        ]

    def release(self, blocks):
        first, second = [
            lax.ppermute(block, BOTH, self.trade(turn, True)) for turn, block in enumerate(blocks)
        ]
        even = self.place % 2 == 0
        return jnp.stack([jnp.where(even, first, second), jnp.where(even, second, first)])

    def around(self, shard):
        return [shard] + [self.turn(shard, by) for by in range(1, self.parts)]

    def gather(self, lots):
        arrays, numbers, table_rows = [], [], []
        for lot, names, falling in lots:
            held = jnp.stack(lot)[None]
            for bit in self.bits[::-1] if falling else self.bits:
                held = jnp.concatenate([held, self.swap(held, 2 * bit)])
            other = self.swap(held, 1)
            if self.flat:
                arrays.append(self.natural(held, other, self.orders[falling]))
                numbers.append(names)
                table_rows.append(0)
            else:
                arrays += [held, other]
                numbers += [names, names]
                table_rows += [2 * falling, 2 * falling + 1]
        return Blocks(arrays, numbers, table_rows)

    def natural(self, mine, other, order):
        where = jnp.array([order.index(n) for n in range(self.outers)])
        both = []
        for n in range(self.outers):
            at = where[n ^ self.outer]
            pair = [lax.dynamic_index_in_dim(v, at, 0, False) for v in (mine, other)]
            both.append(jnp.where(self.core == 0, pair[0], pair[1]))
            both.append(jnp.where(self.core == 0, pair[1], pair[0]))
        return jnp.concatenate(both, axis=1)[None]

    def exits(self, falling):
        row = 0 if falling else 2
        return Exits(self.flat, self.outers, self.rows, (row, row + 1))

    def reduce(self, blocks, names, falling):
        if self.flat:
            order = self.orders[not falling]
            value = blocks[0].reshape(len(names), self.outers, 2, self.rows, -1)
            pair = [
                jnp.concatenate(
                    [
                        lax.dynamic_slice(
                            value,
                            (0, n ^ self.outer, core, 0, 0),
                            (len(names), 1, 1, self.rows, value.shape[-1]),
                        )[:, 0]
                        for n in order
                    ],
                    axis=1,
                ).swapaxes(0, 1)
                for core in (self.core, 1 - self.core)
            ]
            blocks = pair
        keep, send = blocks
        terms = [keep, self.swap(send, 1)]
        n = self.outers
        for bit in self.bits[::-1] if falling else self.bits:
            n //= 2
            away = sum(t[n:].astype(FULL) for t in terms).astype(LOW)
            terms = [t[:n] for t in terms] + [self.swap(away, 2 * bit)]
        value = 0.0
        for i, by in enumerate(names):
            term = sum(t[0, i].astype(FULL) for t in terms)
            value = value + (self.turn(term.astype(LOW), -by).astype(FULL) if by else term)
        return value


def column(vector, rows):
    return jnp.pad(vector, (0, rows - vector.shape[0]))[:, None]


def shards(
    tokens, lengths, cotangent, query_proj, key_proj, value_proj, output_proj, expand_proj,
    shrink_proj, query_bias, value_bias, expand_bias, output_bias, attn_gain, attn_shift,
    shrink_bias, ffn_gain, ffn_shift,
):
    rows, width = query_proj.shape
    plan = Plan(rows)
    parts = plan.parts
    hidden = expand_proj.shape[1]
    few = query_bias.shape[0]
    block = tokens.shape[2]
    mine = 2 * block
    model = tokens.shape[3]
    three = 3 * width
    table = plan.table

    smalls = [output_bias, attn_gain, attn_shift, shrink_bias, ffn_gain, ffn_shift, expand_bias]
    pack_one = jnp.concatenate(
        [query_proj, key_proj, value_proj]
        + [column(v, rows) for v in smalls]
        + [column(jnp.concatenate([query_bias, value_bias]), rows)]
        + [jnp.zeros((rows, SMALL - 8), LOW)],
        axis=1,
    )
    pack_two = jnp.concatenate([expand_proj, output_proj.T, shrink_proj.T], axis=1)
    wide_one, wide_two, wide_three = pack_one.shape[1], hidden + width, hidden
    ones = plan.around(pack_one)
    own_tokens = plan.collect(tokens[:, 0])
    twos = plan.around(pack_two)
    half = parts // 2
    low_names, high_names, names = list(range(half)), list(range(half, parts)), list(range(parts))
    qkv_w = plan.gather([(ones[:half], low_names, False), (ones[half:], high_names, True)])
    up_w = plan.gather([([t[:, :wide_two] for t in twos], names, False)])
    down_w = plan.gather([([t[:, wide_two:] for t in twos], names, True)])
    place = jnp.arange(model)[:, None]
    head = jnp.arange(2 * width)[None, :]
    inside = head % width
    pick = (place == inside // few * rows + inside % few + few * (head // width)).astype(LOW)

    micro, parity = plan.place // 2, plan.place % 2
    seen = jnp.where(parity == plan.core, lengths, plan.swap(lengths, 1))[:, 0]
    length = jnp.where(micro == 0, seen[0], seen[1])

    def slots_of(core):
        return jnp.concatenate(
            [block * (2 * core + (micro + n) % 2) + jnp.arange(block) for n in range(2)]
        )

    row_slots = slots_of(plan.core)
    live_rows = jnp.broadcast_to((row_slots < length).astype(FULL)[:, None], (mine, LANES))
    live = jnp.concatenate([row_slots, slots_of(1 - plan.core)]) < length
    lead = jnp.arange(HD)[None, :] == 0
    extra_k = jnp.where(lead & ~live[:, None], DEAD, 0.0).astype(LOW)
    extra_q = jnp.broadcast_to(lead, (mine, HD)).astype(LOW)

    x = jnp.concatenate(own_tokens)
    dot_cost = 2 * mine * model * model
    query, key_value, small = pl.pallas_call(
        functools.partial(project_kernel, qkv_w, few),
        out_shape=[shape((mine, model), LOW), shape((mine, 2 * model), LOW), shape((16, model), FULL)],
        in_specs=[IN_SMEM, IN_VMEM, IN_VMEM] + [ANYWHERE] * len(qkv_w.arrays),
        out_specs=[IN_VMEM] * 3,
        scratch_shapes=[
            pltpu.VMEM((parts, model, wide_one), LOW),
            pltpu.SemaphoreType.DMA((qkv_w.count(),)),
        ],
        compiler_params=params(),
        cost_estimate=cost(3 * dot_cost, 8 * MIB),
        name="project",
    )(table, x, pick, *qkv_w.arrays)
    other = plan.swap(key_value, 1)
    pairs = model // LANES
    heads = 2 * pairs
    pad_heads = -(-heads // 8) * 8
    all_rows = 2 * mine

    def lane_block(offset):
        return pl.BlockSpec((mine, LANES), lambda i: (0, i + offset))

    score_cost = 2 * mine * all_rows * HD
    attended, log_total = pl.pallas_call(
        attend_kernel,
        out_shape=[shape((mine, model), LOW), shape((pad_heads, mine), FULL)],
        grid=(pairs,),
        in_specs=[
            lane_block(0), lane_block(0), lane_block(0), lane_block(pairs), lane_block(pairs),
            fixed((all_rows, HD)), fixed((mine, HD)),
        ],
        out_specs=[lane_block(0), fixed((pad_heads, mine))],
        compiler_params=params(1),
        cost_estimate=cost(6 * heads * score_cost, 6 * MIB, heads * mine * all_rows),
        name="attend",
    )(query, key_value, other, key_value, other, extra_k, extra_q)

    chunks = parts * hidden // CHUNK
    per = hidden // CHUNK
    chunk_block = pl.BlockSpec((mine, CHUNK), lambda i: (0, i))
    full_rows = fixed((mine, model))
    normed, unit, inv, normed_low, active, slope = pl.pallas_call(
        functools.partial(expand_kernel, up_w),
        out_shape=[
            shape((mine, model), FULL), shape((mine, model), FULL), shape((mine, LANES), FULL),
            shape((mine, model), LOW), shape((mine, parts * hidden), LOW), shape((mine, parts * hidden), LOW),
        ],
        grid=(chunks,),
        in_specs=[IN_SMEM, full_rows, full_rows, fixed((16, model))] + [ANYWHERE] * len(up_w.arrays),
        out_specs=[full_rows, full_rows, fixed((mine, LANES)), full_rows, chunk_block, chunk_block],
        scratch_shapes=[
            pltpu.VMEM((parts, model, wide_two), LOW),
            pltpu.VMEM((mine, model), FULL),
            pltpu.SemaphoreType.DMA((up_w.count(),)),
        ],
        compiler_params=params(1),
        cost_estimate=cost(8 * dot_cost, 20 * MIB),
        name="expand",
    )(table, x, attended, small, *up_w.arrays)
    cot = jnp.concatenate(plan.collect(cotangent[:, 0]))
    layer_rows, second_grad, second_low, vec_two = pl.pallas_call(
        functools.partial(shrink_kernel, down_w),
        out_shape=[
            shape((mine, model), LOW), shape((mine, model), FULL), shape((mine, model), LOW), shape((8, model), FULL),
        ],
        grid=(chunks,),
        in_specs=[
            IN_SMEM, chunk_block, full_rows, fixed((16, model)), full_rows, fixed((mine, LANES)),
        ] + [ANYWHERE] * len(down_w.arrays),
        out_specs=[full_rows, full_rows, full_rows, fixed((8, model))],
        scratch_shapes=[
            pltpu.VMEM((parts, model, wide_three), LOW),
            pltpu.VMEM((mine, model), FULL),
            pltpu.SemaphoreType.DMA((down_w.count(),)),
        ],
        compiler_params=params(1),
        cost_estimate=cost(5 * dot_cost, 16 * MIB),
        name="shrink",
    )(table, active, normed, small, cot, live_rows, *down_w.arrays)
    layer_out = plan.release([layer_rows[:block], layer_rows[block:]])

    exits = plan.exits(False)
    if plan.flat:
        grad_block = [pl.BlockSpec((1, model, CHUNK), lambda i: (i // per, 0, i % per))]
    else:
        grad_block = [
            pl.BlockSpec((plan.outers, 1, rows, CHUNK), lambda i: (0, i // per, 0, i % per))
        ] * 2
    blocks = pl.pallas_call(
        functools.partial(shrink_grad_kernel, exits),
        out_shape=exits.shapes(parts, hidden),
        grid=(chunks,),
        in_specs=[IN_SMEM, full_rows, chunk_block],
        out_specs=grad_block,
        scratch_shapes=[pltpu.VMEM((model, mine), LOW), pltpu.VMEM((model, CHUNK), FULL)],
        compiler_params=params(1),
        cost_estimate=cost(4 * dot_cost, 9 * MIB),
        name="shrink_grad",
    )(table, second_low, active)
    sums_three = plan.reduce(blocks, names, False)

    exits = plan.exits(True)
    grad_shapes = exits.shapes(parts, wide_two)
    first_grad, first_low, attended_grad, vec_one, expand_sums, *blocks = pl.pallas_call(
        functools.partial(middle_kernel, up_w, down_w, exits),
        out_shape=[
            shape((mine, model), FULL), shape((mine, model), LOW), shape((mine, model), LOW),
            shape((8, model), FULL), shape((8, model), FULL),
        ] + grad_shapes,
        grid=(chunks,),
        in_specs=[
            IN_SMEM, full_rows, full_rows, chunk_block, full_rows, full_rows, fixed((mine, LANES)),
            fixed((16, model)), full_rows,
        ] + [ANYWHERE] * (len(up_w.arrays) + len(down_w.arrays)),
        out_specs=[full_rows, full_rows, full_rows, fixed((8, model)), fixed((8, model))]
        + [fixed(g.shape) for g in grad_shapes],
        scratch_shapes=[
            pltpu.VMEM((parts, model, wide_two), LOW),
            pltpu.VMEM((parts, model, wide_three), LOW),
            pltpu.SemaphoreType.DMA((up_w.count(),)),
            pltpu.SemaphoreType.DMA((down_w.count(),)),
            pltpu.VMEM((model, mine), LOW),
            pltpu.VMEM((mine, model), FULL),
            pltpu.VMEM((model, CHUNK), FULL),
            pltpu.VMEM((model, width), FULL),
        ],
        compiler_params=params(1),
        cost_estimate=cost(14 * dot_cost, 30 * MIB),
        name="middle",
    )(
        table, second_low, normed_low, slope, second_grad, unit, inv, small, attended,
        *up_w.arrays, *down_w.arrays,
    )
    sums_two = plan.reduce(blocks, names, True)

    input_grad, sums_one = first_grad, 0.0
    few_pairs = pairs // 2
    for turn, lot in enumerate((high_names, low_names)):
        last = turn == 1
        first = lot[0] * width // LANES
        wide = len(lot) * width

        def from_block(offset, first=first):
            return pl.BlockSpec((mine, LANES), lambda i: (0, i + first + offset))

        lot_block = pl.BlockSpec((mine, LANES), lambda i: (0, i))
        dq, dq_sum, dk, dv, away_k, away_v = pl.pallas_call(
            functools.partial(attend_back_kernel, first),
            out_shape=[
                shape((mine, wide), LOW), shape((8, wide), FULL), shape((mine, wide), FULL),
                shape((mine, wide), FULL), shape((mine, wide), LOW), shape((mine, wide), LOW),
            ],
            grid=(few_pairs,),
            in_specs=[
                from_block(0), from_block(0), from_block(0), from_block(0), from_block(0),
                from_block(pairs), from_block(pairs), fixed((all_rows, HD)), fixed((mine, HD)),
                fixed((pad_heads, mine)),
            ],
            out_specs=[lot_block, pl.BlockSpec((8, LANES), lambda i: (0, i))] + [lot_block] * 4,
            compiler_params=params(1),
            cost_estimate=cost(10 * heads * score_cost, 8 * MIB, heads * mine * all_rows // 2),
            name="attend_back",
        )(
            query, attended_grad, attended, key_value, other, key_value, other, extra_k, extra_q,
            log_total,
        )
        added = plan.swap(jnp.concatenate([away_k, away_v], axis=1), 1)
        index = [i for i, names_here in enumerate(qkv_w.slices) if names_here == lot]
        part_w = Blocks(
            [qkv_w.arrays[i] for i in index], [lot] * len(index), [qkv_w.table_rows[i] for i in index]
        )
        exits = plan.exits(turn == 0)
        grad_shapes = exits.shapes(len(lot), wide_one)
        input_grad, *blocks = pl.pallas_call(
            functools.partial(input_kernel, part_w, exits, lot),
            out_shape=[shape((mine, model), LOW if last else FULL)] + grad_shapes,
            in_specs=[IN_SMEM] + [IN_VMEM] * 11 + [ANYWHERE] * len(part_w.arrays),
            out_specs=[IN_VMEM] * (1 + len(grad_shapes)),
            scratch_shapes=[
                pltpu.VMEM((parts, model, wide_one), LOW),
                pltpu.VMEM((LANES, model), FULL),
                pltpu.VMEM((model, wide_one), FULL),
                pltpu.SemaphoreType.DMA((part_w.count(),)),
            ],
            compiler_params=params(),
            cost_estimate=cost(3 * dot_cost, 12 * MIB),
            name="input_grad",
        )(table, x, dq, dq_sum, dk, dv, added, input_grad, vec_one, vec_two, expand_sums, pick, *part_w.arrays)
        sums_one = sums_one + plan.reduce(blocks, lot, turn == 0)
    input_rows = plan.release([input_grad[:block], input_grad[block:]]).astype(FULL)
    quarter = rows // parts
    own = lax.dynamic_slice_in_dim(sums_one[:, three : three + 6], plan.place * quarter, quarter, 0)
    return (
        layer_out[:, None],
        input_rows[:, None],
        sums_one[:, :width],
        sums_one[:, width : 2 * width],
        sums_one[:, 2 * width : three],
        sums_two[:, hidden:].T,
        sums_two[:, :hidden],
        sums_three.T,
        sums_one[:few, three + 7],
        sums_one[few : 2 * few, three + 7],
        sums_one[:, three + 6],
        own[:, 0],
        own[:, 1],
        own[:, 2],
        own[:, 3],
        own[:, 4],
        own[:, 5],
    )


def solution(mesh):
    rows = P(None, "fsdp", "tensor", None)
    split = P("fsdp", "tensor")
    turned = P("tensor", "fsdp")
    heads = P(("tensor", "fsdp"))
    model = P("fsdp")
    spread = P(("fsdp", "tensor"))
    return jax.shard_map(
        shards,
        mesh=mesh,
        in_specs=(rows, P(None, "fsdp"), rows, split, split, split, turned, split, turned)
        + (heads,) * 3
        + (model,) * 6,
        out_specs=(rows, rows, split, split, split, turned, split, turned)
        + (heads,) * 3
        + (spread,) * 6,
        check_vma=False,
    )
```

```python
import functools
import math

import jax
import jax.numpy as jnp
from jax import lax
from jax.experimental import pallas as pl
from jax.experimental.pallas import tpu as pltpu
from jax.sharding import PartitionSpec as P

HD = 64
EPS = 1e-05
DEAD = -8000000000.0
ROOT_HALF = 0.7071067811865476
DENSITY = 0.3989422804014327
LOG2E = 1.4426950408889634
SCALE2 = 0.125 * LOG2E
BOTH = ("fsdp", "tensor")
LOW = jnp.bfloat16
FULL = jnp.float32
LANES = 128
CHUNK = 768
QUERIES = 512
ROWS = 128
MIB = 1 << 20
NT = (((1,), (1,)), ((), ()))
SMALL = 64

IN_VMEM = pl.BlockSpec(memory_space=pltpu.VMEM)
IN_SMEM = pl.BlockSpec(memory_space=pltpu.SMEM)
ANYWHERE = pl.BlockSpec(memory_space=pl.ANY)


def shape(dims, dtype):
    return jax.ShapeDtypeStruct(dims, dtype)


def fixed(dims):
    return pl.BlockSpec(dims, lambda i: (0,) * len(dims))


def params(grid=0, vmem=56):
    return pltpu.CompilerParams(
        vmem_limit_bytes=vmem * MIB, dimension_semantics=("arbitrary",) * grid if grid else None
    )


def cost(flops, touched, exps=0, weight=20):
    return pl.CostEstimate(
        flops=int(weight * flops), bytes_accessed=int(weight * touched), transcendentals=int(weight * exps)
    )


def mm(left, right):
    return jnp.dot(left, right, preferred_element_type=FULL)


def mm_nt(left, right):
    return lax.dot_general(left, right, NT, preferred_element_type=FULL)


def flip(value):
    return value.astype(FULL).T.astype(value.dtype)


class Blocks:
    def __init__(self, pieces, width):
        self.pieces, self.width = pieces, width
        self.arrays = [p[0] for p in pieces]

    def count(self):
        return sum(len(p[1]) for p in self.pieces)

    def copies(self, table, refs, scratch, sems, wanted=None):
        found = {}
        at = 0
        for ref, (_, slices, lane, where) in zip(refs, self.pieces):
            rows = ref.shape[1]
            start = 0 if where is None else pl.multiple_of(table[where[0], where[1]], 16)
            for place, s in enumerate(slices):
                if wanted is not None and s not in wanted:
                    continue
                found.setdefault(s, []).append(
                    pltpu.make_async_copy(
                        ref.at[place, :, pl.ds(lane, self.width)],
                        scratch.at[s, pl.ds(start, rows), :],
                        sems.at[at],
                    )
                )
                at += 1
        return found


def begin(copies):
    for group in copies.values():
        for copy in group:
            copy.start()


def finish(group):
    for copy in group:
        copy.wait()


def project_kernel(blocks, table, x_ref, other_ref, pick_ref, *rest):
    n = len(blocks.arrays)
    refs, (q_ref, kv_ref, other_kv_ref, small_ref, w, sems) = rest[:n], rest[n:]
    copies = blocks.copies(table, refs, w, sems)
    begin(copies)
    parts = len(copies)
    third = q_ref.shape[1] // parts
    base = 3 * third // LANES * LANES
    skip = 3 * third - base
    small_ref[...] = jnp.zeros_like(small_ref)
    lead = third // LANES * LANES
    queries, keys, values, other_keys, other_values = [], [], [], [], []
    for s in range(parts):
        finish(copies[s])
        turned = w[s, :, base:].astype(FULL).T
        few = turned[skip : skip + 8]
        if s == 0:
            small_ref[0:8] = few
        small_ref[8 + s : 9 + s] = few[6:7]
        bias = mm(few.astype(LOW), pick_ref[...])[7:8]
        y = mm(x_ref[...], w[s])
        queries.append(y[:, :third] + bias[:, :third])
        keys.append(y[:, third : 2 * third])
        values.append(y[:, 2 * third : 3 * third] + bias[:, third:])
        y = mm(other_ref[...], w[s, :, lead:])
        other_keys.append(y[:, third - lead : 2 * third - lead])
        other_values.append(y[:, 2 * third - lead : 3 * third - lead] + bias[:, third:])
    q_ref[...] = jnp.concatenate(queries, axis=1).astype(LOW)
    width = q_ref.shape[1]
    for ref, k, v in ((kv_ref, keys, values), (other_kv_ref, other_keys, other_values)):
        ref[:, :width] = jnp.concatenate(k, axis=1).astype(LOW)
        ref[:, width:] = jnp.concatenate(v, axis=1).astype(LOW)


def attend_kernel(q_ref, ko, ke, vo, ve, xk_ref, xq_ref, att_ref, lse_ref):
    pair = pl.program_id(0)
    k = jnp.concatenate([ko[...], ke[...]], axis=0)
    v_t = flip(jnp.concatenate([vo[...], ve[...]], axis=0))
    q = q_ref[...]
    rows = q.shape[0]
    ones = jnp.ones((16, k.shape[0]), LOW)
    outs = []
    for h in range(2):
        side = slice(HD * h, HD * h + HD)
        kh = jnp.concatenate([k[:, side], xk_ref[...]], axis=1)
        qh = jnp.concatenate([q[:, side], xq_ref[...]], axis=1)
        vt = jnp.concatenate([v_t[side], ones], axis=0)
        got = []
        for start in range(0, rows, QUERIES):
            span = slice(start, start + QUERIES)
            scores = mm_nt(kh, qh[span])
            top = jnp.max(scores, axis=0, keepdims=True)
            raised = jnp.exp2((scores - top) * SCALE2).astype(LOW)
            o = mm(vt, raised)
            denom = o[HD : HD + 1]
            got.append(o[:HD] * (1.0 / denom))
            lse_ref[pl.ds(2 * pair + h, 1), span] = top * SCALE2 + jnp.log2(denom)
        outs.append(jnp.concatenate(got, axis=1))
    att_ref[...] = jnp.concatenate(outs, axis=0).T.astype(LOW)


def attend_back_kernel(
    first, q_ref, g_ref, att_ref, ko, ke, vo, ve, xk_ref, xq_ref, lse_ref,
    dq_ref, sum_ref, dk_ref, dv_ref, ak_ref, av_ref,
):
    pair = pl.program_id(0) + first
    k = jnp.concatenate([ko[...], ke[...]], axis=0)
    v = jnp.concatenate([vo[...], ve[...]], axis=0)
    k_t = flip(k)
    q, g = q_ref[...], g_ref[...]
    rows = q.shape[0]
    product = (g.astype(FULL) * att_ref[...].astype(FULL)).T
    dqs, dks, dvs = [], [], []
    for h in range(2):
        side = slice(HD * h, HD * h + HD)
        kh = jnp.concatenate([k[:, side], xk_ref[...]], axis=1)
        qh = jnp.concatenate([q[:, side], xq_ref[...]], axis=1)
        inner = jnp.sum(product[side], axis=0, keepdims=True)
        lse = lse_ref[pl.ds(2 * pair + h, 1), :]
        vh, gh, qs = v[:, side], g[:, side], q[:, side]
        dk = dv = None
        got = []
        for start in range(0, rows, QUERIES):
            span = slice(start, start + QUERIES)
            probs = jnp.exp2(mm_nt(kh, qh[span]) * SCALE2 - lse[:, span])
            prob_grad = mm_nt(vh, gh[span])
            score_grad = (probs * (prob_grad - inner[:, span])).astype(LOW)
            more_v = mm(probs.astype(LOW), gh[span])
            more_k = mm(score_grad, qs[span])
            dv = more_v if dv is None else dv + more_v
            dk = more_k if dk is None else dk + more_k
            got.append(mm(k_t[side], score_grad))
        dqs.append(jnp.concatenate(got, axis=1))
        dks.append(dk)
        dvs.append(dv)
    dq = jnp.concatenate(dqs, axis=0).T * 0.125
    dq_ref[...] = dq.astype(LOW)
    sum_ref[...] = jnp.broadcast_to(jnp.sum(dq, axis=0, keepdims=True), sum_ref.shape)
    dk = jnp.concatenate(dks, axis=1) * 0.125
    dv = jnp.concatenate(dvs, axis=1)
    dk_ref[...] = dk[:rows]
    dv_ref[...] = dv[:rows]
    ak_ref[...] = dk[rows:].astype(LOW)
    av_ref[...] = dv[rows:].astype(LOW)


def means(value):
    return jnp.mean(value, axis=-1, keepdims=True)


def normalize(summed):
    center = summed - means(summed)
    inv = lax.rsqrt(means(center * center) + EPS)
    return center * inv, inv


def norm_back(grad, gain, unit, inv):
    scaled = grad * gain
    return inv * (scaled - means(scaled) - unit * means(scaled * unit))


def total(value):
    return jnp.sum(value, axis=0, keepdims=True)


def expand_kernel(blocks, table, x_ref, att_ref, small_ref, *rest):
    n = len(blocks.arrays)
    refs = rest[:n]
    normed_ref, unit_ref, inv_ref, low_ref, act_ref, slope_ref, w, attn, sems = rest[n:]
    copies = blocks.copies(table, refs, w, sems)
    parts = len(copies)
    step = pl.program_id(0)
    hidden = x_ref.shape[1]
    width = hidden // parts

    @pl.when(step == 0)
    def _():
        begin(copies)
        for s in range(parts):
            finish(copies[s])
        value = None
        for s in range(parts):
            more = mm_nt(att_ref[:, width * s : width * s + width], w[s, :, hidden : hidden + width])
            value = more if value is None else value + more
        attn[...] = value

        @pl.loop(0, x_ref.shape[0] // ROWS)
        def _(i):
            span = pl.ds(pl.multiple_of(i * ROWS, ROWS), ROWS)
            summed = x_ref[span].astype(FULL) + attn[span] + small_ref[0:1]
            unit, inv = normalize(summed)
            normed = unit * small_ref[1:2] + small_ref[2:3]
            normed_ref[span] = normed
            unit_ref[span] = unit
            inv_ref[span] = jnp.broadcast_to(inv, (ROWS, LANES))
            low_ref[span] = normed.astype(LOW)

    per = hidden // CHUNK
    s, lanes = step // per, pl.ds(pl.multiple_of(step % per * CHUNK, CHUNK), CHUNK)
    bias = small_ref[pl.ds(8 + s, 1), lanes]
    upper = mm(low_ref[...], w[s, :, lanes]) + bias
    below = 0.5 * (1.0 + lax.erf(upper * ROOT_HALF))
    act_ref[...] = (upper * below).astype(LOW)
    slope_ref[...] = (below + upper * jnp.exp(-0.5 * upper * upper) * DENSITY).astype(LOW)


def shrink_kernel(blocks, table, act_ref, normed_ref, small_ref, cot_ref, live_ref, *rest):
    n = len(blocks.arrays)
    refs = rest[:n]
    out_ref, grad_ref, low_ref, vec_ref, w, acc, sems = rest[n:]
    copies = blocks.copies(table, refs, w, sems)
    step = pl.program_id(0)
    hidden = normed_ref.shape[1]
    per = hidden // CHUNK
    s, lanes = step // per, pl.ds(pl.multiple_of(step % per * CHUNK, CHUNK), CHUNK)

    @pl.when(step == 0)
    def _():
        begin(copies)

    for part, group in copies.items():

        @pl.when(step == part * per)
        def _(group=group):
            finish(group)

    more = mm_nt(act_ref[...], w[s, :, lanes])

    @pl.when(step == 0)
    def _():
        acc[...] = more

    @pl.when(step > 0)
    def _():
        acc[...] += more

    @pl.when(step == pl.num_programs(0) - 1)
    def _():
        vec_ref[...] = jnp.zeros_like(vec_ref)

        @pl.loop(0, normed_ref.shape[0] // ROWS)
        def _(i):
            span = pl.ds(pl.multiple_of(i * ROWS, ROWS), ROWS)
            summed = normed_ref[span] + acc[span] + small_ref[3:4]
            unit, inv = normalize(summed)
            out_ref[span] = (unit * small_ref[4:5] + small_ref[5:6]).astype(LOW)
            arriving = cot_ref[span].astype(FULL) * live_ref[span, 0:1]
            grad = norm_back(arriving, small_ref[4:5], unit, inv)
            grad_ref[span] = grad
            low_ref[span] = grad.astype(LOW)
            vec_ref[0:1] += total(grad)
            vec_ref[1:2] += total(arriving * unit)
            vec_ref[2:3] += total(arriving)


class Exits:
    def __init__(self, flat, outers, rows, order, sides=(0, 1)):
        self.flat, self.outers, self.rows, self.order, self.sides = flat, outers, rows, order, sides

    def height(self):
        return 2 * self.outers * self.rows if self.flat else len(self.sides) * self.outers * self.rows

    def shapes(self, slices, width):
        if self.flat:
            return [shape((slices, self.height(), width), LOW)]
        return [shape((self.outers, slices, self.rows, width), LOW)] * len(self.sides)

    def arrange(self, table, source, target):
        if self.flat:
            target[...] = source[...]
            return
        at = 0
        for side in self.sides:
            for n in self.order:
                start = pl.multiple_of(table[side, n], 16)
                target[at : at + self.rows] = source[pl.ds(start, self.rows), :]
                at += self.rows

    def emit(self, value, refs, s, lanes):
        value = value.astype(LOW)
        if self.flat:
            refs[0][s, :, lanes] = value
            return
        at = 0
        for ref in refs:
            for i in range(self.outers):
                ref[i, s, :, lanes] = value[at : at + self.rows]
                at += self.rows


def shrink_grad_kernel(exits, table, low_ref, act_ref, *rest):
    outs, (natural, turned) = rest[:-2], rest[-2:]

    @pl.when(pl.program_id(0) == 0)
    def _():
        natural[...] = flip(low_ref[...])
        exits.arrange(table, natural, turned)

    exits.emit(mm(turned[...], act_ref[...]), outs, 0, slice(None))


def middle_kernel(
    ups, downs, exits, table, low_ref, normed_low_ref, slope_ref, grad_ref, unit_ref, inv_ref,
    small_ref, att_ref, *rest,
):
    n, m = len(ups.arrays), len(downs.arrays)
    up_refs, down_refs, rest = rest[:n], rest[n : n + m], rest[n + m :]
    first_ref, first_low_ref, att_grad_ref, vec_ref, expand_ref = rest[:5]
    outs = rest[5:-7]
    up_w, down_w, up_sems, down_sems, natural, turned, acc = rest[-7:]
    up_copies = ups.copies(table, up_refs, up_w, up_sems)
    down_copies = downs.copies(table, down_refs, down_w, down_sems)
    parts = len(up_copies)
    step = pl.program_id(0)
    hidden = unit_ref.shape[1]
    width = hidden // parts
    per = hidden // CHUNK
    s, lanes = step // per, pl.ds(pl.multiple_of(step % per * CHUNK, CHUNK), CHUNK)

    @pl.when(step == 0)
    def _():
        for part in range(parts):
            begin({0: down_copies[part], 1: up_copies[part]})
        natural[...] = flip(normed_low_ref[...])
        exits.arrange(table, natural, turned)
        expand_ref[...] = jnp.zeros_like(expand_ref)

    for part in range(parts):

        @pl.when(step == part * per)
        def _(part=part):
            finish(down_copies[part])
            finish(up_copies[part])

    upper_grad = mm(low_ref[...], down_w[s, :, lanes]) * slope_ref[...].astype(FULL)
    expand_ref[pl.ds(s, 1), lanes] = total(upper_grad)
    upper_low = upper_grad.astype(LOW)
    exits.emit(mm(turned[...], upper_low), outs, s, lanes)
    more = mm_nt(upper_low, up_w[s, :, lanes])

    @pl.when(step == 0)
    def _():
        acc[...] = more

    @pl.when(step > 0)
    def _():
        acc[...] += more

    @pl.when(step == pl.num_programs(0) - 1)
    def _():
        vec_ref[...] = jnp.zeros_like(vec_ref)

        @pl.loop(0, unit_ref.shape[0] // ROWS)
        def _(i):
            span = pl.ds(pl.multiple_of(i * ROWS, ROWS), ROWS)
            grad = acc[span] + grad_ref[span]
            unit = unit_ref[span]
            first = norm_back(grad, small_ref[1:2], unit, inv_ref[span, 0:1])
            first_ref[span] = first
            first_low_ref[span] = first.astype(LOW)
            vec_ref[0:1] += total(first)
            vec_ref[1:2] += total(grad * unit)
            vec_ref[2:3] += total(grad)

        natural[...] = flip(first_low_ref[...])
        exits.arrange(table, natural, turned)
        grads = []
        for part in range(parts):
            o = up_w[part, :, hidden : hidden + width]
            grads.append(mm(first_low_ref[...], o))
            value = mm(turned[...], att_ref[:, width * part : width * part + width])
            exits.emit(value, outs, part, slice(hidden, hidden + width))
        att_grad_ref[...] = jnp.concatenate(grads, axis=1).astype(LOW)


def input_kernel(
    blocks, exits, slices, table, x_ref, dq_ref, dqs_ref, dk_ref, dv_ref, add_ref, sofar_ref,
    one_ref, two_ref, expand_ref, pick_ref, *rest,
):
    n = len(blocks.arrays)
    refs, rest = rest[:n], rest[n:]
    grad_ref = rest[0]
    w, vecs, natural, turned, columns, sorted_columns, sems = rest[-7:]
    outs = rest[1:-7]
    copies = blocks.copies(table, refs, w, sems, slices)
    begin(copies)
    natural[...] = flip(x_ref[...])
    exits.arrange(table, natural, turned)
    rows = x_ref.shape[0]
    wide = dq_ref.shape[1]
    width = wide // len(slices)
    dq = dq_ref[...]
    dk = (dk_ref[...] + add_ref[:, :wide].astype(FULL)).astype(LOW)
    dv_full = dv_ref[...] + add_ref[:, wide:].astype(FULL)
    dv = dv_full.astype(LOW)
    dvs = total(dv_full)
    base = 3 * width // LANES * LANES
    skip = 3 * width - base
    vecs[...] = jnp.zeros_like(vecs)
    vecs[skip : skip + 3] = one_ref[0:3]
    vecs[skip + 3 : skip + 6] = two_ref[0:3]
    grad = sofar_ref[...]
    for i, s in enumerate(slices):
        side = slice(width * i, width * i + width)
        low = jnp.concatenate([dq[:, side], dk[:, side], dv[:, side], jnp.zeros((rows, SMALL), LOW)], axis=1)
        value = mm(turned[...], low)
        sums = jnp.concatenate([dqs_ref[:, side], jnp.broadcast_to(dvs[:, side], (8, width))], axis=1)
        high = sums.astype(LOW)
        rest_of = (sums - high.astype(FULL)).astype(LOW)
        heads = mm_nt(high, pick_ref[...]) + mm_nt(rest_of, pick_ref[...])
        vecs[skip + 6 : skip + 7] = expand_ref[s : s + 1]
        vecs[skip + 7 : skip + 8] = heads[0:1]
        columns[...] = vecs[...].T
        exits.arrange(table, columns, sorted_columns)
        value = jnp.concatenate([value[:, :base], value[:, base:] + sorted_columns[...]], axis=1)
        exits.emit(value, outs, i, slice(None))
        finish(copies[s])
        grad = grad + mm_nt(low, w[s])
    grad_ref[...] = grad.astype(grad_ref.dtype)


class Plan:
    def __init__(self, rows):
        self.parts = lax.axis_size("tensor")
        self.owners = lax.axis_size("fsdp")
        self.place = lax.axis_index("tensor")
        self.owner = lax.axis_index("fsdp")
        self.core = self.owner % 2
        self.outer = self.owner // 2
        self.outers = self.owners // 2
        self.rows = rows
        self.flat = rows % 16 != 0
        self.bits = [1 << n for n in range((self.outers - 1).bit_length())]
        rising = list(range(self.outers))
        falling = [0]
        for bit in self.bits[::-1]:
            falling = falling + [n ^ bit for n in falling]
        self.orders = (rising, falling)
        own = jnp.array([rising, rising], jnp.int32) ^ self.outer
        core = jnp.array([0, 1], jnp.int32)[:, None] ^ self.core
        self.table = ((own * 2 + core) * rows).astype(jnp.int32)

    def swap(self, value, bit):
        return lax.ppermute(value, "fsdp", [(n, n ^ bit) for n in range(self.owners)])

    def turn(self, value, by):
        n = self.parts
        return lax.ppermute(value, "tensor", [(i, (i + by) % n) for i in range(n)])

    def trade(self, turn, back):
        pairs = []
        half = self.parts // 2
        for owner in range(self.owners):
            for place in range(self.parts):
                micro = (place + turn) % 2
                there = (owner - owner % 2 + place // half) * self.parts + 2 * micro + owner % 2
                here = owner * self.parts + place
                pairs.append((there, here) if back else (here, there))
        return pairs

    def collect(self, value):
        return [
            lax.ppermute(
                lax.dynamic_index_in_dim(value, (self.place + turn) % 2, 0, False),
                BOTH,
                self.trade(turn, False),
            )
            for turn in range(2)
        ]

    def release(self, blocks):
        first, second = [
            lax.ppermute(block, BOTH, self.trade(turn, True)) for turn, block in enumerate(blocks)
        ]
        even = self.place % 2 == 0
        return jnp.stack([jnp.where(even, first, second), jnp.where(even, second, first)])

    def around(self, shard):
        return [shard] + [self.turn(shard, by) for by in range(1, self.parts)]

    def gather(self, lot):
        held = jnp.stack(lot)
        if self.flat:
            held = held[None]
            for bit in self.bits:
                held = jnp.concatenate([held, self.swap(held, 2 * bit)])
            return [(self.natural(held, self.swap(held, 1), self.orders[0]), None)]
        others = range(1, self.outers)
        return [(held, (0, 0))] + [(self.swap(held, 2 * n), (0, n)) for n in others]

    def both_cores(self, pieces):
        if self.flat:
            return pieces
        return pieces + [(self.swap(v, 1), (1, n)) for v, (_, n) in pieces]

    def natural(self, mine, other, order):
        where = jnp.array([order.index(n) for n in range(self.outers)])
        both = []
        for n in range(self.outers):
            at = where[n ^ self.outer]
            pair = [lax.dynamic_index_in_dim(v, at, 0, False) for v in (mine, other)]
            both.append(jnp.where(self.core == 0, pair[0], pair[1]))
            both.append(jnp.where(self.core == 0, pair[1], pair[0]))
        return jnp.concatenate(both, axis=1)

    def exits(self, sides=(0, 1)):
        return Exits(self.flat, self.outers, self.rows, self.orders[0], sides)


class Reduction:
    def __init__(self, plan, names, keep, send=None):
        self.plan, self.names = plan, names
        self.halving = send is None
        if self.halving:
            keep, send = self.sort(keep, plan.orders[1])
        self.terms = [keep, plan.swap(send, 1)]

    def sort(self, value, order):
        plan, names = self.plan, self.names
        value = value.reshape(len(names), plan.outers, 2, plan.rows, -1)
        size = (len(names), 1, 1, plan.rows, value.shape[-1])
        return [
            jnp.concatenate(
                [lax.dynamic_slice(value, (0, n ^ plan.outer, core, 0, 0), size)[:, 0] for n in order],
                axis=1,
            ).swapaxes(0, 1)
            for core in (plan.core, 1 - plan.core)
        ]

    def spread(self):
        plan = self.plan
        if self.halving:
            left = plan.outers
            for bit in plan.bits:
                left //= 2
                away = sum(t[left:].astype(FULL) for t in self.terms).astype(LOW)
                self.terms = [t[:left] for t in self.terms] + [plan.swap(away, 2 * bit)]
            return self.terms
        sent = [
            sum(t[n].astype(FULL) for t in self.terms).astype(LOW) for n in range(1, plan.outers)
        ]
        got = [plan.swap(v, 2 * n + 2)[None] for n, v in enumerate(sent)]
        self.terms = [t[:1] for t in self.terms] + got
        return sent

    def turn(self):
        terms = [sum(t[0, i].astype(FULL) for t in self.terms) for i in range(len(self.names))]
        self.sent = [t.astype(LOW) for t, by in zip(terms, self.names) if by]
        self.terms = [t for t, by in zip(terms, self.names) if not by]
        turns = [by for by in self.names if by]
        self.terms += [self.plan.turn(t, -by) for t, by in zip(self.sent, turns)]
        return self.sent

    def total(self):
        return sum(t.astype(FULL) for t in self.terms)


def after(value, *first):
    return lax.optimization_barrier((value, first))[0]


def shards(
    tokens, lengths, cotangent, query_proj, key_proj, value_proj, output_proj, expand_proj,
    shrink_proj, query_bias, value_bias, expand_bias, output_bias, attn_gain, attn_shift,
    shrink_bias, ffn_gain, ffn_shift,
):
    rows, width = query_proj.shape
    plan = Plan(rows)
    parts = plan.parts
    hidden = expand_proj.shape[1]
    few = query_bias.shape[0]
    block = tokens.shape[2]
    mine = 2 * block
    model = tokens.shape[3]
    three = 3 * width
    table = plan.table
    half = parts // 2
    low_names, high_names, names = list(range(half)), list(range(half, parts)), list(range(parts))

    smalls = [output_bias, attn_gain, attn_shift, shrink_bias, ffn_gain, ffn_shift, expand_bias]
    heads_biases = jnp.pad(jnp.concatenate([query_bias, value_bias]), (0, rows - 2 * few))
    blank = jnp.zeros((rows,), LOW)
    pack_one = jnp.concatenate(
        [query_proj, key_proj, value_proj, jnp.stack(smalls + [heads_biases] + [blank] * (SMALL - 8)).T],
        axis=1,
    )
    gap = jnp.zeros((rows, -width % LANES), LOW)
    pack_two = jnp.concatenate([expand_proj, output_proj.T, gap, shrink_proj.T], axis=1)
    wide_one, wide_two, wide_three = pack_one.shape[1], hidden + width, hidden
    edge = pack_two.shape[1] - wide_three
    ones = plan.around(pack_one)
    ups = plan.around(after(pack_two[:, :edge], *ones[1:]))
    one_part = plan.gather(ones)
    own_tokens = plan.collect(after(tokens[:, 0], *ups[1:]))
    x = jnp.concatenate(own_tokens)
    other_x = plan.swap(x, 1)
    up_part = plan.gather([after(t, *[a for a, _ in one_part[1:]]) for t in ups])
    qkv_w = Blocks([(a, names, 0, w) for a, w in plan.both_cores(one_part)], wide_one)
    place = jnp.arange(model)[:, None]
    head = jnp.arange(2 * width)[None, :]
    inside = head % width
    pick = (place == inside // few * rows + inside % few + few * (head // width)).astype(LOW)

    micro, parity = plan.place // 2, plan.place % 2
    seen = jnp.where(parity == plan.core, lengths, plan.swap(lengths, 1))[:, 0]
    length = jnp.where(micro == 0, seen[0], seen[1])

    def slots_of(core):
        return jnp.concatenate(
            [block * (2 * core + (micro + n) % 2) + jnp.arange(block) for n in range(2)]
        )

    row_slots = slots_of(plan.core)
    live_rows = jnp.broadcast_to((row_slots < length).astype(FULL)[:, None], (mine, LANES))
    live = jnp.concatenate([row_slots, slots_of(1 - plan.core)]) < length
    lead = jnp.arange(HD)[None, :] == 0
    extra_k = jnp.where(lead & ~live[:, None], DEAD, 0.0).astype(LOW)
    extra_q = jnp.broadcast_to(lead, (mine, HD)).astype(LOW)

    dot_cost = 2 * mine * model * model
    query, key_value, other, small = pl.pallas_call(
        functools.partial(project_kernel, qkv_w),
        out_shape=[
            shape((mine, model), LOW), shape((mine, 2 * model), LOW), shape((mine, 2 * model), LOW),
            shape((16, model), FULL),
        ],
        in_specs=[IN_SMEM, IN_VMEM, IN_VMEM, IN_VMEM] + [ANYWHERE] * len(qkv_w.arrays),
        out_specs=[IN_VMEM] * 4,
        scratch_shapes=[
            pltpu.VMEM((parts, model, wide_one), LOW),
            pltpu.SemaphoreType.DMA((qkv_w.count(),)),
        ],
        compiler_params=params(),
        cost_estimate=cost(3 * dot_cost, 8 * MIB, 0, 0.05),
        name="project",
    )(table, x, other_x, pick, *qkv_w.arrays)
    down_own = after(pack_two[:, edge:], x)
    downs = {by: plan.turn(down_own, by) for by in range(1, parts, 2)}
    query = after(query, *downs.values())
    pairs = model // LANES
    heads = 2 * pairs
    pad_heads = -(-heads // 8) * 8
    all_rows = 2 * mine

    def lane_block(offset):
        return pl.BlockSpec((mine, LANES), lambda i: (0, i + offset))

    score_cost = 2 * mine * all_rows * HD
    attended, log_total = pl.pallas_call(
        attend_kernel,
        out_shape=[shape((mine, model), LOW), shape((pad_heads, mine), FULL)],
        grid=(pairs,),
        in_specs=[
            lane_block(0), lane_block(0), lane_block(0), lane_block(pairs), lane_block(pairs),
            fixed((all_rows, HD)), fixed((mine, HD)),
        ],
        out_specs=[lane_block(0), fixed((pad_heads, mine))],
        compiler_params=params(1),
        cost_estimate=cost(6 * heads * score_cost, 6 * MIB, heads * mine * all_rows, 0.05),
        name="attend",
    )(query, key_value, other, key_value, other, extra_k, extra_q)

    down_own = after(down_own, attended)
    downs.update({by: plan.turn(down_own, by) for by in range(2, parts, 2)})
    up_pieces = plan.both_cores([(after(a, attended), w) for a, w in up_part])
    up_w = Blocks([(a, names, 0, w) for a, w in up_pieces], edge)
    there = [a for a, _ in up_pieces]
    down_part = plan.gather([after(t, *there) for t in [down_own] + [downs[n] for n in range(1, parts)]])
    own_cot = plan.collect(after(cotangent[:, 0], *there))
    chunks = parts * hidden // CHUNK
    per = hidden // CHUNK
    chunk_block = pl.BlockSpec((mine, CHUNK), lambda i: (0, i))
    full_rows = fixed((mine, model))
    normed, unit, inv, normed_low, active, slope = pl.pallas_call(
        functools.partial(expand_kernel, up_w),
        out_shape=[
            shape((mine, model), FULL), shape((mine, model), FULL), shape((mine, LANES), FULL),
            shape((mine, model), LOW), shape((mine, parts * hidden), LOW), shape((mine, parts * hidden), LOW),
        ],
        grid=(chunks,),
        in_specs=[IN_SMEM, full_rows, full_rows, fixed((16, model))] + [ANYWHERE] * len(up_w.arrays),
        out_specs=[full_rows, full_rows, fixed((mine, LANES)), full_rows, chunk_block, chunk_block],
        scratch_shapes=[
            pltpu.VMEM((parts, model, edge), LOW),
            pltpu.VMEM((mine, model), FULL),
            pltpu.SemaphoreType.DMA((up_w.count(),)),
        ],
        compiler_params=params(1),
        cost_estimate=cost(8 * dot_cost, 20 * MIB, 0, 0.05),
        name="expand",
    )(table, x, attended, small, *up_w.arrays)
    cot = jnp.concatenate(own_cot)
    down_w = Blocks(
        [(a, names, 0, w) for a, w in plan.both_cores([(after(a, normed_low), w) for a, w in down_part])],
        wide_three,
    )
    layer_rows, second_grad, second_low, vec_two = pl.pallas_call(
        functools.partial(shrink_kernel, down_w),
        out_shape=[
            shape((mine, model), LOW), shape((mine, model), FULL), shape((mine, model), LOW), shape((8, model), FULL),
        ],
        grid=(chunks,),
        in_specs=[
            IN_SMEM, chunk_block, full_rows, fixed((16, model)), full_rows, fixed((mine, LANES)),
        ] + [ANYWHERE] * len(down_w.arrays),
        out_specs=[full_rows, full_rows, full_rows, fixed((8, model))],
        scratch_shapes=[
            pltpu.VMEM((parts, model, wide_three), LOW),
            pltpu.VMEM((mine, model), FULL),
            pltpu.SemaphoreType.DMA((down_w.count(),)),
        ],
        compiler_params=params(1),
        cost_estimate=cost(5 * dot_cost, 16 * MIB),
        name="shrink",
    )(table, active, normed, small, cot, live_rows, *down_w.arrays)
    def shrink_grad(sides, ready):
        exits = plan.exits(sides)
        if plan.flat:
            grad_block = [pl.BlockSpec((1, model, CHUNK), lambda i: (i // per, 0, i % per))]
        else:
            grad_block = [
                pl.BlockSpec((plan.outers, 1, rows, CHUNK), lambda i: (0, i // per, 0, i % per))
            ] * len(sides)
        return pl.pallas_call(
            functools.partial(shrink_grad_kernel, exits),
            out_shape=exits.shapes(parts, hidden),
            grid=(chunks,),
            in_specs=[IN_SMEM, full_rows, chunk_block],
            out_specs=grad_block,
            scratch_shapes=[pltpu.VMEM((model, mine), LOW), pltpu.VMEM((exits.height(), mine), LOW)],
            compiler_params=params(1),
            cost_estimate=cost(4 * dot_cost // (3 - len(sides)), 9 * MIB),
            name="shrink_grad",
        )(table, ready, active)

    if plan.flat:
        three_red = Reduction(plan, names, *shrink_grad((0, 1), second_low))
    else:
        (send,) = shrink_grad((1,), second_low)
        (keep,) = shrink_grad((0,), after(second_low, send))
        three_red = Reduction(plan, names, keep, send)
    three_sent = three_red.spread()
    layer_rows = after(layer_rows, *three_sent)
    layer_out = plan.release([layer_rows[:block], layer_rows[block:]])

    exits = plan.exits()
    grad_shapes = exits.shapes(parts, wide_two)
    first_grad, first_low, attended_grad, vec_one, expand_sums, *blocks = pl.pallas_call(
        functools.partial(middle_kernel, up_w, down_w, exits),
        out_shape=[
            shape((mine, model), FULL), shape((mine, model), LOW), shape((mine, model), LOW),
            shape((8, model), FULL), shape((8, model), FULL),
        ] + grad_shapes,
        grid=(chunks,),
        in_specs=[
            IN_SMEM, full_rows, full_rows, chunk_block, full_rows, full_rows, fixed((mine, LANES)),
            fixed((16, model)), full_rows,
        ] + [ANYWHERE] * (len(up_w.arrays) + len(down_w.arrays)),
        out_specs=[full_rows, full_rows, full_rows, fixed((8, model)), fixed((8, model))]
        + [fixed(g.shape) for g in grad_shapes],
        scratch_shapes=[
            pltpu.VMEM((parts, model, edge), LOW),
            pltpu.VMEM((parts, model, wide_three), LOW),
            pltpu.SemaphoreType.DMA((up_w.count(),)),
            pltpu.SemaphoreType.DMA((down_w.count(),)),
            pltpu.VMEM((model, mine), LOW),
            pltpu.VMEM((model, mine), LOW),
            pltpu.VMEM((mine, model), FULL),
        ],
        compiler_params=params(1),
        cost_estimate=cost(14 * dot_cost, 30 * MIB),
        name="middle",
    )(
        table, after(second_low, *three_sent), normed_low, slope, second_grad, unit, inv, small, attended,
        *up_w.arrays, *down_w.arrays,
    )
    two_red = Reduction(plan, names, *blocks)
    three_sent = three_red.turn()

    few_pairs = pairs // 2

    def attend_back(lot, grad):
        first = lot[0] * width // LANES
        wide = len(lot) * width

        def from_block(offset):
            return pl.BlockSpec((mine, LANES), lambda i: (0, i + first + offset))

        lot_block = pl.BlockSpec((mine, LANES), lambda i: (0, i))
        return pl.pallas_call(
            functools.partial(attend_back_kernel, first),
            out_shape=[
                shape((mine, wide), LOW), shape((8, wide), FULL), shape((mine, wide), FULL),
                shape((mine, wide), FULL), shape((mine, wide), LOW), shape((mine, wide), LOW),
            ],
            grid=(few_pairs,),
            in_specs=[
                from_block(0), from_block(0), from_block(0), from_block(0), from_block(0),
                from_block(pairs), from_block(pairs), fixed((all_rows, HD)), fixed((mine, HD)),
                fixed((pad_heads, mine)),
            ],
            out_specs=[lot_block, pl.BlockSpec((8, LANES), lambda i: (0, i))] + [lot_block] * 4,
            compiler_params=params(1),
            cost_estimate=cost(10 * heads * score_cost, 8 * MIB, heads * mine * all_rows // 2),
            name="attend_back",
        )(
            query, grad, attended, key_value, other, key_value, other, extra_k, extra_q, log_total,
        )

    def input_step(lot, exits, got, sofar, last):
        dq, dq_sum, dk, dv, added = got
        part_w = qkv_w
        grad_shapes = exits.shapes(len(lot), wide_one)
        return pl.pallas_call(
            functools.partial(input_kernel, part_w, exits, lot),
            out_shape=[shape((mine, model), LOW if last else FULL)] + grad_shapes,
            in_specs=[IN_SMEM] + [IN_VMEM] * 11 + [ANYWHERE] * len(part_w.arrays),
            out_specs=[IN_VMEM] * (1 + len(grad_shapes)),
            scratch_shapes=[
                pltpu.VMEM((parts, model, wide_one), LOW),
                pltpu.VMEM((LANES, model), FULL),
                pltpu.VMEM((model, mine), LOW),
                pltpu.VMEM((model, mine), LOW),
                pltpu.VMEM((model, LANES), FULL),
                pltpu.VMEM((model, LANES), FULL),
                pltpu.SemaphoreType.DMA((part_w.count(),)),
            ],
            compiler_params=params(),
            cost_estimate=cost(3 * dot_cost, 12 * MIB),
            name="input_grad",
        )(table, x, dq, dq_sum, dk, dv, added, sofar, vec_one, vec_two, expand_sums, pick, *part_w.arrays)

    def cross(got):
        dq, dq_sum, dk, dv, away_k, away_v = got
        return dq, dq_sum, dk, dv, plan.swap(jnp.concatenate([away_k, away_v], axis=1), 1)

    high = cross(attend_back(high_names, after(attended_grad, *three_sent)))
    two_sent = two_red.spread()
    low = cross(attend_back(low_names, after(attended_grad, *two_sent, high[0])))
    exits = plan.exits()
    sofar, *blocks = input_step(high_names, exits, high, after(first_grad, low[0]), False)
    high_red = Reduction(plan, high_names, *blocks)
    input_grad, *blocks = input_step(low_names, exits, low, sofar, True)
    input_rows = plan.release([input_grad[:block], input_grad[block:]]).astype(FULL)
    low_red = Reduction(plan, low_names, *blocks)
    high_red.spread()
    low_red.spread()
    two_red.terms = [after(t, input_grad) for t in two_red.terms]
    for red in (two_red, high_red, low_red):
        red.turn()
    sums_one = high_red.total() + low_red.total()
    sums_two, sums_three = two_red.total(), three_red.total()
    quarter = rows // parts
    own = lax.dynamic_slice_in_dim(sums_one[:, three : three + 6], plan.place * quarter, quarter, 0)
    return (
        layer_out[:, None],
        input_rows[:, None],
        sums_one[:, :width],
        sums_one[:, width : 2 * width],
        sums_one[:, 2 * width : three],
        sums_two[:, hidden:].T,
        sums_two[:, :hidden],
        sums_three.T,
        sums_one[:few, three + 7],
        sums_one[few : 2 * few, three + 7],
        sums_one[:, three + 6],
        own[:, 0],
        own[:, 1],
        own[:, 2],
        own[:, 3],
        own[:, 4],
        own[:, 5],
    )


def solution(mesh):
    rows = P(None, "fsdp", "tensor", None)
    split = P("fsdp", "tensor")
    turned = P("tensor", "fsdp")
    heads = P(("tensor", "fsdp"))
    model = P("fsdp")
    spread = P(("fsdp", "tensor"))
    return jax.shard_map(
        shards,
        mesh=mesh,
        in_specs=(rows, P(None, "fsdp"), rows, split, split, split, turned, split, turned)
        + (heads,) * 3
        + (model,) * 6,
        out_specs=(rows, rows, split, split, split, turned, split, turned)
        + (heads,) * 3
        + (spread,) * 6,
        check_vma=False,
    )
```

```python
import functools
import math

import jax
import jax.numpy as jnp
from jax import lax
from jax.experimental import pallas as pl
from jax.experimental.pallas import tpu as pltpu
from jax.sharding import PartitionSpec as P

HD = 64
EPS = 1e-05
DEAD = -8000000000.0
ROOT_HALF = 0.7071067811865476
DENSITY = 0.3989422804014327
LOG2E = 1.4426950408889634
SCALE2 = 0.125 * LOG2E
BOTH = ("fsdp", "tensor")
LOW = jnp.bfloat16
FULL = jnp.float32
LANES = 128
CHUNK = 768
QUERIES = 512
ROWS = 128
MIB = 1 << 20
NT = (((1,), (1,)), ((), ()))
SMALL = 64

IN_VMEM = pl.BlockSpec(memory_space=pltpu.VMEM)
IN_SMEM = pl.BlockSpec(memory_space=pltpu.SMEM)
ANYWHERE = pl.BlockSpec(memory_space=pl.ANY)


def shape(dims, dtype):
    return jax.ShapeDtypeStruct(dims, dtype)


def fixed(dims):
    return pl.BlockSpec(dims, lambda i: (0,) * len(dims))


def params(grid=0, vmem=56):
    return pltpu.CompilerParams(
        vmem_limit_bytes=vmem * MIB, dimension_semantics=("arbitrary",) * grid if grid else None
    )


def cost(flops, touched, exps=0, weight=20):
    return pl.CostEstimate(
        flops=int(weight * flops), bytes_accessed=int(weight * touched), transcendentals=int(weight * exps)
    )


def mm(left, right):
    return jnp.dot(left, right, preferred_element_type=FULL)


def mm_nt(left, right):
    return lax.dot_general(left, right, NT, preferred_element_type=FULL)


def flip(value):
    return value.astype(FULL).T.astype(value.dtype)


def pace_kernel(in_ref, *rest):
    out_ref = rest[-1]
    for row in range(in_ref.shape[0]):
        for n in range(in_ref.shape[1]):
            out_ref[row, n] = in_ref[row, n]


def pace(table, *ready):
    return pl.pallas_call(
        pace_kernel,
        out_shape=shape(table.shape, table.dtype),
        in_specs=[IN_SMEM] + [ANYWHERE] * len(ready),
        out_specs=IN_SMEM,
        cost_estimate=pl.CostEstimate(flops=10**11, bytes_accessed=10**9, transcendentals=0),
        name="pace",
    )(table, *ready)


def hold(*values):
    return lax.optimization_barrier(values)


class Blocks:
    def __init__(self, pieces, width):
        self.pieces, self.width = pieces, width
        self.arrays = [p[0] for p in pieces]

    def count(self):
        return sum(len(p[1]) for p in self.pieces)

    def copies(self, table, refs, scratch, sems, wanted=None):
        found = {}
        at = 0
        for ref, (_, slices, lane, where) in zip(refs, self.pieces):
            rows = ref.shape[1]
            start = 0 if where is None else pl.multiple_of(table[where[0], where[1]], 16)
            for place, s in enumerate(slices):
                if wanted is not None and s not in wanted:
                    continue
                found.setdefault(s, []).append(
                    pltpu.make_async_copy(
                        ref.at[place, :, pl.ds(lane, self.width)],
                        scratch.at[s, pl.ds(start, rows), :],
                        sems.at[at],
                    )
                )
                at += 1
        return found


def begin(copies):
    for group in copies.values():
        for copy in group:
            copy.start()


def finish(group):
    for copy in group:
        copy.wait()


def project_kernel(blocks, table, x_ref, other_ref, pick_ref, *rest):
    n = len(blocks.arrays)
    refs, (q_ref, kv_ref, other_kv_ref, small_ref, w, sems) = rest[:n], rest[n:]
    copies = blocks.copies(table, refs, w, sems)
    begin(copies)
    parts = len(copies)
    third = q_ref.shape[1] // parts
    base = 3 * third // LANES * LANES
    skip = 3 * third - base
    small_ref[...] = jnp.zeros_like(small_ref)
    lead = third // LANES * LANES
    queries, keys, values, other_keys, other_values = [], [], [], [], []
    for s in range(parts):
        finish(copies[s])
        turned = w[s, :, base:].astype(FULL).T
        few = turned[skip : skip + 8]
        if s == 0:
            small_ref[0:8] = few
        small_ref[8 + s : 9 + s] = few[6:7]
        bias = mm(few.astype(LOW), pick_ref[...])[7:8]
        y = mm(x_ref[...], w[s])
        queries.append(y[:, :third] + bias[:, :third])
        keys.append(y[:, third : 2 * third])
        values.append(y[:, 2 * third : 3 * third] + bias[:, third:])
        y = mm(other_ref[...], w[s, :, lead:])
        other_keys.append(y[:, third - lead : 2 * third - lead])
        other_values.append(y[:, 2 * third - lead : 3 * third - lead] + bias[:, third:])
    q_ref[...] = jnp.concatenate(queries, axis=1).astype(LOW)
    width = q_ref.shape[1]
    for ref, k, v in ((kv_ref, keys, values), (other_kv_ref, other_keys, other_values)):
        ref[:, :width] = jnp.concatenate(k, axis=1).astype(LOW)
        ref[:, width:] = jnp.concatenate(v, axis=1).astype(LOW)


def attend_kernel(q_ref, ko, ke, vo, ve, xk_ref, xq_ref, att_ref, lse_ref):
    pair = pl.program_id(0)
    k = jnp.concatenate([ko[...], ke[...]], axis=0)
    v_t = flip(jnp.concatenate([vo[...], ve[...]], axis=0))
    q = q_ref[...]
    rows = q.shape[0]
    ones = jnp.ones((16, k.shape[0]), LOW)
    outs = []
    for h in range(2):
        side = slice(HD * h, HD * h + HD)
        kh = jnp.concatenate([k[:, side], xk_ref[...]], axis=1)
        qh = jnp.concatenate([q[:, side], xq_ref[...]], axis=1)
        vt = jnp.concatenate([v_t[side], ones], axis=0)
        got = []
        for start in range(0, rows, QUERIES):
            span = slice(start, start + QUERIES)
            scores = mm_nt(kh, qh[span])
            top = jnp.max(scores, axis=0, keepdims=True)
            raised = jnp.exp2((scores - top) * SCALE2).astype(LOW)
            o = mm(vt, raised)
            denom = o[HD : HD + 1]
            got.append(o[:HD] * (1.0 / denom))
            lse_ref[pl.ds(2 * pair + h, 1), span] = top * SCALE2 + jnp.log2(denom)
        outs.append(jnp.concatenate(got, axis=1))
    att_ref[...] = jnp.concatenate(outs, axis=0).T.astype(LOW)


def attend_back_kernel(
    first, q_ref, g_ref, att_ref, ko, ke, vo, ve, xk_ref, xq_ref, lse_ref,
    dq_ref, sum_ref, dk_ref, dv_ref, away_ref,
):
    pair = pl.program_id(0) + first
    k = jnp.concatenate([ko[...], ke[...]], axis=0)
    v = jnp.concatenate([vo[...], ve[...]], axis=0)
    k_t = flip(k)
    q, g = q_ref[...], g_ref[...]
    rows = q.shape[0]
    product = (g.astype(FULL) * att_ref[...].astype(FULL)).T
    dqs, dks, dvs = [], [], []
    for h in range(2):
        side = slice(HD * h, HD * h + HD)
        kh = jnp.concatenate([k[:, side], xk_ref[...]], axis=1)
        qh = jnp.concatenate([q[:, side], xq_ref[...]], axis=1)
        inner = jnp.sum(product[side], axis=0, keepdims=True)
        lse = lse_ref[pl.ds(2 * pair + h, 1), :]
        vh, gh, qs = v[:, side], g[:, side], q[:, side]
        dk = dv = None
        got = []
        for start in range(0, rows, QUERIES):
            span = slice(start, start + QUERIES)
            probs = jnp.exp2(mm_nt(kh, qh[span]) * SCALE2 - lse[:, span])
            prob_grad = mm_nt(vh, gh[span])
            score_grad = (probs * (prob_grad - inner[:, span])).astype(LOW)
            more_v = mm(probs.astype(LOW), gh[span])
            more_k = mm(score_grad, qs[span])
            dv = more_v if dv is None else dv + more_v
            dk = more_k if dk is None else dk + more_k
            got.append(mm(k_t[side], score_grad))
        dqs.append(jnp.concatenate(got, axis=1))
        dks.append(dk)
        dvs.append(dv)
    dq = jnp.concatenate(dqs, axis=0).T * 0.125
    dq_ref[...] = dq.astype(LOW)
    sum_ref[...] = jnp.broadcast_to(jnp.sum(dq, axis=0, keepdims=True), sum_ref.shape)
    dk = jnp.concatenate(dks, axis=1) * 0.125
    dv = jnp.concatenate(dvs, axis=1)
    dk_ref[...] = dk[:rows]
    dv_ref[...] = dv[:rows]
    away_ref[:, :LANES] = dk[rows:].astype(LOW)
    away_ref[:, LANES:] = dv[rows:].astype(LOW)


def means(value):
    return jnp.mean(value, axis=-1, keepdims=True)


def normalize(summed):
    center = summed - means(summed)
    inv = lax.rsqrt(means(center * center) + EPS)
    return center * inv, inv


def norm_back(grad, gain, unit, inv):
    scaled = grad * gain
    return inv * (scaled - means(scaled) - unit * means(scaled * unit))


def total(value):
    return jnp.sum(value, axis=0, keepdims=True)


def expand_kernel(blocks, table, x_ref, att_ref, small_ref, *rest):
    n = len(blocks.arrays)
    refs = rest[:n]
    normed_ref, unit_ref, inv_ref, low_ref, act_ref, slope_ref, w, attn, sems = rest[n:]
    copies = blocks.copies(table, refs, w, sems)
    parts = len(copies)
    step = pl.program_id(0)
    hidden = x_ref.shape[1]
    width = hidden // parts

    @pl.when(step == 0)
    def _():
        begin(copies)
        for s in range(parts):
            finish(copies[s])
        value = None
        for s in range(parts):
            more = mm_nt(att_ref[:, width * s : width * s + width], w[s, :, hidden : hidden + width])
            value = more if value is None else value + more
        attn[...] = value

        @pl.loop(0, x_ref.shape[0] // ROWS)
        def _(i):
            span = pl.ds(pl.multiple_of(i * ROWS, ROWS), ROWS)
            summed = x_ref[span].astype(FULL) + attn[span] + small_ref[0:1]
            unit, inv = normalize(summed)
            normed = unit * small_ref[1:2] + small_ref[2:3]
            normed_ref[span] = normed
            unit_ref[span] = unit
            inv_ref[span] = jnp.broadcast_to(inv, (ROWS, LANES))
            low_ref[span] = normed.astype(LOW)

    per = hidden // CHUNK
    s, lanes = step // per, pl.ds(pl.multiple_of(step % per * CHUNK, CHUNK), CHUNK)
    bias = small_ref[pl.ds(8 + s, 1), lanes]
    upper = mm(low_ref[...], w[s, :, lanes]) + bias
    below = 0.5 * (1.0 + lax.erf(upper * ROOT_HALF))
    act_ref[...] = (upper * below).astype(LOW)
    slope_ref[...] = (below + upper * jnp.exp(-0.5 * upper * upper) * DENSITY).astype(LOW)


def shrink_kernel(blocks, table, act_ref, normed_ref, small_ref, cot_ref, live_ref, *rest):
    n = len(blocks.arrays)
    refs = rest[:n]
    out_ref, grad_ref, low_ref, vec_ref, w, acc, sems = rest[n:]
    copies = blocks.copies(table, refs, w, sems)
    step = pl.program_id(0)
    hidden = normed_ref.shape[1]
    per = hidden // CHUNK
    s, lanes = step // per, pl.ds(pl.multiple_of(step % per * CHUNK, CHUNK), CHUNK)

    @pl.when(step == 0)
    def _():
        begin(copies)

    for part, group in copies.items():

        @pl.when(step == part * per)
        def _(group=group):
            finish(group)

    more = mm_nt(act_ref[...], w[s, :, lanes])

    @pl.when(step == 0)
    def _():
        acc[...] = more

    @pl.when(step > 0)
    def _():
        acc[...] += more

    @pl.when(step == pl.num_programs(0) - 1)
    def _():
        vec_ref[...] = jnp.zeros_like(vec_ref)

        @pl.loop(0, normed_ref.shape[0] // ROWS)
        def _(i):
            span = pl.ds(pl.multiple_of(i * ROWS, ROWS), ROWS)
            summed = normed_ref[span] + acc[span] + small_ref[3:4]
            unit, inv = normalize(summed)
            out_ref[span] = (unit * small_ref[4:5] + small_ref[5:6]).astype(LOW)
            arriving = cot_ref[span].astype(FULL) * live_ref[span, 0:1]
            grad = norm_back(arriving, small_ref[4:5], unit, inv)
            grad_ref[span] = grad
            low_ref[span] = grad.astype(LOW)
            vec_ref[0:1] += total(grad)
            vec_ref[1:2] += total(arriving * unit)
            vec_ref[2:3] += total(arriving)


class Exits:
    def __init__(self, flat, outers, rows, order, sides=(0, 1)):
        self.flat, self.outers, self.rows, self.order, self.sides = flat, outers, rows, order, sides

    def height(self):
        return 2 * self.outers * self.rows if self.flat else len(self.sides) * self.outers * self.rows

    def shapes(self, slices, width):
        if self.flat:
            return [shape((slices, self.height(), width), LOW)]
        return [shape((self.outers, slices, self.rows, width), LOW)] * len(self.sides)

    def arrange(self, table, source, target):
        if self.flat:
            target[...] = source[...]
            return
        at = 0
        for side in self.sides:
            for n in self.order:
                start = pl.multiple_of(table[side, n], 16)
                target[at : at + self.rows] = source[pl.ds(start, self.rows), :]
                at += self.rows

    def emit(self, value, refs, s, lanes):
        value = value.astype(LOW)
        if self.flat:
            refs[0][s, :, lanes] = value
            return
        at = 0
        for ref in refs:
            for i in range(self.outers):
                ref[i, s, :, lanes] = value[at : at + self.rows]
                at += self.rows


def shrink_grad_kernel(exits, table, low_ref, act_ref, *rest):
    outs, (natural, turned) = rest[:-2], rest[-2:]

    @pl.when(pl.program_id(0) == 0)
    def _():
        natural[...] = flip(low_ref[...])
        exits.arrange(table, natural, turned)

    exits.emit(mm(turned[...], act_ref[...]), outs, 0, slice(None))


def middle_kernel(
    ups, downs, exits, table, low_ref, normed_low_ref, slope_ref, grad_ref, unit_ref, inv_ref,
    small_ref, att_ref, *rest,
):
    n, m = len(ups.arrays), len(downs.arrays)
    up_refs, down_refs, rest = rest[:n], rest[n : n + m], rest[n + m :]
    first_ref, first_low_ref, att_grad_ref, vec_ref, expand_ref = rest[:5]
    outs = rest[5:-7]
    up_w, down_w, up_sems, down_sems, natural, turned, acc = rest[-7:]
    up_copies = ups.copies(table, up_refs, up_w, up_sems)
    down_copies = downs.copies(table, down_refs, down_w, down_sems)
    parts = len(up_copies)
    step = pl.program_id(0)
    hidden = unit_ref.shape[1]
    width = hidden // parts
    per = hidden // CHUNK
    s, lanes = step // per, pl.ds(pl.multiple_of(step % per * CHUNK, CHUNK), CHUNK)

    @pl.when(step == 0)
    def _():
        for part in range(parts):
            begin({0: down_copies[part], 1: up_copies[part]})
        natural[...] = flip(normed_low_ref[...])
        exits.arrange(table, natural, turned)
        expand_ref[...] = jnp.zeros_like(expand_ref)

    for part in range(parts):

        @pl.when(step == part * per)
        def _(part=part):
            finish(down_copies[part])
            finish(up_copies[part])

    upper_grad = mm(low_ref[...], down_w[s, :, lanes]) * slope_ref[...].astype(FULL)
    expand_ref[pl.ds(s, 1), lanes] = total(upper_grad)
    upper_low = upper_grad.astype(LOW)
    exits.emit(mm(turned[...], upper_low), outs, s, lanes)
    more = mm_nt(upper_low, up_w[s, :, lanes])

    @pl.when(step == 0)
    def _():
        acc[...] = more

    @pl.when(step > 0)
    def _():
        acc[...] += more

    @pl.when(step == pl.num_programs(0) - 1)
    def _():
        vec_ref[...] = jnp.zeros_like(vec_ref)

        @pl.loop(0, unit_ref.shape[0] // ROWS)
        def _(i):
            span = pl.ds(pl.multiple_of(i * ROWS, ROWS), ROWS)
            grad = acc[span] + grad_ref[span]
            unit = unit_ref[span]
            first = norm_back(grad, small_ref[1:2], unit, inv_ref[span, 0:1])
            first_ref[span] = first
            first_low_ref[span] = first.astype(LOW)
            vec_ref[0:1] += total(first)
            vec_ref[1:2] += total(grad * unit)
            vec_ref[2:3] += total(grad)

        natural[...] = flip(first_low_ref[...])
        exits.arrange(table, natural, turned)
        grads = []
        for part in range(parts):
            o = up_w[part, :, hidden : hidden + width]
            grads.append(mm(first_low_ref[...], o))
            value = mm(turned[...], att_ref[:, width * part : width * part + width])
            exits.emit(value, outs, part, slice(hidden, hidden + width))
        att_grad_ref[...] = jnp.concatenate(grads, axis=1).astype(LOW)


def combine(dq_ref, dk_ref, dv_ref, add_ref, number):
    rows, wide = dq_ref.shape
    width = wide // number
    added = [add_ref[:, at : at + LANES] for at in range(0, 2 * wide, LANES)]
    dq = dq_ref[...]
    dk = (dk_ref[...] + jnp.concatenate(added[::2], axis=1).astype(FULL)).astype(LOW)
    dv_full = dv_ref[...] + jnp.concatenate(added[1::2], axis=1).astype(FULL)
    dv = dv_full.astype(LOW)
    blank = jnp.zeros((rows, SMALL), LOW)
    spans = [slice(width * i, width * i + width) for i in range(number)]
    return [jnp.concatenate([dq[:, p], dk[:, p], dv[:, p], blank], axis=1) for p in spans], dv_full


def last_kernel(
    blocks, exits, lots, table, x_ref, first_ref, one_ref, two_ref, expand_ref, pick_ref, *rest
):
    n = len(blocks.arrays)
    gots, rest = rest[: 5 * len(lots)], rest[5 * len(lots) :]
    refs, rest = rest[:n], rest[n:]
    grad_ref, outs = rest[0], rest[1:-7]
    w, vecs, natural, turned, columns, sorted_columns, sems = rest[-7:]
    copies = blocks.copies(table, refs, w, sems)
    begin(copies)
    natural[...] = flip(x_ref[...])
    exits.arrange(table, natural, turned)
    vecs[...] = jnp.zeros_like(vecs)
    grad = first_ref[...]
    for number, lot in enumerate(lots):
        dq_ref, dqs_ref, dk_ref, dv_ref, add_ref = gots[5 * number : 5 * number + 5]
        lows, dv_full = combine(dq_ref, dk_ref, dv_ref, add_ref, len(lot))
        width = dq_ref.shape[1] // len(lot)
        dvs = total(dv_full)
        base = 3 * width // LANES * LANES
        skip = 3 * width - base
        vecs[skip : skip + 3] = one_ref[0:3]
        vecs[skip + 3 : skip + 6] = two_ref[0:3]
        for i, s in enumerate(lot):
            side = slice(width * i, width * i + width)
            value = mm(turned[...], lows[i])
            sums = jnp.concatenate([dqs_ref[:, side], jnp.broadcast_to(dvs[:, side], (8, width))], axis=1)
            high = sums.astype(LOW)
            rest_of = (sums - high.astype(FULL)).astype(LOW)
            heads = mm_nt(high, pick_ref[...]) + mm_nt(rest_of, pick_ref[...])
            vecs[skip + 6 : skip + 7] = expand_ref[s : s + 1]
            vecs[skip + 7 : skip + 8] = heads[0:1]
            columns[...] = vecs[...].T
            exits.arrange(table, columns, sorted_columns)
            value = jnp.concatenate([value[:, :base], value[:, base:] + sorted_columns[...]], axis=1)
            exits.emit(value, outs, s, slice(None))
            finish(copies[s])
            grad = grad + mm_nt(lows[i], w[s])
    grad_ref[...] = grad.astype(LOW)


class Plan:
    def __init__(self, rows):
        self.parts = lax.axis_size("tensor")
        self.owners = lax.axis_size("fsdp")
        self.place = lax.axis_index("tensor")
        self.owner = lax.axis_index("fsdp")
        self.core = self.owner % 2
        self.outer = self.owner // 2
        self.outers = self.owners // 2
        self.rows = rows
        self.flat = rows % 16 != 0
        self.bits = [1 << n for n in range((self.outers - 1).bit_length())]
        rising = list(range(self.outers))
        falling = [0]
        for bit in self.bits[::-1]:
            falling = falling + [n ^ bit for n in falling]
        self.orders = (rising, falling)
        own = jnp.array([rising, rising], jnp.int32) ^ self.outer
        core = jnp.array([0, 1], jnp.int32)[:, None] ^ self.core
        self.table = ((own * 2 + core) * rows).astype(jnp.int32)

    def swap(self, value, bit):
        return lax.ppermute(value, "fsdp", [(n, n ^ bit) for n in range(self.owners)])

    def turn(self, value, by):
        n = self.parts
        return lax.ppermute(value, "tensor", [(i, (i + by) % n) for i in range(n)])

    def trade(self, turn, back):
        pairs = []
        half = self.parts // 2
        for owner in range(self.owners):
            for place in range(self.parts):
                micro = (place + turn) % 2
                there = (owner - owner % 2 + place // half) * self.parts + 2 * micro + owner % 2
                here = owner * self.parts + place
                pairs.append((there, here) if back else (here, there))
        return pairs

    def blocks_of(self, value):
        return [lax.dynamic_index_in_dim(value, (self.place + turn) % 2, 0, False) for turn in range(2)]

    def collect(self, blocks):
        return [lax.ppermute(v, BOTH, self.trade(turn, False)) for turn, v in enumerate(blocks)]

    def release(self, blocks):
        return [lax.ppermute(v, BOTH, self.trade(turn, True)) for turn, v in enumerate(blocks)]

    def settle(self, first, second):
        even = self.place % 2 == 0
        return jnp.stack([jnp.where(even, first, second), jnp.where(even, second, first)])

    def around(self, shard):
        return [shard] + [self.turn(shard, by) for by in range(1, self.parts)]

    def gather(self, held):
        if self.flat:
            held = held[None]
            for bit in self.bits:
                held = jnp.concatenate([held, self.swap(held, 2 * bit)])
            return [self.natural(held, self.swap(held, 1), self.orders[0])]
        return [held] + [self.swap(held, 2 * n) for n in range(1, self.outers)]

    def pieces(self, arrays, names):
        if self.flat:
            return [(v, names, 0, None) for v in arrays]
        mine = [(v, names, 0, (0, n)) for n, v in enumerate(arrays)]
        return mine + [(self.swap(v, 1), names, 0, (1, n)) for n, v in enumerate(arrays)]

    def natural(self, mine, other, order):
        where = jnp.array([order.index(n) for n in range(self.outers)])
        both = []
        for n in range(self.outers):
            at = where[n ^ self.outer]
            pair = [lax.dynamic_index_in_dim(v, at, 0, False) for v in (mine, other)]
            both.append(jnp.where(self.core == 0, pair[0], pair[1]))
            both.append(jnp.where(self.core == 0, pair[1], pair[0]))
        return jnp.concatenate(both, axis=1)

    def exits(self, sides=(0, 1), halving=False):
        return Exits(self.flat, self.outers, self.rows, self.orders[halving], sides)


class Reduction:
    def __init__(self, plan, names, keep, send=None, halving=False):
        self.plan, self.names = plan, names
        self.halving = halving or send is None
        if send is None:
            keep, send = self.sort(keep, plan.orders[1])
        self.terms = [keep, plan.swap(send, 1)]
        self.left, self.bits = plan.outers, list(plan.bits)

    def sort(self, value, order):
        plan, names = self.plan, self.names
        value = value.reshape(len(names), plan.outers, 2, plan.rows, -1)
        size = (len(names), 1, 1, plan.rows, value.shape[-1])
        return [
            jnp.concatenate(
                [lax.dynamic_slice(value, (0, n ^ plan.outer, core, 0, 0), size)[:, 0] for n in order],
                axis=1,
            ).swapaxes(0, 1)
            for core in (plan.core, 1 - plan.core)
        ]

    def step(self):
        bit, self.bits = self.bits[0], self.bits[1:]
        self.left //= 2
        away = sum(t[self.left : 2 * self.left].astype(FULL) for t in self.terms).astype(LOW)
        self.terms = self.terms + [self.plan.swap(away, 2 * bit)]
        return away

    def ready(self):
        if self.halving:
            return [self.step() for _ in self.bits]
        return [sum(t[n].astype(FULL) for t in self.terms).astype(LOW) for n in range(1, self.plan.outers)]

    def launch(self, away, first=1):
        if not self.halving:
            self.terms += [self.plan.swap(v, 2 * (n + first))[None] for n, v in enumerate(away)]

    def turns(self):
        terms = [sum(t[0, i].astype(FULL) for t in self.terms) for i in range(len(self.names))]
        self.terms = [t for t, by in zip(terms, self.names) if not by]
        return [t.astype(LOW) for t, by in zip(terms, self.names) if by]

    def launch_turns(self, sent):
        self.terms += [self.plan.turn(t, -by) for t, by in zip(sent, [by for by in self.names if by])]

    def total(self):
        return sum(t.astype(FULL) for t in self.terms)


def shards(
    tokens, lengths, cotangent, query_proj, key_proj, value_proj, output_proj, expand_proj,
    shrink_proj, query_bias, value_bias, expand_bias, output_bias, attn_gain, attn_shift,
    shrink_bias, ffn_gain, ffn_shift,
):
    rows, width = query_proj.shape
    plan = Plan(rows)
    parts = plan.parts
    hidden = expand_proj.shape[1]
    few = query_bias.shape[0]
    block = tokens.shape[2]
    mine = 2 * block
    model = tokens.shape[3]
    three = 3 * width
    table = plan.table
    half = parts // 2
    low_names, high_names, names = list(range(half)), list(range(half, parts)), list(range(parts))

    smalls = [output_bias, attn_gain, attn_shift, shrink_bias, ffn_gain, ffn_shift, expand_bias]
    heads_biases = jnp.pad(jnp.concatenate([query_bias, value_bias]), (0, rows - 2 * few))
    blank = jnp.zeros((rows,), LOW)
    pack_one = jnp.concatenate(
        [query_proj, key_proj, value_proj, jnp.stack(smalls + [heads_biases] + [blank] * (SMALL - 8)).T],
        axis=1,
    )
    gap = jnp.zeros((rows, -width % LANES), LOW)
    pack_two = jnp.concatenate([expand_proj, output_proj.T, gap, shrink_proj.T], axis=1)
    wide_one, wide_two, wide_three = pack_one.shape[1], hidden + width, hidden
    edge = pack_two.shape[1] - wide_three
    ones = plan.around(pack_one)
    ones, up_own = hold(ones, pack_two[:, :edge])
    ups = plan.around(up_own)
    one_part = plan.gather(jnp.stack(ones))
    ups, blocks = hold(ups, plan.blocks_of(tokens[:, 0]))
    own_tokens = plan.collect(blocks)
    x = jnp.concatenate(own_tokens)
    other_x = plan.swap(x, 1)
    x, down_own = hold(x, pack_two[:, edge:])
    downs = {by: plan.turn(down_own, by) for by in range(1, parts, 2)}
    one_part, up_held = hold(one_part, jnp.stack(ups))
    up_part = plan.gather(up_held)
    qkv_w = Blocks(plan.pieces(one_part, names), wide_one)
    place = jnp.arange(model)[:, None]
    head = jnp.arange(2 * width)[None, :]
    inside = head % width
    pick = (place == inside // few * rows + inside % few + few * (head // width)).astype(LOW)

    micro, parity = plan.place // 2, plan.place % 2
    seen = jnp.where(parity == plan.core, lengths, plan.swap(lengths, 1))[:, 0]
    length = jnp.where(micro == 0, seen[0], seen[1])

    def slots_of(core):
        return jnp.concatenate(
            [block * (2 * core + (micro + n) % 2) + jnp.arange(block) for n in range(2)]
        )

    row_slots = slots_of(plan.core)
    live_rows = jnp.broadcast_to((row_slots < length).astype(FULL)[:, None], (mine, LANES))
    live = jnp.concatenate([row_slots, slots_of(1 - plan.core)]) < length
    lead = jnp.arange(HD)[None, :] == 0
    extra_k = jnp.where(lead & ~live[:, None], DEAD, 0.0).astype(LOW)
    extra_q = jnp.broadcast_to(lead, (mine, HD)).astype(LOW)

    dot_cost = 2 * mine * model * model
    query, key_value, other, small = pl.pallas_call(
        functools.partial(project_kernel, qkv_w),
        out_shape=[
            shape((mine, model), LOW), shape((mine, 2 * model), LOW), shape((mine, 2 * model), LOW),
            shape((16, model), FULL),
        ],
        in_specs=[IN_SMEM, IN_VMEM, IN_VMEM, IN_VMEM] + [ANYWHERE] * len(qkv_w.arrays),
        out_specs=[IN_VMEM] * 4,
        scratch_shapes=[
            pltpu.VMEM((parts, model, wide_one), LOW),
            pltpu.SemaphoreType.DMA((qkv_w.count(),)),
        ],
        compiler_params=params(),
        cost_estimate=cost(3 * dot_cost, 8 * MIB, 0, 0.05),
        name="project",
    )(table, x, other_x, pick, *qkv_w.arrays)
    query, downs, down_own = hold(query, downs, down_own)
    downs.update({by: plan.turn(down_own, by) for by in range(2, parts, 2)})
    pairs = model // LANES
    heads = 2 * pairs
    pad_heads = -(-heads // 8) * 8
    all_rows = 2 * mine

    def lane_block(offset):
        return pl.BlockSpec((mine, LANES), lambda i: (0, i + offset))

    score_cost = 2 * mine * all_rows * HD
    attended, log_total = pl.pallas_call(
        attend_kernel,
        out_shape=[shape((mine, model), LOW), shape((pad_heads, mine), FULL)],
        grid=(pairs,),
        in_specs=[
            lane_block(0), lane_block(0), lane_block(0), lane_block(pairs), lane_block(pairs),
            fixed((all_rows, HD)), fixed((mine, HD)),
        ],
        out_specs=[lane_block(0), fixed((pad_heads, mine))],
        compiler_params=params(1),
        cost_estimate=cost(6 * heads * score_cost, 6 * MIB, heads * mine * all_rows, 0.05),
        name="attend",
    )(query, key_value, other, key_value, other, extra_k, extra_q)

    attended, up_part, downs, down_own = hold(attended, up_part, downs, down_own)
    down_part = plan.gather(jnp.stack([down_own] + [downs[n] for n in range(1, parts)]))
    up_pieces = plan.pieces(up_part, names)
    there, blocks = hold([p[0] for p in up_pieces], plan.blocks_of(cotangent[:, 0]))
    up_w = Blocks([(a, *p[1:]) for a, p in zip(there, up_pieces)], edge)
    own_cot = plan.collect(blocks)
    chunks = parts * hidden // CHUNK
    per = hidden // CHUNK
    chunk_block = pl.BlockSpec((mine, CHUNK), lambda i: (0, i))
    full_rows = fixed((mine, model))
    normed, unit, inv, normed_low, active, slope = pl.pallas_call(
        functools.partial(expand_kernel, up_w),
        out_shape=[
            shape((mine, model), FULL), shape((mine, model), FULL), shape((mine, LANES), FULL),
            shape((mine, model), LOW), shape((mine, parts * hidden), LOW), shape((mine, parts * hidden), LOW),
        ],
        grid=(chunks,),
        in_specs=[IN_SMEM, full_rows, full_rows, fixed((16, model))] + [ANYWHERE] * len(up_w.arrays),
        out_specs=[full_rows, full_rows, fixed((mine, LANES)), full_rows, chunk_block, chunk_block],
        scratch_shapes=[
            pltpu.VMEM((parts, model, edge), LOW),
            pltpu.VMEM((mine, model), FULL),
            pltpu.SemaphoreType.DMA((up_w.count(),)),
        ],
        compiler_params=params(1),
        cost_estimate=cost(8 * dot_cost, 20 * MIB),
        name="expand",
    )(table, x, attended, small, *up_w.arrays)
    active, own_cot, down_part = hold(active, own_cot, down_part)
    cot = jnp.concatenate(own_cot)
    down_w = Blocks(plan.pieces(down_part, names), wide_three)
    gate = pace(table, *down_part[:1])
    layer_rows, second_grad, second_low, vec_two = pl.pallas_call(
        functools.partial(shrink_kernel, down_w),
        out_shape=[
            shape((mine, model), LOW), shape((mine, model), FULL), shape((mine, model), LOW), shape((8, model), FULL),
        ],
        grid=(chunks,),
        in_specs=[
            IN_SMEM, chunk_block, full_rows, fixed((16, model)), full_rows, fixed((mine, LANES)),
        ] + [ANYWHERE] * len(down_w.arrays),
        out_specs=[full_rows, full_rows, full_rows, fixed((8, model))],
        scratch_shapes=[
            pltpu.VMEM((parts, model, wide_three), LOW),
            pltpu.VMEM((mine, model), FULL),
            pltpu.SemaphoreType.DMA((down_w.count(),)),
        ],
        compiler_params=params(1),
        cost_estimate=cost(5 * dot_cost, 16 * MIB),
        name="shrink",
    )(gate, active, normed, small, cot, live_rows, *down_w.arrays)
    def shrink_grad(sides, ready):
        exits = plan.exits(sides)
        if plan.flat:
            grad_block = [pl.BlockSpec((1, model, CHUNK), lambda i: (i // per, 0, i % per))]
        else:
            grad_block = [
                pl.BlockSpec((plan.outers, 1, rows, CHUNK), lambda i: (0, i // per, 0, i % per))
            ] * len(sides)
        return pl.pallas_call(
            functools.partial(shrink_grad_kernel, exits),
            out_shape=exits.shapes(parts, hidden),
            grid=(chunks,),
            in_specs=[IN_SMEM, full_rows, chunk_block],
            out_specs=grad_block,
            scratch_shapes=[pltpu.VMEM((model, mine), LOW), pltpu.VMEM((exits.height(), mine), LOW)],
            compiler_params=params(1),
            cost_estimate=cost(4 * dot_cost // (3 - len(sides)), 9 * MIB),
            name="shrink_grad",
        )(table, ready, active)

    if plan.flat:
        three_red = Reduction(plan, names, *shrink_grad((0, 1), second_low))
    else:
        (send,) = shrink_grad((1,), second_low)
        second_low, send = hold(second_low, send)
        (keep,) = shrink_grad((0,), second_low)
        three_red = Reduction(plan, names, keep, send)
    second_low, away, layer_rows = hold(second_low, three_red.ready(), layer_rows)
    three_red.launch(away)
    layer_got = plan.release([layer_rows[:block], layer_rows[block:]])

    exits = plan.exits()
    grad_shapes = exits.shapes(parts, wide_two)
    first_grad, first_low, attended_grad, vec_one, expand_sums, *blocks = pl.pallas_call(
        functools.partial(middle_kernel, up_w, down_w, exits),
        out_shape=[
            shape((mine, model), FULL), shape((mine, model), LOW), shape((mine, model), LOW),
            shape((8, model), FULL), shape((8, model), FULL),
        ] + grad_shapes,
        grid=(chunks,),
        in_specs=[
            IN_SMEM, full_rows, full_rows, chunk_block, full_rows, full_rows, fixed((mine, LANES)),
            fixed((16, model)), full_rows,
        ] + [ANYWHERE] * (len(up_w.arrays) + len(down_w.arrays)),
        out_specs=[full_rows, full_rows, full_rows, fixed((8, model)), fixed((8, model))]
        + [fixed(g.shape) for g in grad_shapes],
        scratch_shapes=[
            pltpu.VMEM((parts, model, edge), LOW),
            pltpu.VMEM((parts, model, wide_three), LOW),
            pltpu.SemaphoreType.DMA((up_w.count(),)),
            pltpu.SemaphoreType.DMA((down_w.count(),)),
            pltpu.VMEM((model, mine), LOW),
            pltpu.VMEM((model, mine), LOW),
            pltpu.VMEM((mine, model), FULL),
        ],
        compiler_params=params(1),
        cost_estimate=cost(14 * dot_cost, 30 * MIB),
        name="middle",
    )(
        table, second_low, normed_low, slope, second_grad, unit, inv, small, attended,
        *up_w.arrays, *down_w.arrays,
    )
    two_red = Reduction(plan, names, *blocks)
    gate = pace(table, first_low, *three_red.terms[2:], *layer_got)
    gate, attended_grad, two_red.terms, three_red.terms, layer_got = hold(
        gate, attended_grad, two_red.terms, three_red.terms, layer_got
    )
    layer_out = plan.settle(*layer_got)
    attended_grad, away, sent = hold(attended_grad, two_red.ready(), three_red.turns())
    two_red.launch(away[:-1])
    three_red.launch_turns(sent)

    few_pairs = pairs // 2

    def attend_back(lot, grad, weight):
        first = lot[0] * width // LANES
        wide = len(lot) * width

        def from_block(offset):
            return pl.BlockSpec((mine, LANES), lambda i: (0, i + first + offset))

        lot_block = pl.BlockSpec((mine, LANES), lambda i: (0, i))
        return pl.pallas_call(
            functools.partial(attend_back_kernel, first),
            out_shape=[
                shape((mine, wide), LOW), shape((8, wide), FULL), shape((mine, wide), FULL),
                shape((mine, wide), FULL), shape((mine, 2 * wide), LOW),
            ],
            grid=(few_pairs,),
            in_specs=[
                from_block(0), from_block(0), from_block(0), from_block(0), from_block(0),
                from_block(pairs), from_block(pairs), fixed((all_rows, HD)), fixed((mine, HD)),
                fixed((pad_heads, mine)),
            ],
            out_specs=[
                lot_block, pl.BlockSpec((8, LANES), lambda i: (0, i)), lot_block, lot_block,
                pl.BlockSpec((mine, 2 * LANES), lambda i: (0, i)),
            ],
            compiler_params=params(1),
            cost_estimate=cost(10 * heads * score_cost, 8 * MIB, heads * mine * all_rows // 2, weight),
            name="attend_back",
        )(
            query, grad, attended, key_value, other, key_value, other, extra_k, extra_q, log_total,
        )

    def last_step(gate, lots, gots):
        exits = plan.exits()
        grad_shapes = exits.shapes(parts, wide_one)
        return pl.pallas_call(
            functools.partial(last_kernel, qkv_w, exits, lots),
            out_shape=[shape((mine, model), LOW)] + grad_shapes,
            in_specs=[IN_SMEM] + [IN_VMEM] * (6 + 5 * len(lots)) + [ANYWHERE] * len(qkv_w.arrays),
            out_specs=[IN_VMEM] * (1 + len(grad_shapes)),
            scratch_shapes=[
                pltpu.VMEM((parts, model, wide_one), LOW),
                pltpu.VMEM((LANES, model), FULL),
                pltpu.VMEM((model, mine), LOW),
                pltpu.VMEM((model, mine), LOW),
                pltpu.VMEM((model, LANES), FULL),
                pltpu.VMEM((model, LANES), FULL),
                pltpu.SemaphoreType.DMA((qkv_w.count(),)),
            ],
            compiler_params=params(),
            cost_estimate=cost(6 * dot_cost, 20 * MIB),
            name="input_grad",
        )(
            gate, x, first_grad, vec_one, vec_two, expand_sums, pick, *[v for g in gots for v in g],
            *qkv_w.arrays,
        )

    def cross(got):
        return *got[:-1], plan.swap(got[-1], 1)

    high = attend_back(high_names, attended_grad, 20)
    high, attended_grad, far, three_red.terms = hold(high, attended_grad, away[-1:], three_red.terms)
    two_red.launch(far, plan.outers - 1)
    high = cross(high)
    low = cross(attend_back(low_names, attended_grad, 20))
    gate = pace(gate, low[0], *two_red.terms[2:])
    gate, first_grad, sent = hold(gate, first_grad, two_red.turns())
    two_red.launch_turns(sent)
    input_grad, *blocks = last_step(gate, (high_names, low_names), (high, low))
    input_grad, blocks, two_red.terms = hold(input_grad, blocks, two_red.terms)
    one_red = Reduction(plan, names, *blocks)
    input_grad, away = hold(input_grad, one_red.ready())
    one_red.launch(away)
    input_got = plan.release([input_grad[:block], input_grad[block:]])
    sent, input_got, two_red.terms, three_red.terms = hold(
        one_red.turns(), input_got, two_red.terms, three_red.terms
    )
    one_red.launch_turns(sent)
    input_rows = plan.settle(*input_got).astype(FULL)
    sums_one = one_red.total()
    sums_two, sums_three = two_red.total(), three_red.total()
    quarter = rows // parts
    own = lax.dynamic_slice_in_dim(sums_one[:, three : three + 6], plan.place * quarter, quarter, 0)
    return (
        layer_out[:, None],
        input_rows[:, None],
        sums_one[:, :width],
        sums_one[:, width : 2 * width],
        sums_one[:, 2 * width : three],
        sums_two[:, hidden:].T,
        sums_two[:, :hidden],
        sums_three.T,
        sums_one[:few, three + 7],
        sums_one[few : 2 * few, three + 7],
        sums_one[:, three + 6],
        own[:, 0],
        own[:, 1],
        own[:, 2],
        own[:, 3],
        own[:, 4],
        own[:, 5],
    )


def solution(mesh):
    rows = P(None, "fsdp", "tensor", None)
    split = P("fsdp", "tensor")
    turned = P("tensor", "fsdp")
    heads = P(("tensor", "fsdp"))
    model = P("fsdp")
    spread = P(("fsdp", "tensor"))
    return jax.shard_map(
        shards,
        mesh=mesh,
        in_specs=(rows, P(None, "fsdp"), rows, split, split, split, turned, split, turned)
        + (heads,) * 3
        + (model,) * 6,
        out_specs=(rows, rows, split, split, split, turned, split, turned)
        + (heads,) * 3
        + (spread,) * 6,
        check_vma=False,
    )
```

```python
import functools
import math

import jax
import jax.numpy as jnp
from jax import lax
from jax.experimental import pallas as pl
from jax.experimental.pallas import tpu as pltpu
from jax.sharding import PartitionSpec as P

HD = 64
EPS = 1e-05
DEAD = -8000000000.0
ROOT_HALF = 0.7071067811865476
DENSITY = 0.3989422804014327
LOG2E = 1.4426950408889634
SCALE2 = 0.125 * LOG2E
BOTH = ("fsdp", "tensor")
LOW = jnp.bfloat16
FULL = jnp.float32
LANES = 128
CHUNK = 768
QUERIES = 512
ROWS = 128
MIB = 1 << 20
NT = (((1,), (1,)), ((), ()))
SMALL = 64

IN_VMEM = pl.BlockSpec(memory_space=pltpu.VMEM)
IN_SMEM = pl.BlockSpec(memory_space=pltpu.SMEM)
ANYWHERE = pl.BlockSpec(memory_space=pl.ANY)


def shape(dims, dtype):
    return jax.ShapeDtypeStruct(dims, dtype)


def fixed(dims):
    return pl.BlockSpec(dims, lambda i: (0,) * len(dims))


def params(grid=0, vmem=56):
    return pltpu.CompilerParams(
        vmem_limit_bytes=vmem * MIB, dimension_semantics=("arbitrary",) * grid if grid else None
    )


def cost(flops, touched, exps=0, weight=20):
    return pl.CostEstimate(
        flops=int(weight * flops), bytes_accessed=int(weight * touched), transcendentals=int(weight * exps)
    )


def mm(left, right):
    return jnp.dot(left, right, preferred_element_type=FULL)


def mm_nt(left, right):
    return lax.dot_general(left, right, NT, preferred_element_type=FULL)


def flip(value):
    return value.astype(FULL).T.astype(value.dtype)


def pace_kernel(in_ref, *rest):
    out_ref = rest[-1]
    for row in range(in_ref.shape[0]):
        for n in range(in_ref.shape[1]):
            out_ref[row, n] = in_ref[row, n]


def pace(table, *ready):
    return pl.pallas_call(
        pace_kernel,
        out_shape=shape(table.shape, table.dtype),
        in_specs=[IN_SMEM] + [ANYWHERE] * len(ready),
        out_specs=IN_SMEM,
        cost_estimate=pl.CostEstimate(flops=10**11, bytes_accessed=10**9, transcendentals=0),
        name="pace",
    )(table, *ready)


def hold(*values):
    return lax.optimization_barrier(values)


class Blocks:
    def __init__(self, pieces, width):
        self.pieces, self.width = pieces, width
        self.arrays = [p[0] for p in pieces]

    def count(self):
        return sum(len(p[1]) for p in self.pieces)

    def copies(self, table, refs, scratch, sems, wanted=None):
        found = {}
        at = 0
        for ref, (_, slices, lane, where) in zip(refs, self.pieces):
            rows = ref.shape[1]
            start = 0 if where is None else pl.multiple_of(table[where[0], where[1]], 16)
            for place, s in enumerate(slices):
                if wanted is not None and s not in wanted:
                    continue
                found.setdefault(s, []).append(
                    pltpu.make_async_copy(
                        ref.at[place, :, pl.ds(lane, self.width)],
                        scratch.at[s, pl.ds(start, rows), :],
                        sems.at[at],
                    )
                )
                at += 1
        return found


def begin(copies):
    for group in copies.values():
        for copy in group:
            copy.start()


def finish(group):
    for copy in group:
        copy.wait()


def project_kernel(blocks, table, x_ref, other_ref, pick_ref, *rest):
    n = len(blocks.arrays)
    refs, (q_ref, kv_ref, other_kv_ref, small_ref, w, sems) = rest[:n], rest[n:]
    copies = blocks.copies(table, refs, w, sems)
    begin(copies)
    parts = len(copies)
    third = q_ref.shape[1] // parts
    base = 3 * third // LANES * LANES
    skip = 3 * third - base
    small_ref[...] = jnp.zeros_like(small_ref)
    lead = third // LANES * LANES
    queries, keys, values, other_keys, other_values = [], [], [], [], []
    for s in range(parts):
        finish(copies[s])
        turned = w[s, :, base:].astype(FULL).T
        few = turned[skip : skip + 8]
        if s == 0:
            small_ref[0:8] = few
        small_ref[8 + s : 9 + s] = few[6:7]
        bias = mm(few.astype(LOW), pick_ref[...])[7:8]
        y = mm(x_ref[...], w[s])
        queries.append(y[:, :third] + bias[:, :third])
        keys.append(y[:, third : 2 * third])
        values.append(y[:, 2 * third : 3 * third] + bias[:, third:])
        y = mm(other_ref[...], w[s, :, lead:])
        other_keys.append(y[:, third - lead : 2 * third - lead])
        other_values.append(y[:, 2 * third - lead : 3 * third - lead] + bias[:, third:])
    q_ref[...] = jnp.concatenate(queries, axis=1).astype(LOW)
    width = q_ref.shape[1]
    for ref, k, v in ((kv_ref, keys, values), (other_kv_ref, other_keys, other_values)):
        ref[:, :width] = jnp.concatenate(k, axis=1).astype(LOW)
        ref[:, width:] = jnp.concatenate(v, axis=1).astype(LOW)


def attend_kernel(q_ref, ko, ke, vo, ve, xk_ref, xq_ref, att_ref, lse_ref):
    pair = pl.program_id(0)
    k = jnp.concatenate([ko[...], ke[...]], axis=0)
    v_t = flip(jnp.concatenate([vo[...], ve[...]], axis=0))
    q = q_ref[...]
    rows = q.shape[0]
    ones = jnp.ones((16, k.shape[0]), LOW)
    outs = []
    for h in range(2):
        side = slice(HD * h, HD * h + HD)
        kh = jnp.concatenate([k[:, side], xk_ref[...]], axis=1)
        qh = jnp.concatenate([q[:, side], xq_ref[...]], axis=1)
        vt = jnp.concatenate([v_t[side], ones], axis=0)
        got = []
        for start in range(0, rows, QUERIES):
            span = slice(start, start + QUERIES)
            scores = mm_nt(kh, qh[span])
            top = jnp.max(scores, axis=0, keepdims=True)
            raised = jnp.exp2((scores - top) * SCALE2).astype(LOW)
            o = mm(vt, raised)
            denom = o[HD : HD + 1]
            got.append(o[:HD] * (1.0 / denom))
            lse_ref[pl.ds(2 * pair + h, 1), span] = top * SCALE2 + jnp.log2(denom)
        outs.append(jnp.concatenate(got, axis=1))
    att_ref[...] = jnp.concatenate(outs, axis=0).T.astype(LOW)


def attend_back_kernel(
    first, q_ref, g_ref, att_ref, ko, ke, vo, ve, xk_ref, xq_ref, lse_ref,
    dq_ref, sum_ref, dk_ref, dv_ref, away_ref,
):
    pair = pl.program_id(0) + first
    k = jnp.concatenate([ko[...], ke[...]], axis=0)
    v = jnp.concatenate([vo[...], ve[...]], axis=0)
    k_t = flip(k)
    q, g = q_ref[...], g_ref[...]
    rows = q.shape[0]
    product = (g.astype(FULL) * att_ref[...].astype(FULL)).T
    dqs, dks, dvs = [], [], []
    for h in range(2):
        side = slice(HD * h, HD * h + HD)
        kh = jnp.concatenate([k[:, side], xk_ref[...]], axis=1)
        qh = jnp.concatenate([q[:, side], xq_ref[...]], axis=1)
        inner = jnp.sum(product[side], axis=0, keepdims=True)
        lse = lse_ref[pl.ds(2 * pair + h, 1), :]
        vh, gh, qs = v[:, side], g[:, side], q[:, side]
        dk = dv = None
        got = []
        for start in range(0, rows, QUERIES):
            span = slice(start, start + QUERIES)
            probs = jnp.exp2(mm_nt(kh, qh[span]) * SCALE2 - lse[:, span])
            prob_grad = mm_nt(vh, gh[span])
            score_grad = (probs * (prob_grad - inner[:, span])).astype(LOW)
            more_v = mm(probs.astype(LOW), gh[span])
            more_k = mm(score_grad, qs[span])
            dv = more_v if dv is None else dv + more_v
            dk = more_k if dk is None else dk + more_k
            got.append(mm(k_t[side], score_grad))
        dqs.append(jnp.concatenate(got, axis=1))
        dks.append(dk)
        dvs.append(dv)
    dq = jnp.concatenate(dqs, axis=0).T * 0.125
    dq_ref[...] = dq.astype(LOW)
    sum_ref[...] = jnp.broadcast_to(jnp.sum(dq, axis=0, keepdims=True), sum_ref.shape)
    dk = jnp.concatenate(dks, axis=1) * 0.125
    dv = jnp.concatenate(dvs, axis=1)
    dk_ref[...] = dk[:rows]
    dv_ref[...] = dv[:rows]
    away_ref[:, :LANES] = dk[rows:].astype(LOW)
    away_ref[:, LANES:] = dv[rows:].astype(LOW)


def means(value):
    return jnp.mean(value, axis=-1, keepdims=True)


def normalize(summed):
    center = summed - means(summed)
    inv = lax.rsqrt(means(center * center) + EPS)
    return center * inv, inv


def norm_back(grad, gain, unit, inv):
    scaled = grad * gain
    return inv * (scaled - means(scaled) - unit * means(scaled * unit))


def total(value):
    return jnp.sum(value, axis=0, keepdims=True)


def expand_kernel(blocks, table, x_ref, att_ref, small_ref, *rest):
    n = len(blocks.arrays)
    refs = rest[:n]
    normed_ref, unit_ref, inv_ref, low_ref, act_ref, slope_ref, w, attn, sems = rest[n:]
    copies = blocks.copies(table, refs, w, sems)
    parts = len(copies)
    step = pl.program_id(0)
    hidden = x_ref.shape[1]
    width = hidden // parts

    @pl.when(step == 0)
    def _():
        begin(copies)
        for s in range(parts):
            finish(copies[s])
        value = None
        for s in range(parts):
            more = mm_nt(att_ref[:, width * s : width * s + width], w[s, :, hidden : hidden + width])
            value = more if value is None else value + more
        attn[...] = value

        @pl.loop(0, x_ref.shape[0] // ROWS)
        def _(i):
            span = pl.ds(pl.multiple_of(i * ROWS, ROWS), ROWS)
            summed = x_ref[span].astype(FULL) + attn[span] + small_ref[0:1]
            unit, inv = normalize(summed)
            normed = unit * small_ref[1:2] + small_ref[2:3]
            normed_ref[span] = normed
            unit_ref[span] = unit
            inv_ref[span] = jnp.broadcast_to(inv, (ROWS, LANES))
            low_ref[span] = normed.astype(LOW)

    per = hidden // CHUNK
    s, lanes = step // per, pl.ds(pl.multiple_of(step % per * CHUNK, CHUNK), CHUNK)
    bias = small_ref[pl.ds(8 + s, 1), lanes]
    upper = mm(low_ref[...], w[s, :, lanes]) + bias
    below = 0.5 * (1.0 + lax.erf(upper * ROOT_HALF))
    act_ref[...] = (upper * below).astype(LOW)
    slope_ref[...] = (below + upper * jnp.exp(-0.5 * upper * upper) * DENSITY).astype(LOW)


def shrink_kernel(blocks, table, act_ref, normed_ref, small_ref, cot_ref, live_ref, *rest):
    n = len(blocks.arrays)
    refs = rest[:n]
    out_ref, grad_ref, low_ref, vec_ref, w, acc, sems = rest[n:]
    copies = blocks.copies(table, refs, w, sems)
    step = pl.program_id(0)
    hidden = normed_ref.shape[1]
    per = hidden // CHUNK
    s, lanes = step // per, pl.ds(pl.multiple_of(step % per * CHUNK, CHUNK), CHUNK)

    @pl.when(step == 0)
    def _():
        begin(copies)

    for part, group in copies.items():

        @pl.when(step == part * per)
        def _(group=group):
            finish(group)

    more = mm_nt(act_ref[...], w[s, :, lanes])

    @pl.when(step == 0)
    def _():
        acc[...] = more

    @pl.when(step > 0)
    def _():
        acc[...] += more

    @pl.when(step == pl.num_programs(0) - 1)
    def _():
        vec_ref[...] = jnp.zeros_like(vec_ref)

        @pl.loop(0, normed_ref.shape[0] // ROWS)
        def _(i):
            span = pl.ds(pl.multiple_of(i * ROWS, ROWS), ROWS)
            summed = normed_ref[span] + acc[span] + small_ref[3:4]
            unit, inv = normalize(summed)
            out_ref[span] = (unit * small_ref[4:5] + small_ref[5:6]).astype(LOW)
            arriving = cot_ref[span].astype(FULL) * live_ref[span, 0:1]
            grad = norm_back(arriving, small_ref[4:5], unit, inv)
            grad_ref[span] = grad
            low_ref[span] = grad.astype(LOW)
            vec_ref[0:1] += total(grad)
            vec_ref[1:2] += total(arriving * unit)
            vec_ref[2:3] += total(arriving)


class Exits:
    def __init__(self, flat, outers, rows, order, sides=(0, 1)):
        self.flat, self.outers, self.rows, self.order, self.sides = flat, outers, rows, order, sides

    def height(self):
        return 2 * self.outers * self.rows if self.flat else len(self.sides) * self.outers * self.rows

    def shapes(self, slices, width):
        if self.flat:
            return [shape((slices, self.height(), width), LOW)]
        return [shape((self.outers, slices, self.rows, width), LOW)] * len(self.sides)

    def arrange(self, table, source, target):
        if self.flat:
            target[...] = source[...]
            return
        at = 0
        for side in self.sides:
            for n in self.order:
                start = pl.multiple_of(table[side, n], 16)
                target[at : at + self.rows] = source[pl.ds(start, self.rows), :]
                at += self.rows

    def emit(self, value, refs, s, lanes):
        value = value.astype(LOW)
        if self.flat:
            refs[0][s, :, lanes] = value
            return
        at = 0
        for ref in refs:
            for i in range(self.outers):
                ref[i, s, :, lanes] = value[at : at + self.rows]
                at += self.rows


def shrink_grad_kernel(exits, table, low_ref, act_ref, *rest):
    outs, (natural, turned) = rest[:-2], rest[-2:]

    @pl.when(pl.program_id(0) == 0)
    def _():
        natural[...] = flip(low_ref[...])
        exits.arrange(table, natural, turned)

    exits.emit(mm(turned[...], act_ref[...]), outs, 0, slice(None))


def middle_kernel(
    ups, downs, exits, table, low_ref, normed_low_ref, slope_ref, grad_ref, unit_ref, inv_ref,
    small_ref, att_ref, *rest,
):
    n, m = len(ups.arrays), len(downs.arrays)
    up_refs, down_refs, rest = rest[:n], rest[n : n + m], rest[n + m :]
    first_ref, first_low_ref, att_grad_ref, vec_ref, expand_ref = rest[:5]
    outs = rest[5:-7]
    up_w, down_w, up_sems, down_sems, natural, turned, acc = rest[-7:]
    up_copies = ups.copies(table, up_refs, up_w, up_sems)
    down_copies = downs.copies(table, down_refs, down_w, down_sems)
    parts = len(up_copies)
    step = pl.program_id(0)
    hidden = unit_ref.shape[1]
    width = hidden // parts
    per = hidden // CHUNK
    s, lanes = step // per, pl.ds(pl.multiple_of(step % per * CHUNK, CHUNK), CHUNK)

    @pl.when(step == 0)
    def _():
        for part in range(parts):
            begin({0: down_copies[part], 1: up_copies[part]})
        natural[...] = flip(normed_low_ref[...])
        exits.arrange(table, natural, turned)
        expand_ref[...] = jnp.zeros_like(expand_ref)

    for part in range(parts):

        @pl.when(step == part * per)
        def _(part=part):
            finish(down_copies[part])
            finish(up_copies[part])

    upper_grad = mm(low_ref[...], down_w[s, :, lanes]) * slope_ref[...].astype(FULL)
    expand_ref[pl.ds(s, 1), lanes] = total(upper_grad)
    upper_low = upper_grad.astype(LOW)
    exits.emit(mm(turned[...], upper_low), outs, s, lanes)
    more = mm_nt(upper_low, up_w[s, :, lanes])

    @pl.when(step == 0)
    def _():
        acc[...] = more

    @pl.when(step > 0)
    def _():
        acc[...] += more

    @pl.when(step == pl.num_programs(0) - 1)
    def _():
        vec_ref[...] = jnp.zeros_like(vec_ref)

        @pl.loop(0, unit_ref.shape[0] // ROWS)
        def _(i):
            span = pl.ds(pl.multiple_of(i * ROWS, ROWS), ROWS)
            grad = acc[span] + grad_ref[span]
            unit = unit_ref[span]
            first = norm_back(grad, small_ref[1:2], unit, inv_ref[span, 0:1])
            first_ref[span] = first
            first_low_ref[span] = first.astype(LOW)
            vec_ref[0:1] += total(first)
            vec_ref[1:2] += total(grad * unit)
            vec_ref[2:3] += total(grad)

        natural[...] = flip(first_low_ref[...])
        exits.arrange(table, natural, turned)
        grads = []
        for part in range(parts):
            o = up_w[part, :, hidden : hidden + width]
            grads.append(mm(first_low_ref[...], o))
            value = mm(turned[...], att_ref[:, width * part : width * part + width])
            exits.emit(value, outs, part, slice(hidden, hidden + width))
        att_grad_ref[...] = jnp.concatenate(grads, axis=1).astype(LOW)


def combine(dq_ref, dk_ref, dv_ref, add_ref, number):
    rows, wide = dq_ref.shape
    width = wide // number
    added = [add_ref[:, at : at + LANES] for at in range(0, 2 * wide, LANES)]
    dq = dq_ref[...]
    dk = (dk_ref[...] + jnp.concatenate(added[::2], axis=1).astype(FULL)).astype(LOW)
    dv_full = dv_ref[...] + jnp.concatenate(added[1::2], axis=1).astype(FULL)
    dv = dv_full.astype(LOW)
    blank = jnp.zeros((rows, SMALL), LOW)
    spans = [slice(width * i, width * i + width) for i in range(number)]
    return [jnp.concatenate([dq[:, p], dk[:, p], dv[:, p], blank], axis=1) for p in spans], dv_full


def weight_kernel(
    exits, slices, table, x_ref, dq_ref, dqs_ref, dk_ref, dv_ref, add_ref, one_ref, two_ref,
    expand_ref, pick_ref, *rest,
):
    outs = rest[:-5]
    vecs, natural, turned, columns, sorted_columns = rest[-5:]
    natural[...] = flip(x_ref[...])
    exits.arrange(table, natural, turned)
    lows, dv_full = combine(dq_ref, dk_ref, dv_ref, add_ref, len(slices))
    width = dq_ref.shape[1] // len(slices)
    dvs = total(dv_full)
    base = 3 * width // LANES * LANES
    skip = 3 * width - base
    vecs[...] = jnp.zeros_like(vecs)
    vecs[skip : skip + 3] = one_ref[0:3]
    vecs[skip + 3 : skip + 6] = two_ref[0:3]
    for i, s in enumerate(slices):
        side = slice(width * i, width * i + width)
        value = mm(turned[...], lows[i])
        sums = jnp.concatenate([dqs_ref[:, side], jnp.broadcast_to(dvs[:, side], (8, width))], axis=1)
        high = sums.astype(LOW)
        rest_of = (sums - high.astype(FULL)).astype(LOW)
        heads = mm_nt(high, pick_ref[...]) + mm_nt(rest_of, pick_ref[...])
        vecs[skip + 6 : skip + 7] = expand_ref[s : s + 1]
        vecs[skip + 7 : skip + 8] = heads[0:1]
        columns[...] = vecs[...].T
        exits.arrange(table, columns, sorted_columns)
        value = jnp.concatenate([value[:, :base], value[:, base:] + sorted_columns[...]], axis=1)
        exits.emit(value, outs, i, slice(None))


def last_kernel(
    blocks, exits, lots, table, x_ref, first_ref, one_ref, two_ref, expand_ref, pick_ref, *rest
):
    n = len(blocks.arrays)
    gots, rest = rest[: 5 * len(lots)], rest[5 * len(lots) :]
    refs, rest = rest[:n], rest[n:]
    grad_ref, outs = rest[0], rest[1:-7]
    w, vecs, natural, turned, columns, sorted_columns, sems = rest[-7:]
    copies = blocks.copies(table, refs, w, sems)
    begin(copies)
    natural[...] = flip(x_ref[...])
    exits.arrange(table, natural, turned)
    vecs[...] = jnp.zeros_like(vecs)
    grad = first_ref[...]
    for number, lot in enumerate(lots):
        dq_ref, dqs_ref, dk_ref, dv_ref, add_ref = gots[5 * number : 5 * number + 5]
        lows, dv_full = combine(dq_ref, dk_ref, dv_ref, add_ref, len(lot))
        if number < len(lots) - 1:
            for low, s in zip(lows, lot):
                finish(copies[s])
                grad = grad + mm_nt(low, w[s])
            continue
        width = dq_ref.shape[1] // len(lot)
        dvs = total(dv_full)
        base = 3 * width // LANES * LANES
        skip = 3 * width - base
        vecs[skip : skip + 3] = one_ref[0:3]
        vecs[skip + 3 : skip + 6] = two_ref[0:3]
        for i, s in enumerate(lot):
            side = slice(width * i, width * i + width)
            value = mm(turned[...], lows[i])
            sums = jnp.concatenate([dqs_ref[:, side], jnp.broadcast_to(dvs[:, side], (8, width))], axis=1)
            high = sums.astype(LOW)
            rest_of = (sums - high.astype(FULL)).astype(LOW)
            heads = mm_nt(high, pick_ref[...]) + mm_nt(rest_of, pick_ref[...])
            vecs[skip + 6 : skip + 7] = expand_ref[s : s + 1]
            vecs[skip + 7 : skip + 8] = heads[0:1]
            columns[...] = vecs[...].T
            exits.arrange(table, columns, sorted_columns)
            value = jnp.concatenate([value[:, :base], value[:, base:] + sorted_columns[...]], axis=1)
            exits.emit(value, outs, i, slice(None))
            finish(copies[s])
            grad = grad + mm_nt(lows[i], w[s])
    grad_ref[...] = grad.astype(LOW)


class Plan:
    def __init__(self, rows):
        self.parts = lax.axis_size("tensor")
        self.owners = lax.axis_size("fsdp")
        self.place = lax.axis_index("tensor")
        self.owner = lax.axis_index("fsdp")
        self.core = self.owner % 2
        self.outer = self.owner // 2
        self.outers = self.owners // 2
        self.rows = rows
        self.flat = rows % 16 != 0
        self.bits = [1 << n for n in range((self.outers - 1).bit_length())]
        rising = list(range(self.outers))
        falling = [0]
        for bit in self.bits[::-1]:
            falling = falling + [n ^ bit for n in falling]
        self.orders = (rising, falling)
        own = jnp.array([rising, rising], jnp.int32) ^ self.outer
        core = jnp.array([0, 1], jnp.int32)[:, None] ^ self.core
        self.table = ((own * 2 + core) * rows).astype(jnp.int32)

    def swap(self, value, bit):
        return lax.ppermute(value, "fsdp", [(n, n ^ bit) for n in range(self.owners)])

    def turn(self, value, by):
        n = self.parts
        return lax.ppermute(value, "tensor", [(i, (i + by) % n) for i in range(n)])

    def trade(self, turn, back):
        pairs = []
        half = self.parts // 2
        for owner in range(self.owners):
            for place in range(self.parts):
                micro = (place + turn) % 2
                there = (owner - owner % 2 + place // half) * self.parts + 2 * micro + owner % 2
                here = owner * self.parts + place
                pairs.append((there, here) if back else (here, there))
        return pairs

    def blocks_of(self, value):
        return [lax.dynamic_index_in_dim(value, (self.place + turn) % 2, 0, False) for turn in range(2)]

    def collect(self, blocks):
        return [lax.ppermute(v, BOTH, self.trade(turn, False)) for turn, v in enumerate(blocks)]

    def release(self, blocks):
        return [lax.ppermute(v, BOTH, self.trade(turn, True)) for turn, v in enumerate(blocks)]

    def settle(self, first, second):
        even = self.place % 2 == 0
        return jnp.stack([jnp.where(even, first, second), jnp.where(even, second, first)])

    def around(self, shard):
        return [shard] + [self.turn(shard, by) for by in range(1, self.parts)]

    def gather(self, held):
        if self.flat:
            held = held[None]
            for bit in self.bits:
                held = jnp.concatenate([held, self.swap(held, 2 * bit)])
            return [self.natural(held, self.swap(held, 1), self.orders[0])]
        return [held] + [self.swap(held, 2 * n) for n in range(1, self.outers)]

    def pieces(self, arrays, names):
        if self.flat:
            return [(v, names, 0, None) for v in arrays]
        mine = [(v, names, 0, (0, n)) for n, v in enumerate(arrays)]
        return mine + [(self.swap(v, 1), names, 0, (1, n)) for n, v in enumerate(arrays)]

    def natural(self, mine, other, order):
        where = jnp.array([order.index(n) for n in range(self.outers)])
        both = []
        for n in range(self.outers):
            at = where[n ^ self.outer]
            pair = [lax.dynamic_index_in_dim(v, at, 0, False) for v in (mine, other)]
            both.append(jnp.where(self.core == 0, pair[0], pair[1]))
            both.append(jnp.where(self.core == 0, pair[1], pair[0]))
        return jnp.concatenate(both, axis=1)

    def exits(self, sides=(0, 1), halving=False):
        return Exits(self.flat, self.outers, self.rows, self.orders[halving], sides)


class Reduction:
    def __init__(self, plan, names, keep, send=None, halving=False):
        self.plan, self.names = plan, names
        self.halving = halving or send is None
        if send is None:
            keep, send = self.sort(keep, plan.orders[1])
        self.terms = [keep, plan.swap(send, 1)]
        self.left, self.bits = plan.outers, list(plan.bits)

    def sort(self, value, order):
        plan, names = self.plan, self.names
        value = value.reshape(len(names), plan.outers, 2, plan.rows, -1)
        size = (len(names), 1, 1, plan.rows, value.shape[-1])
        return [
            jnp.concatenate(
                [lax.dynamic_slice(value, (0, n ^ plan.outer, core, 0, 0), size)[:, 0] for n in order],
                axis=1,
            ).swapaxes(0, 1)
            for core in (plan.core, 1 - plan.core)
        ]

    def step(self):
        bit, self.bits = self.bits[0], self.bits[1:]
        self.left //= 2
        away = sum(t[self.left : 2 * self.left].astype(FULL) for t in self.terms).astype(LOW)
        self.terms = self.terms + [self.plan.swap(away, 2 * bit)]
        return away

    def ready(self):
        if self.halving:
            return [self.step() for _ in self.bits]
        return [sum(t[n].astype(FULL) for t in self.terms).astype(LOW) for n in range(1, self.plan.outers)]

    def launch(self, away, first=1):
        if not self.halving:
            self.terms += [self.plan.swap(v, 2 * (n + first))[None] for n, v in enumerate(away)]

    def turns(self):
        terms = [sum(t[0, i].astype(FULL) for t in self.terms) for i in range(len(self.names))]
        self.terms = [t for t, by in zip(terms, self.names) if not by]
        return [t.astype(LOW) for t, by in zip(terms, self.names) if by]

    def launch_turns(self, sent, which=None):
        turns = [by for by in self.names if by]
        self.terms += [
            self.plan.turn(t, -by) for t, by in zip(sent, turns) if which is None or by in which
        ]

    def total(self):
        return sum(t.astype(FULL) for t in self.terms)


def shards(
    tokens, lengths, cotangent, query_proj, key_proj, value_proj, output_proj, expand_proj,
    shrink_proj, query_bias, value_bias, expand_bias, output_bias, attn_gain, attn_shift,
    shrink_bias, ffn_gain, ffn_shift,
):
    rows, width = query_proj.shape
    plan = Plan(rows)
    parts = plan.parts
    hidden = expand_proj.shape[1]
    few = query_bias.shape[0]
    block = tokens.shape[2]
    mine = 2 * block
    model = tokens.shape[3]
    three = 3 * width
    table = plan.table
    half = parts // 2
    low_names, high_names, names = list(range(half)), list(range(half, parts)), list(range(parts))

    smalls = [output_bias, attn_gain, attn_shift, shrink_bias, ffn_gain, ffn_shift, expand_bias]
    heads_biases = jnp.pad(jnp.concatenate([query_bias, value_bias]), (0, rows - 2 * few))
    blank = jnp.zeros((rows,), LOW)
    pack_one = jnp.concatenate(
        [query_proj, key_proj, value_proj, jnp.stack(smalls + [heads_biases] + [blank] * (SMALL - 8)).T],
        axis=1,
    )
    gap = jnp.zeros((rows, -width % LANES), LOW)
    pack_two = jnp.concatenate([expand_proj, output_proj.T, gap, shrink_proj.T], axis=1)
    wide_one, wide_two, wide_three = pack_one.shape[1], hidden + width, hidden
    edge = pack_two.shape[1] - wide_three
    ones = plan.around(pack_one)
    ones, up_own = hold(ones, pack_two[:, :edge])
    ups = plan.around(up_own)
    one_part = plan.gather(jnp.stack(ones))
    ups, blocks = hold(ups, plan.blocks_of(tokens[:, 0]))
    own_tokens = plan.collect(blocks)
    x = jnp.concatenate(own_tokens)
    other_x = plan.swap(x, 1)
    x, down_own = hold(x, pack_two[:, edge:])
    downs = {by: plan.turn(down_own, by) for by in range(1, parts, 2)}
    one_part, up_held = hold(one_part, jnp.stack(ups))
    up_part = plan.gather(up_held)
    qkv_w = Blocks(plan.pieces(one_part, names), wide_one)
    place = jnp.arange(model)[:, None]
    head = jnp.arange(2 * width)[None, :]
    inside = head % width
    pick = (place == inside // few * rows + inside % few + few * (head // width)).astype(LOW)

    micro, parity = plan.place // 2, plan.place % 2
    seen = jnp.where(parity == plan.core, lengths, plan.swap(lengths, 1))[:, 0]
    length = jnp.where(micro == 0, seen[0], seen[1])

    def slots_of(core):
        return jnp.concatenate(
            [block * (2 * core + (micro + n) % 2) + jnp.arange(block) for n in range(2)]
        )

    row_slots = slots_of(plan.core)
    live_rows = jnp.broadcast_to((row_slots < length).astype(FULL)[:, None], (mine, LANES))
    live = jnp.concatenate([row_slots, slots_of(1 - plan.core)]) < length
    lead = jnp.arange(HD)[None, :] == 0
    extra_k = jnp.where(lead & ~live[:, None], DEAD, 0.0).astype(LOW)
    extra_q = jnp.broadcast_to(lead, (mine, HD)).astype(LOW)

    dot_cost = 2 * mine * model * model
    query, key_value, other, small = pl.pallas_call(
        functools.partial(project_kernel, qkv_w),
        out_shape=[
            shape((mine, model), LOW), shape((mine, 2 * model), LOW), shape((mine, 2 * model), LOW),
            shape((16, model), FULL),
        ],
        in_specs=[IN_SMEM, IN_VMEM, IN_VMEM, IN_VMEM] + [ANYWHERE] * len(qkv_w.arrays),
        out_specs=[IN_VMEM] * 4,
        scratch_shapes=[
            pltpu.VMEM((parts, model, wide_one), LOW),
            pltpu.SemaphoreType.DMA((qkv_w.count(),)),
        ],
        compiler_params=params(),
        cost_estimate=cost(3 * dot_cost, 8 * MIB, 0, 0.05),
        name="project",
    )(table, x, other_x, pick, *qkv_w.arrays)
    query, downs, down_own = hold(query, downs, down_own)
    downs.update({by: plan.turn(down_own, by) for by in range(2, parts, 2)})
    pairs = model // LANES
    heads = 2 * pairs
    pad_heads = -(-heads // 8) * 8
    all_rows = 2 * mine

    def lane_block(offset):
        return pl.BlockSpec((mine, LANES), lambda i: (0, i + offset))

    score_cost = 2 * mine * all_rows * HD
    attended, log_total = pl.pallas_call(
        attend_kernel,
        out_shape=[shape((mine, model), LOW), shape((pad_heads, mine), FULL)],
        grid=(pairs,),
        in_specs=[
            lane_block(0), lane_block(0), lane_block(0), lane_block(pairs), lane_block(pairs),
            fixed((all_rows, HD)), fixed((mine, HD)),
        ],
        out_specs=[lane_block(0), fixed((pad_heads, mine))],
        compiler_params=params(1),
        cost_estimate=cost(6 * heads * score_cost, 6 * MIB, heads * mine * all_rows, 0.05),
        name="attend",
    )(query, key_value, other, key_value, other, extra_k, extra_q)

    attended, up_part, downs, down_own = hold(attended, up_part, downs, down_own)
    down_part = plan.gather(jnp.stack([down_own] + [downs[n] for n in range(1, parts)]))
    up_pieces = plan.pieces(up_part, names)
    there, blocks = hold([p[0] for p in up_pieces], plan.blocks_of(cotangent[:, 0]))
    up_w = Blocks([(a, *p[1:]) for a, p in zip(there, up_pieces)], edge)
    own_cot = plan.collect(blocks)
    chunks = parts * hidden // CHUNK
    per = hidden // CHUNK
    chunk_block = pl.BlockSpec((mine, CHUNK), lambda i: (0, i))
    full_rows = fixed((mine, model))
    normed, unit, inv, normed_low, active, slope = pl.pallas_call(
        functools.partial(expand_kernel, up_w),
        out_shape=[
            shape((mine, model), FULL), shape((mine, model), FULL), shape((mine, LANES), FULL),
            shape((mine, model), LOW), shape((mine, parts * hidden), LOW), shape((mine, parts * hidden), LOW),
        ],
        grid=(chunks,),
        in_specs=[IN_SMEM, full_rows, full_rows, fixed((16, model))] + [ANYWHERE] * len(up_w.arrays),
        out_specs=[full_rows, full_rows, fixed((mine, LANES)), full_rows, chunk_block, chunk_block],
        scratch_shapes=[
            pltpu.VMEM((parts, model, edge), LOW),
            pltpu.VMEM((mine, model), FULL),
            pltpu.SemaphoreType.DMA((up_w.count(),)),
        ],
        compiler_params=params(1),
        cost_estimate=cost(8 * dot_cost, 20 * MIB),
        name="expand",
    )(table, x, attended, small, *up_w.arrays)
    active, own_cot, down_part = hold(active, own_cot, down_part)
    cot = jnp.concatenate(own_cot)
    down_w = Blocks(plan.pieces(down_part, names), wide_three)
    gate = pace(table, *down_part[:1])
    layer_rows, second_grad, second_low, vec_two = pl.pallas_call(
        functools.partial(shrink_kernel, down_w),
        out_shape=[
            shape((mine, model), LOW), shape((mine, model), FULL), shape((mine, model), LOW), shape((8, model), FULL),
        ],
        grid=(chunks,),
        in_specs=[
            IN_SMEM, chunk_block, full_rows, fixed((16, model)), full_rows, fixed((mine, LANES)),
        ] + [ANYWHERE] * len(down_w.arrays),
        out_specs=[full_rows, full_rows, full_rows, fixed((8, model))],
        scratch_shapes=[
            pltpu.VMEM((parts, model, wide_three), LOW),
            pltpu.VMEM((mine, model), FULL),
            pltpu.SemaphoreType.DMA((down_w.count(),)),
        ],
        compiler_params=params(1),
        cost_estimate=cost(5 * dot_cost, 16 * MIB),
        name="shrink",
    )(gate, active, normed, small, cot, live_rows, *down_w.arrays)
    def shrink_grad(sides, ready):
        exits = plan.exits(sides)
        if plan.flat:
            grad_block = [pl.BlockSpec((1, model, CHUNK), lambda i: (i // per, 0, i % per))]
        else:
            grad_block = [
                pl.BlockSpec((plan.outers, 1, rows, CHUNK), lambda i: (0, i // per, 0, i % per))
            ] * len(sides)
        return pl.pallas_call(
            functools.partial(shrink_grad_kernel, exits),
            out_shape=exits.shapes(parts, hidden),
            grid=(chunks,),
            in_specs=[IN_SMEM, full_rows, chunk_block],
            out_specs=grad_block,
            scratch_shapes=[pltpu.VMEM((model, mine), LOW), pltpu.VMEM((exits.height(), mine), LOW)],
            compiler_params=params(1),
            cost_estimate=cost(4 * dot_cost // (3 - len(sides)), 9 * MIB),
            name="shrink_grad",
        )(table, ready, active)

    if plan.flat:
        three_red = Reduction(plan, names, *shrink_grad((0, 1), second_low))
    else:
        (send,) = shrink_grad((1,), second_low)
        second_low, send = hold(second_low, send)
        (keep,) = shrink_grad((0,), second_low)
        three_red = Reduction(plan, names, keep, send)
    second_low, away, layer_rows = hold(second_low, three_red.ready(), layer_rows)
    three_red.launch(away)
    layer_got = plan.release([layer_rows[:block], layer_rows[block:]])

    exits = plan.exits()
    grad_shapes = exits.shapes(parts, wide_two)
    first_grad, first_low, attended_grad, vec_one, expand_sums, *blocks = pl.pallas_call(
        functools.partial(middle_kernel, up_w, down_w, exits),
        out_shape=[
            shape((mine, model), FULL), shape((mine, model), LOW), shape((mine, model), LOW),
            shape((8, model), FULL), shape((8, model), FULL),
        ] + grad_shapes,
        grid=(chunks,),
        in_specs=[
            IN_SMEM, full_rows, full_rows, chunk_block, full_rows, full_rows, fixed((mine, LANES)),
            fixed((16, model)), full_rows,
        ] + [ANYWHERE] * (len(up_w.arrays) + len(down_w.arrays)),
        out_specs=[full_rows, full_rows, full_rows, fixed((8, model)), fixed((8, model))]
        + [fixed(g.shape) for g in grad_shapes],
        scratch_shapes=[
            pltpu.VMEM((parts, model, edge), LOW),
            pltpu.VMEM((parts, model, wide_three), LOW),
            pltpu.SemaphoreType.DMA((up_w.count(),)),
            pltpu.SemaphoreType.DMA((down_w.count(),)),
            pltpu.VMEM((model, mine), LOW),
            pltpu.VMEM((model, mine), LOW),
            pltpu.VMEM((mine, model), FULL),
        ],
        compiler_params=params(1),
        cost_estimate=cost(14 * dot_cost, 30 * MIB),
        name="middle",
    )(
        table, second_low, normed_low, slope, second_grad, unit, inv, small, attended,
        *up_w.arrays, *down_w.arrays,
    )
    two_red = Reduction(plan, names, *blocks)
    gate = pace(table, first_low, *three_red.terms[2:], *layer_got)
    gate, attended_grad, two_red.terms, three_red.terms, layer_got = hold(
        gate, attended_grad, two_red.terms, three_red.terms, layer_got
    )
    attended_grad, away, sent = hold(attended_grad, two_red.ready(), three_red.turns())
    two_red.launch(away[:-1])
    three_red.launch_turns(sent)

    few_pairs = pairs // 2

    def attend_back(lot, grad, weight):
        first = lot[0] * width // LANES
        wide = len(lot) * width

        def from_block(offset):
            return pl.BlockSpec((mine, LANES), lambda i: (0, i + first + offset))

        lot_block = pl.BlockSpec((mine, LANES), lambda i: (0, i))
        return pl.pallas_call(
            functools.partial(attend_back_kernel, first),
            out_shape=[
                shape((mine, wide), LOW), shape((8, wide), FULL), shape((mine, wide), FULL),
                shape((mine, wide), FULL), shape((mine, 2 * wide), LOW),
            ],
            grid=(few_pairs,),
            in_specs=[
                from_block(0), from_block(0), from_block(0), from_block(0), from_block(0),
                from_block(pairs), from_block(pairs), fixed((all_rows, HD)), fixed((mine, HD)),
                fixed((pad_heads, mine)),
            ],
            out_specs=[
                lot_block, pl.BlockSpec((8, LANES), lambda i: (0, i)), lot_block, lot_block,
                pl.BlockSpec((mine, 2 * LANES), lambda i: (0, i)),
            ],
            compiler_params=params(1),
            cost_estimate=cost(10 * heads * score_cost, 8 * MIB, heads * mine * all_rows // 2, weight),
            name="attend_back",
        )(
            query, grad, attended, key_value, other, key_value, other, extra_k, extra_q, log_total,
        )

    def weight_step(lot, got):
        exits = plan.exits()
        grad_shapes = exits.shapes(len(lot), wide_one)
        return pl.pallas_call(
            functools.partial(weight_kernel, exits, lot),
            out_shape=grad_shapes,
            in_specs=[IN_SMEM] + [IN_VMEM] * 10,
            out_specs=[IN_VMEM] * len(grad_shapes),
            scratch_shapes=[
                pltpu.VMEM((LANES, model), FULL),
                pltpu.VMEM((model, mine), LOW),
                pltpu.VMEM((model, mine), LOW),
                pltpu.VMEM((model, LANES), FULL),
                pltpu.VMEM((model, LANES), FULL),
            ],
            compiler_params=params(),
            cost_estimate=cost(2 * dot_cost, 9 * MIB, 0, 0.05),
            name="weight_grad",
        )(table, x, *got, vec_one, vec_two, expand_sums, pick)

    def last_step(gate, lots, gots):
        exits = plan.exits()
        grad_shapes = exits.shapes(len(lots[-1]), wide_one)
        return pl.pallas_call(
            functools.partial(last_kernel, qkv_w, exits, lots),
            out_shape=[shape((mine, model), LOW)] + grad_shapes,
            in_specs=[IN_SMEM] + [IN_VMEM] * (6 + 5 * len(lots)) + [ANYWHERE] * len(qkv_w.arrays),
            out_specs=[IN_VMEM] * (1 + len(grad_shapes)),
            scratch_shapes=[
                pltpu.VMEM((parts, model, wide_one), LOW),
                pltpu.VMEM((LANES, model), FULL),
                pltpu.VMEM((model, mine), LOW),
                pltpu.VMEM((model, mine), LOW),
                pltpu.VMEM((model, LANES), FULL),
                pltpu.VMEM((model, LANES), FULL),
                pltpu.SemaphoreType.DMA((qkv_w.count(),)),
            ],
            compiler_params=params(),
            cost_estimate=cost(6 * dot_cost, 20 * MIB),
            name="input_grad",
        )(
            gate, x, first_grad, vec_one, vec_two, expand_sums, pick, *[v for g in gots for v in g],
            *qkv_w.arrays,
        )

    def cross(got):
        return *got[:-1], plan.swap(got[-1], 1)

    high = attend_back(high_names, attended_grad, 20)
    high, attended_grad, far, three_red.terms = hold(high, attended_grad, away[-1:], three_red.terms)
    two_red.launch(far, plan.outers - 1)
    high = cross(high)
    low = cross(attend_back(low_names, attended_grad, 20))
    blocks = weight_step(high_names, high)
    high_red = Reduction(plan, high_names, *blocks)
    gate = pace(gate, blocks[0], low[0], *two_red.terms[2:])
    gate, two_red.terms, high_red.terms = hold(gate, two_red.terms, high_red.terms)
    gate, away, sent = hold(gate, high_red.ready(), two_red.turns())
    high_red.launch(away[:-1])
    two_red.launch_turns(sent)
    input_grad, *blocks = last_step(gate, (high_names, low_names), (high, low))
    input_grad, blocks, two_red.terms, high_red.terms, far = hold(
        input_grad, blocks, two_red.terms, high_red.terms, away[-1:]
    )
    low_red = Reduction(plan, low_names, *blocks)
    high_red.launch(far, plan.outers - 1)
    input_got = plan.release([input_grad[:block], input_grad[block:]])
    gate = pace(gate, blocks[0])
    gate, low_red.terms = hold(gate, low_red.terms)
    low_red.launch(low_red.ready())
    high_red.launch_turns(high_red.turns())
    sent, input_got, two_red.terms, three_red.terms, layer_got = hold(
        low_red.turns(), input_got, two_red.terms, three_red.terms, layer_got
    )
    layer_out = plan.settle(*layer_got)
    low_red.launch_turns(sent)
    input_rows = plan.settle(*input_got).astype(FULL)
    sums_one = high_red.total() + low_red.total()
    sums_two, sums_three = two_red.total(), three_red.total()
    sums_one += jnp.minimum(gate[0, 0], 0).astype(FULL)
    quarter = rows // parts
    own = lax.dynamic_slice_in_dim(sums_one[:, three : three + 6], plan.place * quarter, quarter, 0)
    return (
        layer_out[:, None],
        input_rows[:, None],
        sums_one[:, :width],
        sums_one[:, width : 2 * width],
        sums_one[:, 2 * width : three],
        sums_two[:, hidden:].T,
        sums_two[:, :hidden],
        sums_three.T,
        sums_one[:few, three + 7],
        sums_one[few : 2 * few, three + 7],
        sums_one[:, three + 6],
        own[:, 0],
        own[:, 1],
        own[:, 2],
        own[:, 3],
        own[:, 4],
        own[:, 5],
    )


def solution(mesh):
    rows = P(None, "fsdp", "tensor", None)
    split = P("fsdp", "tensor")
    turned = P("tensor", "fsdp")
    heads = P(("tensor", "fsdp"))
    model = P("fsdp")
    spread = P(("fsdp", "tensor"))
    return jax.shard_map(
        shards,
        mesh=mesh,
        in_specs=(rows, P(None, "fsdp"), rows, split, split, split, turned, split, turned)
        + (heads,) * 3
        + (model,) * 6,
        out_specs=(rows, rows, split, split, split, turned, split, turned)
        + (heads,) * 3
        + (spread,) * 6,
        check_vma=False,
    )
```

```python
import functools
import math

import jax
import jax.numpy as jnp
from jax import lax
from jax.experimental import pallas as pl
from jax.experimental.pallas import tpu as pltpu
from jax.sharding import PartitionSpec as P

HD = 64
EPS = 1e-05
DEAD = -8000000000.0
ROOT_HALF = 0.7071067811865476
DENSITY = 0.3989422804014327
LOG2E = 1.4426950408889634
SCALE2 = 0.125 * LOG2E
BOTH = ("fsdp", "tensor")
LOW = jnp.bfloat16
FULL = jnp.float32
LANES = 128
CHUNK = 768
QUERIES = 512
ROWS = 128
MIB = 1 << 20
NT = (((1,), (1,)), ((), ()))
SMALL = 64

IN_VMEM = pl.BlockSpec(memory_space=pltpu.VMEM)
IN_SMEM = pl.BlockSpec(memory_space=pltpu.SMEM)
ANYWHERE = pl.BlockSpec(memory_space=pl.ANY)


def shape(dims, dtype):
    return jax.ShapeDtypeStruct(dims, dtype)


def fixed(dims):
    return pl.BlockSpec(dims, lambda i: (0,) * len(dims))


def params(grid=0, vmem=56):
    return pltpu.CompilerParams(
        vmem_limit_bytes=vmem * MIB, dimension_semantics=("arbitrary",) * grid if grid else None
    )


def cost(flops, touched, exps=0, weight=20):
    return pl.CostEstimate(
        flops=int(weight * flops), bytes_accessed=int(weight * touched), transcendentals=int(weight * exps)
    )


def mm(left, right):
    return jnp.dot(left, right, preferred_element_type=FULL)


def mm_nt(left, right):
    return lax.dot_general(left, right, NT, preferred_element_type=FULL)


def flip(value):
    return value.astype(FULL).T.astype(value.dtype)


def pace_kernel(in_ref, *rest):
    out_ref = rest[-1]
    for row in range(in_ref.shape[0]):
        for n in range(in_ref.shape[1]):
            out_ref[row, n] = in_ref[row, n]


def pace(table, *ready):
    return pl.pallas_call(
        pace_kernel,
        out_shape=shape(table.shape, table.dtype),
        in_specs=[IN_SMEM] + [ANYWHERE] * len(ready),
        out_specs=IN_SMEM,
        cost_estimate=pl.CostEstimate(flops=10**11, bytes_accessed=10**9, transcendentals=0),
        name="pace",
    )(table, *ready)


def hold(*values):
    return lax.optimization_barrier(values)


class Blocks:
    def __init__(self, pieces, width):
        self.pieces, self.width = pieces, width
        self.arrays = [p[0] for p in pieces]

    def count(self):
        return sum(len(p[1]) for p in self.pieces)

    def copies(self, table, refs, scratch, sems, wanted=None):
        found = {}
        at = 0
        for ref, (_, slices, lane, where) in zip(refs, self.pieces):
            rows = ref.shape[1]
            start = 0 if where is None else pl.multiple_of(table[where[0], where[1]], 16)
            for place, s in enumerate(slices):
                if wanted is not None and s not in wanted:
                    continue
                found.setdefault(s, []).append(
                    pltpu.make_async_copy(
                        ref.at[place, :, pl.ds(lane, self.width)],
                        scratch.at[s, pl.ds(start, rows), :],
                        sems.at[at],
                    )
                )
                at += 1
        return found


def begin(copies):
    for group in copies.values():
        for copy in group:
            copy.start()


def finish(group):
    for copy in group:
        copy.wait()


def project_kernel(blocks, table, x_ref, other_ref, pick_ref, *rest):
    n = len(blocks.arrays)
    refs, (q_ref, kv_ref, other_kv_ref, small_ref, w, sems) = rest[:n], rest[n:]
    copies = blocks.copies(table, refs, w, sems)
    begin(copies)
    parts = len(copies)
    third = q_ref.shape[1] // parts
    base = 3 * third // LANES * LANES
    skip = 3 * third - base
    small_ref[...] = jnp.zeros_like(small_ref)
    lead = third // LANES * LANES
    queries, keys, values, other_keys, other_values = [], [], [], [], []
    for s in range(parts):
        finish(copies[s])
        turned = w[s, :, base:].astype(FULL).T
        few = turned[skip : skip + 8]
        if s == 0:
            small_ref[0:8] = few
        small_ref[8 + s : 9 + s] = few[6:7]
        bias = mm(few.astype(LOW), pick_ref[...])[7:8]
        y = mm(x_ref[...], w[s])
        queries.append(y[:, :third] + bias[:, :third])
        keys.append(y[:, third : 2 * third])
        values.append(y[:, 2 * third : 3 * third] + bias[:, third:])
        y = mm(other_ref[...], w[s, :, lead:])
        other_keys.append(y[:, third - lead : 2 * third - lead])
        other_values.append(y[:, 2 * third - lead : 3 * third - lead] + bias[:, third:])
    q_ref[...] = jnp.concatenate(queries, axis=1).astype(LOW)
    width = q_ref.shape[1]
    for ref, k, v in ((kv_ref, keys, values), (other_kv_ref, other_keys, other_values)):
        ref[:, :width] = jnp.concatenate(k, axis=1).astype(LOW)
        ref[:, width:] = jnp.concatenate(v, axis=1).astype(LOW)


def attend_kernel(q_ref, ko, ke, vo, ve, xk_ref, xq_ref, att_ref, lse_ref):
    pair = pl.program_id(0)
    k = jnp.concatenate([ko[...], ke[...]], axis=0)
    v_t = flip(jnp.concatenate([vo[...], ve[...]], axis=0))
    q = q_ref[...]
    rows = q.shape[0]
    ones = jnp.ones((16, k.shape[0]), LOW)
    outs = []
    for h in range(2):
        side = slice(HD * h, HD * h + HD)
        kh = jnp.concatenate([k[:, side], xk_ref[...]], axis=1)
        qh = jnp.concatenate([q[:, side], xq_ref[...]], axis=1)
        vt = jnp.concatenate([v_t[side], ones], axis=0)
        got = []
        for start in range(0, rows, QUERIES):
            span = slice(start, start + QUERIES)
            scores = mm_nt(kh, qh[span])
            top = jnp.max(scores, axis=0, keepdims=True)
            raised = jnp.exp2((scores - top) * SCALE2).astype(LOW)
            o = mm(vt, raised)
            denom = o[HD : HD + 1]
            got.append(o[:HD] * (1.0 / denom))
            lse_ref[pl.ds(2 * pair + h, 1), span] = top * SCALE2 + jnp.log2(denom)
        outs.append(jnp.concatenate(got, axis=1))
    att_ref[...] = jnp.concatenate(outs, axis=0).T.astype(LOW)


def attend_back_kernel(
    first, q_ref, g_ref, att_ref, ko, ke, vo, ve, xk_ref, xq_ref, lse_ref,
    dq_ref, sum_ref, dk_ref, dv_ref, away_ref,
):
    pair = pl.program_id(0) + first
    k = jnp.concatenate([ko[...], ke[...]], axis=0)
    v = jnp.concatenate([vo[...], ve[...]], axis=0)
    k_t = flip(k)
    q, g = q_ref[...], g_ref[...]
    rows = q.shape[0]
    product = (g.astype(FULL) * att_ref[...].astype(FULL)).T
    dqs, dks, dvs = [], [], []
    for h in range(2):
        side = slice(HD * h, HD * h + HD)
        kh = jnp.concatenate([k[:, side], xk_ref[...]], axis=1)
        qh = jnp.concatenate([q[:, side], xq_ref[...]], axis=1)
        inner = jnp.sum(product[side], axis=0, keepdims=True)
        lse = lse_ref[pl.ds(2 * pair + h, 1), :]
        vh, gh, qs = v[:, side], g[:, side], q[:, side]
        dk = dv = None
        got = []
        for start in range(0, rows, QUERIES):
            span = slice(start, start + QUERIES)
            probs = jnp.exp2(mm_nt(kh, qh[span]) * SCALE2 - lse[:, span])
            prob_grad = mm_nt(vh, gh[span])
            score_grad = (probs * (prob_grad - inner[:, span])).astype(LOW)
            more_v = mm(probs.astype(LOW), gh[span])
            more_k = mm(score_grad, qs[span])
            dv = more_v if dv is None else dv + more_v
            dk = more_k if dk is None else dk + more_k
            got.append(mm(k_t[side], score_grad))
        dqs.append(jnp.concatenate(got, axis=1))
        dks.append(dk)
        dvs.append(dv)
    dq = jnp.concatenate(dqs, axis=0).T * 0.125
    dq_ref[...] = dq.astype(LOW)
    sum_ref[...] = jnp.broadcast_to(jnp.sum(dq, axis=0, keepdims=True), sum_ref.shape)
    dk = jnp.concatenate(dks, axis=1) * 0.125
    dv = jnp.concatenate(dvs, axis=1)
    dk_ref[...] = dk[:rows]
    dv_ref[...] = dv[:rows]
    away_ref[:, :LANES] = dk[rows:].astype(LOW)
    away_ref[:, LANES:] = dv[rows:].astype(LOW)


def means(value):
    return jnp.mean(value, axis=-1, keepdims=True)


def normalize(summed):
    center = summed - means(summed)
    inv = lax.rsqrt(means(center * center) + EPS)
    return center * inv, inv


def norm_back(grad, gain, unit, inv):
    scaled = grad * gain
    return inv * (scaled - means(scaled) - unit * means(scaled * unit))


def total(value):
    return jnp.sum(value, axis=0, keepdims=True)


def expand_kernel(blocks, table, x_ref, att_ref, small_ref, *rest):
    n = len(blocks.arrays)
    refs = rest[:n]
    normed_ref, unit_ref, inv_ref, low_ref, act_ref, slope_ref, w, attn, sems = rest[n:]
    copies = blocks.copies(table, refs, w, sems)
    parts = len(copies)
    step = pl.program_id(0)
    hidden = x_ref.shape[1]
    width = hidden // parts

    @pl.when(step == 0)
    def _():
        begin(copies)
        for s in range(parts):
            finish(copies[s])
        value = None
        for s in range(parts):
            more = mm_nt(att_ref[:, width * s : width * s + width], w[s, :, hidden : hidden + width])
            value = more if value is None else value + more
        attn[...] = value

        @pl.loop(0, x_ref.shape[0] // ROWS)
        def _(i):
            span = pl.ds(pl.multiple_of(i * ROWS, ROWS), ROWS)
            summed = x_ref[span].astype(FULL) + attn[span] + small_ref[0:1]
            unit, inv = normalize(summed)
            normed = unit * small_ref[1:2] + small_ref[2:3]
            normed_ref[span] = normed
            unit_ref[span] = unit
            inv_ref[span] = jnp.broadcast_to(inv, (ROWS, LANES))
            low_ref[span] = normed.astype(LOW)

    per = hidden // CHUNK
    s, lanes = step // per, pl.ds(pl.multiple_of(step % per * CHUNK, CHUNK), CHUNK)
    bias = small_ref[pl.ds(8 + s, 1), lanes]
    upper = mm(low_ref[...], w[s, :, lanes]) + bias
    below = 0.5 * (1.0 + lax.erf(upper * ROOT_HALF))
    act_ref[...] = (upper * below).astype(LOW)
    slope_ref[...] = (below + upper * jnp.exp(-0.5 * upper * upper) * DENSITY).astype(LOW)


def shrink_kernel(blocks, table, act_ref, normed_ref, small_ref, cot_ref, live_ref, *rest):
    n = len(blocks.arrays)
    refs = rest[:n]
    out_ref, grad_ref, low_ref, vec_ref, w, acc, sems = rest[n:]
    copies = blocks.copies(table, refs, w, sems)
    step = pl.program_id(0)
    hidden = normed_ref.shape[1]
    per = hidden // CHUNK
    s, lanes = step // per, pl.ds(pl.multiple_of(step % per * CHUNK, CHUNK), CHUNK)

    @pl.when(step == 0)
    def _():
        begin(copies)

    for part, group in copies.items():

        @pl.when(step == part * per)
        def _(group=group):
            finish(group)

    more = mm_nt(act_ref[...], w[s, :, lanes])

    @pl.when(step == 0)
    def _():
        acc[...] = more

    @pl.when(step > 0)
    def _():
        acc[...] += more

    @pl.when(step == pl.num_programs(0) - 1)
    def _():
        vec_ref[...] = jnp.zeros_like(vec_ref)

        @pl.loop(0, normed_ref.shape[0] // ROWS)
        def _(i):
            span = pl.ds(pl.multiple_of(i * ROWS, ROWS), ROWS)
            summed = normed_ref[span] + acc[span] + small_ref[3:4]
            unit, inv = normalize(summed)
            out_ref[span] = (unit * small_ref[4:5] + small_ref[5:6]).astype(LOW)
            arriving = cot_ref[span].astype(FULL) * live_ref[span, 0:1]
            grad = norm_back(arriving, small_ref[4:5], unit, inv)
            grad_ref[span] = grad
            low_ref[span] = grad.astype(LOW)
            vec_ref[0:1] += total(grad)
            vec_ref[1:2] += total(arriving * unit)
            vec_ref[2:3] += total(arriving)


class Exits:
    def __init__(self, flat, outers, rows, order, sides=(0, 1)):
        self.flat, self.outers, self.rows, self.order, self.sides = flat, outers, rows, order, sides

    def height(self):
        return 2 * self.outers * self.rows if self.flat else len(self.sides) * self.outers * self.rows

    def shapes(self, slices, width):
        if self.flat:
            return [shape((slices, self.height(), width), LOW)]
        return [shape((self.outers, slices, self.rows, width), LOW)] * len(self.sides)

    def arrange(self, table, source, target):
        if self.flat:
            target[...] = source[...]
            return
        at = 0
        for side in self.sides:
            for n in self.order:
                start = pl.multiple_of(table[side, n], 16)
                target[at : at + self.rows] = source[pl.ds(start, self.rows), :]
                at += self.rows

    def emit(self, value, refs, s, lanes):
        value = value.astype(LOW)
        if self.flat:
            refs[0][s, :, lanes] = value
            return
        at = 0
        for ref in refs:
            for i in range(self.outers):
                ref[i, s, :, lanes] = value[at : at + self.rows]
                at += self.rows


def shrink_grad_kernel(exits, table, low_ref, act_ref, *rest):
    outs, (natural, turned) = rest[:-2], rest[-2:]

    @pl.when(pl.program_id(0) == 0)
    def _():
        natural[...] = flip(low_ref[...])
        exits.arrange(table, natural, turned)

    exits.emit(mm(turned[...], act_ref[...]), outs, 0, slice(None))


def middle_kernel(
    ups, downs, exits, table, low_ref, normed_low_ref, slope_ref, grad_ref, unit_ref, inv_ref,
    small_ref, att_ref, *rest,
):
    n, m = len(ups.arrays), len(downs.arrays)
    up_refs, down_refs, rest = rest[:n], rest[n : n + m], rest[n + m :]
    first_ref, first_low_ref, att_grad_ref, vec_ref, expand_ref = rest[:5]
    outs = rest[5:-7]
    up_w, down_w, up_sems, down_sems, natural, turned, acc = rest[-7:]
    up_copies = ups.copies(table, up_refs, up_w, up_sems)
    down_copies = downs.copies(table, down_refs, down_w, down_sems)
    parts = len(up_copies)
    step = pl.program_id(0)
    hidden = unit_ref.shape[1]
    width = hidden // parts
    per = hidden // CHUNK
    s, lanes = step // per, pl.ds(pl.multiple_of(step % per * CHUNK, CHUNK), CHUNK)

    @pl.when(step == 0)
    def _():
        for part in range(parts):
            begin({0: down_copies[part], 1: up_copies[part]})
        natural[...] = flip(normed_low_ref[...])
        exits.arrange(table, natural, turned)
        expand_ref[...] = jnp.zeros_like(expand_ref)

    for part in range(parts):

        @pl.when(step == part * per)
        def _(part=part):
            finish(down_copies[part])
            finish(up_copies[part])

    upper_grad = mm(low_ref[...], down_w[s, :, lanes]) * slope_ref[...].astype(FULL)
    expand_ref[pl.ds(s, 1), lanes] = total(upper_grad)
    upper_low = upper_grad.astype(LOW)
    exits.emit(mm(turned[...], upper_low), outs, s, lanes)
    more = mm_nt(upper_low, up_w[s, :, lanes])

    @pl.when(step == 0)
    def _():
        acc[...] = more

    @pl.when(step > 0)
    def _():
        acc[...] += more

    @pl.when(step == pl.num_programs(0) - 1)
    def _():
        vec_ref[...] = jnp.zeros_like(vec_ref)

        @pl.loop(0, unit_ref.shape[0] // ROWS)
        def _(i):
            span = pl.ds(pl.multiple_of(i * ROWS, ROWS), ROWS)
            grad = acc[span] + grad_ref[span]
            unit = unit_ref[span]
            first = norm_back(grad, small_ref[1:2], unit, inv_ref[span, 0:1])
            first_ref[span] = first
            first_low_ref[span] = first.astype(LOW)
            vec_ref[0:1] += total(first)
            vec_ref[1:2] += total(grad * unit)
            vec_ref[2:3] += total(grad)

        natural[...] = flip(first_low_ref[...])
        exits.arrange(table, natural, turned)
        grads = []
        for part in range(parts):
            o = up_w[part, :, hidden : hidden + width]
            grads.append(mm(first_low_ref[...], o))
            value = mm(turned[...], att_ref[:, width * part : width * part + width])
            exits.emit(value, outs, part, slice(hidden, hidden + width))
        att_grad_ref[...] = jnp.concatenate(grads, axis=1).astype(LOW)


def combine(dq_ref, dk_ref, dv_ref, add_ref, number):
    rows, wide = dq_ref.shape
    width = wide // number
    added = [add_ref[:, at : at + LANES] for at in range(0, 2 * wide, LANES)]
    dq = dq_ref[...]
    dk = (dk_ref[...] + jnp.concatenate(added[::2], axis=1).astype(FULL)).astype(LOW)
    dv_full = dv_ref[...] + jnp.concatenate(added[1::2], axis=1).astype(FULL)
    dv = dv_full.astype(LOW)
    blank = jnp.zeros((rows, SMALL), LOW)
    spans = [slice(width * i, width * i + width) for i in range(number)]
    return [jnp.concatenate([dq[:, p], dk[:, p], dv[:, p], blank], axis=1) for p in spans], dv_full


def weight_kernel(
    exits, slices, table, x_ref, dq_ref, dqs_ref, dk_ref, dv_ref, add_ref, one_ref, two_ref,
    expand_ref, pick_ref, *rest,
):
    outs = rest[:-5]
    vecs, natural, turned, columns, sorted_columns = rest[-5:]
    natural[...] = flip(x_ref[...])
    exits.arrange(table, natural, turned)
    lows, dv_full = combine(dq_ref, dk_ref, dv_ref, add_ref, len(slices))
    width = dq_ref.shape[1] // len(slices)
    dvs = total(dv_full)
    base = 3 * width // LANES * LANES
    skip = 3 * width - base
    vecs[...] = jnp.zeros_like(vecs)
    vecs[skip : skip + 3] = one_ref[0:3]
    vecs[skip + 3 : skip + 6] = two_ref[0:3]
    for i, s in enumerate(slices):
        side = slice(width * i, width * i + width)
        value = mm(turned[...], lows[i])
        sums = jnp.concatenate([dqs_ref[:, side], jnp.broadcast_to(dvs[:, side], (8, width))], axis=1)
        high = sums.astype(LOW)
        rest_of = (sums - high.astype(FULL)).astype(LOW)
        heads = mm_nt(high, pick_ref[...]) + mm_nt(rest_of, pick_ref[...])
        vecs[skip + 6 : skip + 7] = expand_ref[s : s + 1]
        vecs[skip + 7 : skip + 8] = heads[0:1]
        columns[...] = vecs[...].T
        exits.arrange(table, columns, sorted_columns)
        value = jnp.concatenate([value[:, :base], value[:, base:] + sorted_columns[...]], axis=1)
        exits.emit(value, outs, i, slice(None))


def last_kernel(
    blocks, exits, lots, table, x_ref, first_ref, one_ref, two_ref, expand_ref, pick_ref, *rest
):
    n = len(blocks.arrays)
    gots, rest = rest[: 5 * len(lots)], rest[5 * len(lots) :]
    refs, rest = rest[:n], rest[n:]
    grad_ref, outs = rest[0], rest[1:-7]
    w, vecs, natural, turned, columns, sorted_columns, sems = rest[-7:]
    copies = blocks.copies(table, refs, w, sems)
    begin(copies)
    natural[...] = flip(x_ref[...])
    exits.arrange(table, natural, turned)
    vecs[...] = jnp.zeros_like(vecs)
    grad = first_ref[...]
    for number, lot in enumerate(lots):
        dq_ref, dqs_ref, dk_ref, dv_ref, add_ref = gots[5 * number : 5 * number + 5]
        lows, dv_full = combine(dq_ref, dk_ref, dv_ref, add_ref, len(lot))
        if number < len(lots) - 1:
            for low, s in zip(lows, lot):
                finish(copies[s])
                grad = grad + mm_nt(low, w[s])
            continue
        width = dq_ref.shape[1] // len(lot)
        dvs = total(dv_full)
        base = 3 * width // LANES * LANES
        skip = 3 * width - base
        vecs[skip : skip + 3] = one_ref[0:3]
        vecs[skip + 3 : skip + 6] = two_ref[0:3]
        for i, s in enumerate(lot):
            side = slice(width * i, width * i + width)
            value = mm(turned[...], lows[i])
            sums = jnp.concatenate([dqs_ref[:, side], jnp.broadcast_to(dvs[:, side], (8, width))], axis=1)
            high = sums.astype(LOW)
            rest_of = (sums - high.astype(FULL)).astype(LOW)
            heads = mm_nt(high, pick_ref[...]) + mm_nt(rest_of, pick_ref[...])
            vecs[skip + 6 : skip + 7] = expand_ref[s : s + 1]
            vecs[skip + 7 : skip + 8] = heads[0:1]
            columns[...] = vecs[...].T
            exits.arrange(table, columns, sorted_columns)
            value = jnp.concatenate([value[:, :base], value[:, base:] + sorted_columns[...]], axis=1)
            exits.emit(value, outs, i, slice(None))
            finish(copies[s])
            grad = grad + mm_nt(lows[i], w[s])
    grad_ref[...] = grad.astype(LOW)


class Plan:
    def __init__(self, rows):
        self.parts = lax.axis_size("tensor")
        self.owners = lax.axis_size("fsdp")
        self.place = lax.axis_index("tensor")
        self.owner = lax.axis_index("fsdp")
        self.core = self.owner % 2
        self.outer = self.owner // 2
        self.outers = self.owners // 2
        self.rows = rows
        self.flat = rows % 16 != 0
        self.bits = [1 << n for n in range((self.outers - 1).bit_length())]
        rising = list(range(self.outers))
        falling = [0]
        for bit in self.bits[::-1]:
            falling = falling + [n ^ bit for n in falling]
        self.orders = (rising, falling)
        own = jnp.array([rising, rising], jnp.int32) ^ self.outer
        core = jnp.array([0, 1], jnp.int32)[:, None] ^ self.core
        self.table = ((own * 2 + core) * rows).astype(jnp.int32)

    def swap(self, value, bit):
        return lax.ppermute(value, "fsdp", [(n, n ^ bit) for n in range(self.owners)])

    def turn(self, value, by):
        n = self.parts
        return lax.ppermute(value, "tensor", [(i, (i + by) % n) for i in range(n)])

    def trade(self, turn, back):
        pairs = []
        half = self.parts // 2
        for owner in range(self.owners):
            for place in range(self.parts):
                micro = (place + turn) % 2
                there = (owner - owner % 2 + place // half) * self.parts + 2 * micro + owner % 2
                here = owner * self.parts + place
                pairs.append((there, here) if back else (here, there))
        return pairs

    def blocks_of(self, value):
        return [lax.dynamic_index_in_dim(value, (self.place + turn) % 2, 0, False) for turn in range(2)]

    def collect(self, blocks):
        return [lax.ppermute(v, BOTH, self.trade(turn, False)) for turn, v in enumerate(blocks)]

    def release(self, blocks):
        return [lax.ppermute(v, BOTH, self.trade(turn, True)) for turn, v in enumerate(blocks)]

    def settle(self, first, second):
        even = self.place % 2 == 0
        return jnp.stack([jnp.where(even, first, second), jnp.where(even, second, first)])

    def around(self, shard):
        return [shard] + [self.turn(shard, by) for by in range(1, self.parts)]

    def gather(self, held):
        if self.flat:
            held = held[None]
            for bit in self.bits:
                held = jnp.concatenate([held, self.swap(held, 2 * bit)])
            return [self.natural(held, self.swap(held, 1), self.orders[0])]
        return [held] + [self.swap(held, 2 * n) for n in range(1, self.outers)]

    def pieces(self, arrays, names):
        if self.flat:
            return [(v, names, 0, None) for v in arrays]
        mine = [(v, names, 0, (0, n)) for n, v in enumerate(arrays)]
        return mine + [(self.swap(v, 1), names, 0, (1, n)) for n, v in enumerate(arrays)]

    def natural(self, mine, other, order):
        where = jnp.array([order.index(n) for n in range(self.outers)])
        both = []
        for n in range(self.outers):
            at = where[n ^ self.outer]
            pair = [lax.dynamic_index_in_dim(v, at, 0, False) for v in (mine, other)]
            both.append(jnp.where(self.core == 0, pair[0], pair[1]))
            both.append(jnp.where(self.core == 0, pair[1], pair[0]))
        return jnp.concatenate(both, axis=1)

    def exits(self, sides=(0, 1), halving=False):
        return Exits(self.flat, self.outers, self.rows, self.orders[halving], sides)


class Reduction:
    def __init__(self, plan, names, keep, send=None, halving=False):
        self.plan, self.names = plan, names
        self.halving = halving or send is None
        if send is None:
            keep, send = self.sort(keep, plan.orders[1])
        self.terms = [keep, plan.swap(send, 1)]
        self.left, self.bits = plan.outers, list(plan.bits)

    def sort(self, value, order):
        plan, names = self.plan, self.names
        value = value.reshape(len(names), plan.outers, 2, plan.rows, -1)
        size = (len(names), 1, 1, plan.rows, value.shape[-1])
        return [
            jnp.concatenate(
                [lax.dynamic_slice(value, (0, n ^ plan.outer, core, 0, 0), size)[:, 0] for n in order],
                axis=1,
            ).swapaxes(0, 1)
            for core in (plan.core, 1 - plan.core)
        ]

    def step(self):
        bit, self.bits = self.bits[0], self.bits[1:]
        self.left //= 2
        away = sum(t[self.left : 2 * self.left].astype(FULL) for t in self.terms).astype(LOW)
        self.terms = self.terms + [self.plan.swap(away, 2 * bit)]
        return away

    def ready(self):
        if self.halving:
            return [self.step() for _ in self.bits]
        return [sum(t[n].astype(FULL) for t in self.terms).astype(LOW) for n in range(1, self.plan.outers)]

    def launch(self, away, first=1):
        if not self.halving:
            self.terms += [self.plan.swap(v, 2 * (n + first))[None] for n, v in enumerate(away)]

    def turns(self):
        terms = [sum(t[0, i].astype(FULL) for t in self.terms) for i in range(len(self.names))]
        self.terms = [t for t, by in zip(terms, self.names) if not by]
        return [t.astype(LOW) for t, by in zip(terms, self.names) if by]

    def launch_turns(self, sent, which=None):
        turns = [by for by in self.names if by]
        self.terms += [
            self.plan.turn(t, -by) for t, by in zip(sent, turns) if which is None or by in which
        ]

    def total(self):
        return sum(t.astype(FULL) for t in self.terms)


def shards(
    tokens, lengths, cotangent, query_proj, key_proj, value_proj, output_proj, expand_proj,
    shrink_proj, query_bias, value_bias, expand_bias, output_bias, attn_gain, attn_shift,
    shrink_bias, ffn_gain, ffn_shift,
):
    rows, width = query_proj.shape
    plan = Plan(rows)
    parts = plan.parts
    hidden = expand_proj.shape[1]
    few = query_bias.shape[0]
    block = tokens.shape[2]
    mine = 2 * block
    model = tokens.shape[3]
    three = 3 * width
    table = plan.table
    half = parts // 2
    low_names, high_names, names = list(range(half)), list(range(half, parts)), list(range(parts))

    smalls = [output_bias, attn_gain, attn_shift, shrink_bias, ffn_gain, ffn_shift, expand_bias]
    heads_biases = jnp.pad(jnp.concatenate([query_bias, value_bias]), (0, rows - 2 * few))
    pack_one = jnp.concatenate(
        [query_proj, key_proj, value_proj, jnp.pad(jnp.concatenate(smalls + [heads_biases]).reshape(8, rows).T, ((0, 0), (0, SMALL - 8)))],
        axis=1,
    )
    gap = jnp.zeros((rows, -width % LANES), LOW)
    pack_two = jnp.concatenate([expand_proj, output_proj.T, gap, shrink_proj.T], axis=1)
    wide_one, wide_two, wide_three = pack_one.shape[1], hidden + width, hidden
    edge = pack_two.shape[1] - wide_three
    ones = plan.around(pack_one)
    ones, up_own = hold(ones, pack_two[:, :edge])
    ups = plan.around(up_own)
    one_part = plan.gather(jnp.stack(ones))
    ups, blocks = hold(ups, plan.blocks_of(tokens[:, 0]))
    own_tokens = plan.collect(blocks)
    x = jnp.concatenate(own_tokens)
    other_x = plan.swap(x, 1)
    x, down_own = hold(x, pack_two[:, edge:])
    downs = {by: plan.turn(down_own, by) for by in range(1, parts, 2)}
    one_part, up_held = hold(one_part, jnp.stack(ups))
    up_part = plan.gather(up_held)
    qkv_w = Blocks(plan.pieces(one_part, names), wide_one)
    place = jnp.arange(model)[:, None]
    head = jnp.arange(2 * width)[None, :]
    inside = head % width
    pick = (place == inside // few * rows + inside % few + few * (head // width)).astype(LOW)

    micro, parity = plan.place // 2, plan.place % 2
    seen = jnp.where(parity == plan.core, lengths, plan.swap(lengths, 1))[:, 0]
    length = jnp.where(micro == 0, seen[0], seen[1])

    def slots_of(core):
        return jnp.concatenate(
            [block * (2 * core + (micro + n) % 2) + jnp.arange(block) for n in range(2)]
        )

    row_slots = slots_of(plan.core)
    live_rows = jnp.broadcast_to((row_slots < length).astype(FULL)[:, None], (mine, LANES))
    live = jnp.concatenate([row_slots, slots_of(1 - plan.core)]) < length
    lead = jnp.arange(HD)[None, :] == 0
    extra_k = jnp.where(lead & ~live[:, None], DEAD, 0.0).astype(LOW)
    extra_q = jnp.broadcast_to(lead, (mine, HD)).astype(LOW)

    dot_cost = 2 * mine * model * model
    query, key_value, other, small = pl.pallas_call(
        functools.partial(project_kernel, qkv_w),
        out_shape=[
            shape((mine, model), LOW), shape((mine, 2 * model), LOW), shape((mine, 2 * model), LOW),
            shape((16, model), FULL),
        ],
        in_specs=[IN_SMEM, IN_VMEM, IN_VMEM, IN_VMEM] + [ANYWHERE] * len(qkv_w.arrays),
        out_specs=[IN_VMEM] * 4,
        scratch_shapes=[
            pltpu.VMEM((parts, model, wide_one), LOW),
            pltpu.SemaphoreType.DMA((qkv_w.count(),)),
        ],
        compiler_params=params(),
        cost_estimate=cost(3 * dot_cost, 8 * MIB, 0, 0.05),
        name="project",
    )(table, x, other_x, pick, *qkv_w.arrays)
    query, downs, down_own = hold(query, downs, down_own)
    downs.update({by: plan.turn(down_own, by) for by in range(2, parts, 2)})
    pairs = model // LANES
    heads = 2 * pairs
    pad_heads = -(-heads // 8) * 8
    all_rows = 2 * mine

    def lane_block(offset):
        return pl.BlockSpec((mine, LANES), lambda i: (0, i + offset))

    score_cost = 2 * mine * all_rows * HD
    attended, log_total = pl.pallas_call(
        attend_kernel,
        out_shape=[shape((mine, model), LOW), shape((pad_heads, mine), FULL)],
        grid=(pairs,),
        in_specs=[
            lane_block(0), lane_block(0), lane_block(0), lane_block(pairs), lane_block(pairs),
            fixed((all_rows, HD)), fixed((mine, HD)),
        ],
        out_specs=[lane_block(0), fixed((pad_heads, mine))],
        compiler_params=params(1),
        cost_estimate=cost(6 * heads * score_cost, 6 * MIB, heads * mine * all_rows, 0.05),
        name="attend",
    )(query, key_value, other, key_value, other, extra_k, extra_q)

    attended, up_part, downs, down_own = hold(attended, up_part, downs, down_own)
    down_part = plan.gather(jnp.stack([down_own] + [downs[n] for n in range(1, parts)]))
    up_pieces = plan.pieces(up_part, names)
    there, blocks = hold([p[0] for p in up_pieces], plan.blocks_of(cotangent[:, 0]))
    up_w = Blocks([(a, *p[1:]) for a, p in zip(there, up_pieces)], edge)
    own_cot = plan.collect(blocks)
    chunks = parts * hidden // CHUNK
    per = hidden // CHUNK
    chunk_block = pl.BlockSpec((mine, CHUNK), lambda i: (0, i))
    full_rows = fixed((mine, model))
    normed, unit, inv, normed_low, active, slope = pl.pallas_call(
        functools.partial(expand_kernel, up_w),
        out_shape=[
            shape((mine, model), FULL), shape((mine, model), FULL), shape((mine, LANES), FULL),
            shape((mine, model), LOW), shape((mine, parts * hidden), LOW), shape((mine, parts * hidden), LOW),
        ],
        grid=(chunks,),
        in_specs=[IN_SMEM, full_rows, full_rows, fixed((16, model))] + [ANYWHERE] * len(up_w.arrays),
        out_specs=[full_rows, full_rows, fixed((mine, LANES)), full_rows, chunk_block, chunk_block],
        scratch_shapes=[
            pltpu.VMEM((parts, model, edge), LOW),
            pltpu.VMEM((mine, model), FULL),
            pltpu.SemaphoreType.DMA((up_w.count(),)),
        ],
        compiler_params=params(1),
        cost_estimate=cost(8 * dot_cost, 20 * MIB),
        name="expand",
    )(table, x, attended, small, *up_w.arrays)
    active, own_cot, down_part = hold(active, own_cot, down_part)
    cot = jnp.concatenate(own_cot)
    down_w = Blocks(plan.pieces(down_part, names), wide_three)
    gate = pace(table, *down_part[:1])
    layer_rows, second_grad, second_low, vec_two = pl.pallas_call(
        functools.partial(shrink_kernel, down_w),
        out_shape=[
            shape((mine, model), LOW), shape((mine, model), FULL), shape((mine, model), LOW), shape((8, model), FULL),
        ],
        grid=(chunks,),
        in_specs=[
            IN_SMEM, chunk_block, full_rows, fixed((16, model)), full_rows, fixed((mine, LANES)),
        ] + [ANYWHERE] * len(down_w.arrays),
        out_specs=[full_rows, full_rows, full_rows, fixed((8, model))],
        scratch_shapes=[
            pltpu.VMEM((parts, model, wide_three), LOW),
            pltpu.VMEM((mine, model), FULL),
            pltpu.SemaphoreType.DMA((down_w.count(),)),
        ],
        compiler_params=params(1),
        cost_estimate=cost(5 * dot_cost, 16 * MIB),
        name="shrink",
    )(gate, active, normed, small, cot, live_rows, *down_w.arrays)
    def shrink_grad(sides, ready):
        exits = plan.exits(sides)
        if plan.flat:
            grad_block = [pl.BlockSpec((1, model, CHUNK), lambda i: (i // per, 0, i % per))]
        else:
            grad_block = [
                pl.BlockSpec((plan.outers, 1, rows, CHUNK), lambda i: (0, i // per, 0, i % per))
            ] * len(sides)
        return pl.pallas_call(
            functools.partial(shrink_grad_kernel, exits),
            out_shape=exits.shapes(parts, hidden),
            grid=(chunks,),
            in_specs=[IN_SMEM, full_rows, chunk_block],
            out_specs=grad_block,
            scratch_shapes=[pltpu.VMEM((model, mine), LOW), pltpu.VMEM((exits.height(), mine), LOW)],
            compiler_params=params(1),
            cost_estimate=cost(4 * dot_cost // (3 - len(sides)), 9 * MIB),
            name="shrink_grad",
        )(table, ready, active)

    if plan.flat:
        three_red = Reduction(plan, names, *shrink_grad((0, 1), second_low))
    else:
        (send,) = shrink_grad((1,), second_low)
        second_low, send = hold(second_low, send)
        (keep,) = shrink_grad((0,), second_low)
        three_red = Reduction(plan, names, keep, send)
    second_low, away, layer_rows = hold(second_low, three_red.ready(), layer_rows)
    three_red.launch(away)
    layer_got = plan.release([layer_rows[:block], layer_rows[block:]])

    exits = plan.exits()
    grad_shapes = exits.shapes(parts, wide_two)
    first_grad, first_low, attended_grad, vec_one, expand_sums, *blocks = pl.pallas_call(
        functools.partial(middle_kernel, up_w, down_w, exits),
        out_shape=[
            shape((mine, model), FULL), shape((mine, model), LOW), shape((mine, model), LOW),
            shape((8, model), FULL), shape((8, model), FULL),
        ] + grad_shapes,
        grid=(chunks,),
        in_specs=[
            IN_SMEM, full_rows, full_rows, chunk_block, full_rows, full_rows, fixed((mine, LANES)),
            fixed((16, model)), full_rows,
        ] + [ANYWHERE] * (len(up_w.arrays) + len(down_w.arrays)),
        out_specs=[full_rows, full_rows, full_rows, fixed((8, model)), fixed((8, model))]
        + [fixed(g.shape) for g in grad_shapes],
        scratch_shapes=[
            pltpu.VMEM((parts, model, edge), LOW),
            pltpu.VMEM((parts, model, wide_three), LOW),
            pltpu.SemaphoreType.DMA((up_w.count(),)),
            pltpu.SemaphoreType.DMA((down_w.count(),)),
            pltpu.VMEM((model, mine), LOW),
            pltpu.VMEM((model, mine), LOW),
            pltpu.VMEM((mine, model), FULL),
        ],
        compiler_params=params(1),
        cost_estimate=cost(14 * dot_cost, 30 * MIB),
        name="middle",
    )(
        table, second_low, normed_low, slope, second_grad, unit, inv, small, attended,
        *up_w.arrays, *down_w.arrays,
    )
    two_red = Reduction(plan, names, *blocks)
    gate = pace(table, first_low, *three_red.terms[2:], *layer_got)
    gate, attended_grad, two_red.terms, three_red.terms, layer_got = hold(
        gate, attended_grad, two_red.terms, three_red.terms, layer_got
    )
    attended_grad, away, sent = hold(attended_grad, two_red.ready(), three_red.turns())
    two_red.launch(away[:-1])
    three_red.launch_turns(sent)

    few_pairs = pairs // 2

    def attend_back(lot, grad, weight):
        first = lot[0] * width // LANES
        wide = len(lot) * width

        def from_block(offset):
            return pl.BlockSpec((mine, LANES), lambda i: (0, i + first + offset))

        lot_block = pl.BlockSpec((mine, LANES), lambda i: (0, i))
        return pl.pallas_call(
            functools.partial(attend_back_kernel, first),
            out_shape=[
                shape((mine, wide), LOW), shape((8, wide), FULL), shape((mine, wide), FULL),
                shape((mine, wide), FULL), shape((mine, 2 * wide), LOW),
            ],
            grid=(few_pairs,),
            in_specs=[
                from_block(0), from_block(0), from_block(0), from_block(0), from_block(0),
                from_block(pairs), from_block(pairs), fixed((all_rows, HD)), fixed((mine, HD)),
                fixed((pad_heads, mine)),
            ],
            out_specs=[
                lot_block, pl.BlockSpec((8, LANES), lambda i: (0, i)), lot_block, lot_block,
                pl.BlockSpec((mine, 2 * LANES), lambda i: (0, i)),
            ],
            compiler_params=params(1),
            cost_estimate=cost(10 * heads * score_cost, 8 * MIB, heads * mine * all_rows // 2, weight),
            name="attend_back",
        )(
            query, grad, attended, key_value, other, key_value, other, extra_k, extra_q, log_total,
        )

    def weight_step(lot, got):
        exits = plan.exits()
        grad_shapes = exits.shapes(len(lot), wide_one)
        return pl.pallas_call(
            functools.partial(weight_kernel, exits, lot),
            out_shape=grad_shapes,
            in_specs=[IN_SMEM] + [IN_VMEM] * 10,
            out_specs=[IN_VMEM] * len(grad_shapes),
            scratch_shapes=[
                pltpu.VMEM((LANES, model), FULL),
                pltpu.VMEM((model, mine), LOW),
                pltpu.VMEM((model, mine), LOW),
                pltpu.VMEM((model, LANES), FULL),
                pltpu.VMEM((model, LANES), FULL),
            ],
            compiler_params=params(),
            cost_estimate=cost(2 * dot_cost, 9 * MIB, 0, 0.05),
            name="weight_grad",
        )(table, x, *got, vec_one, vec_two, expand_sums, pick)

    def last_step(gate, lots, gots):
        exits = plan.exits()
        grad_shapes = exits.shapes(len(lots[-1]), wide_one)
        return pl.pallas_call(
            functools.partial(last_kernel, qkv_w, exits, lots),
            out_shape=[shape((mine, model), LOW)] + grad_shapes,
            in_specs=[IN_SMEM] + [IN_VMEM] * (6 + 5 * len(lots)) + [ANYWHERE] * len(qkv_w.arrays),
            out_specs=[IN_VMEM] * (1 + len(grad_shapes)),
            scratch_shapes=[
                pltpu.VMEM((parts, model, wide_one), LOW),
                pltpu.VMEM((LANES, model), FULL),
                pltpu.VMEM((model, mine), LOW),
                pltpu.VMEM((model, mine), LOW),
                pltpu.VMEM((model, LANES), FULL),
                pltpu.VMEM((model, LANES), FULL),
                pltpu.SemaphoreType.DMA((qkv_w.count(),)),
            ],
            compiler_params=params(),
            cost_estimate=cost(6 * dot_cost, 20 * MIB),
            name="input_grad",
        )(
            gate, x, first_grad, vec_one, vec_two, expand_sums, pick, *[v for g in gots for v in g],
            *qkv_w.arrays,
        )

    def cross(got):
        return *got[:-1], plan.swap(got[-1], 1)

    high = attend_back(high_names, attended_grad, 20)
    high, attended_grad, far, three_red.terms = hold(high, attended_grad, away[-1:], three_red.terms)
    two_red.launch(far, plan.outers - 1)
    high = cross(high)
    low = cross(attend_back(low_names, attended_grad, 20))
    blocks = weight_step(high_names, high)
    high_red = Reduction(plan, high_names, *blocks)
    gate = pace(gate, blocks[0], low[0], *two_red.terms[2:])
    gate, two_red.terms, high_red.terms = hold(gate, two_red.terms, high_red.terms)
    gate, away, sent = hold(gate, high_red.ready(), two_red.turns())
    high_red.launch(away[:-1])
    two_red.launch_turns(sent)
    input_grad, *blocks = last_step(gate, (high_names, low_names), (high, low))
    input_grad, blocks, two_red.terms, high_red.terms, far = hold(
        input_grad, blocks, two_red.terms, high_red.terms, away[-1:]
    )
    low_red = Reduction(plan, low_names, *blocks)
    high_red.launch(far, plan.outers - 1)
    input_got = plan.release([input_grad[:block], input_grad[block:]])
    gate = pace(gate, blocks[0])
    gate, low_red.terms = hold(gate, low_red.terms)
    low_red.launch(low_red.ready())
    high_red.launch_turns(high_red.turns())
    sent, two_red.terms, three_red.terms, layer_got = hold(
        low_red.turns(), two_red.terms, three_red.terms, layer_got
    )
    low_red.launch_turns(sent)
    sums_two = two_red.total()
    input_got, layer_out, *done = hold(
        input_got, plan.settle(*layer_got), sums_two[:, hidden:].T, sums_two[:, :hidden], three_red.total().T
    )
    input_rows = plan.settle(*input_got).astype(FULL)
    sums_one = high_red.total() + low_red.total()
    sums_one += jnp.minimum(gate[0, 0], 0).astype(FULL)
    quarter = rows // parts
    own = lax.dynamic_slice_in_dim(sums_one[:, three : three + 6], plan.place * quarter, quarter, 0)
    return (
        layer_out[:, None],
        input_rows[:, None],
        sums_one[:, :width],
        sums_one[:, width : 2 * width],
        sums_one[:, 2 * width : three],
        *done,
        sums_one[:few, three + 7],
        sums_one[few : 2 * few, three + 7],
        sums_one[:, three + 6],
        own[:, 0],
        own[:, 1],
        own[:, 2],
        own[:, 3],
        own[:, 4],
        own[:, 5],
    )


def solution(mesh):
    rows = P(None, "fsdp", "tensor", None)
    split = P("fsdp", "tensor")
    turned = P("tensor", "fsdp")
    heads = P(("tensor", "fsdp"))
    model = P("fsdp")
    spread = P(("fsdp", "tensor"))
    return jax.shard_map(
        shards,
        mesh=mesh,
        in_specs=(rows, P(None, "fsdp"), rows, split, split, split, turned, split, turned)
        + (heads,) * 3
        + (model,) * 6,
        out_specs=(rows, rows, split, split, split, turned, split, turned)
        + (heads,) * 3
        + (spread,) * 6,
        check_vma=False,
    )
```

```python
import functools
import math

import jax
import jax.numpy as jnp
from jax import lax
from jax.experimental import pallas as pl
from jax.experimental.pallas import tpu as pltpu
from jax.sharding import PartitionSpec as P

HD = 64
EPS = 1e-05
DEAD = -8000000000.0
ROOT_HALF = 0.7071067811865476
DENSITY = 0.3989422804014327
LOG2E = 1.4426950408889634
SCALE2 = 0.125 * LOG2E
BOTH = ("fsdp", "tensor")
LOW = jnp.bfloat16
FULL = jnp.float32
LANES = 128
CHUNK = 768
QUERIES = 512
ROWS = 256
MIB = 1 << 20
NT = (((1,), (1,)), ((), ()))
SMALL = 64

IN_VMEM = pl.BlockSpec(memory_space=pltpu.VMEM)
IN_SMEM = pl.BlockSpec(memory_space=pltpu.SMEM)
ANYWHERE = pl.BlockSpec(memory_space=pl.ANY)


def shape(dims, dtype):
    return jax.ShapeDtypeStruct(dims, dtype)


def fixed(dims):
    return pl.BlockSpec(dims, lambda i: (0,) * len(dims))


def params(grid=0, vmem=56):
    return pltpu.CompilerParams(
        vmem_limit_bytes=vmem * MIB, dimension_semantics=("arbitrary",) * grid if grid else None
    )


def cost(flops, touched, exps=0, weight=20):
    return pl.CostEstimate(
        flops=int(weight * flops), bytes_accessed=int(weight * touched), transcendentals=int(weight * exps)
    )


def mm(left, right):
    return jnp.dot(left, right, preferred_element_type=FULL)


def mm_nt(left, right):
    return lax.dot_general(left, right, NT, preferred_element_type=FULL)


def flip(value):
    return value.astype(FULL).T.astype(value.dtype)


def pace_kernel(in_ref, *rest):
    out_ref = rest[-1]
    for row in range(in_ref.shape[0]):
        for n in range(in_ref.shape[1]):
            out_ref[row, n] = in_ref[row, n]


def pace(table, *ready):
    return pl.pallas_call(
        pace_kernel,
        out_shape=shape(table.shape, table.dtype),
        in_specs=[IN_SMEM] + [ANYWHERE] * len(ready),
        out_specs=IN_SMEM,
        cost_estimate=pl.CostEstimate(flops=10**11, bytes_accessed=10**9, transcendentals=0),
        name="pace",
    )(table, *ready)


def hold(*values):
    return lax.optimization_barrier(values)


class Blocks:
    def __init__(self, pieces, width):
        self.pieces, self.width = pieces, width
        self.arrays = [p[0] for p in pieces]

    def count(self):
        return sum(len(p[1]) for p in self.pieces)

    def copies(self, table, refs, scratch, sems, wanted=None):
        found = {}
        at = 0
        for ref, (_, slices, lane, where) in zip(refs, self.pieces):
            rows = ref.shape[1]
            start = 0 if where is None else pl.multiple_of(table[where[0], where[1]], 16)
            for place, s in enumerate(slices):
                if wanted is not None and s not in wanted:
                    continue
                found.setdefault(s, []).append(
                    pltpu.make_async_copy(
                        ref.at[place, :, pl.ds(lane, self.width)],
                        scratch.at[s, pl.ds(start, rows), :],
                        sems.at[at],
                    )
                )
                at += 1
        return found


def begin(copies):
    for group in copies.values():
        for copy in group:
            copy.start()


def finish(group):
    for copy in group:
        copy.wait()


def project_kernel(blocks, table, x_ref, other_ref, pick_ref, *rest):
    n = len(blocks.arrays)
    refs, (q_ref, kv_ref, other_kv_ref, small_ref, w, sems) = rest[:n], rest[n:]
    copies = blocks.copies(table, refs, w, sems)
    begin(copies)
    parts = len(copies)
    third = q_ref.shape[1] // parts
    base = 3 * third // LANES * LANES
    skip = 3 * third - base
    small_ref[...] = jnp.zeros_like(small_ref)
    lead = third // LANES * LANES
    queries, keys, values, other_keys, other_values = [], [], [], [], []
    for s in range(parts):
        finish(copies[s])
        turned = w[s, :, base:].astype(FULL).T
        few = turned[skip : skip + 8]
        if s == 0:
            small_ref[0:8] = few
        small_ref[8 + s : 9 + s] = few[6:7]
        bias = mm(few.astype(LOW), pick_ref[...])[7:8]
        y = mm(x_ref[...], w[s])
        queries.append(y[:, :third] + bias[:, :third])
        keys.append(y[:, third : 2 * third])
        values.append(y[:, 2 * third : 3 * third] + bias[:, third:])
        y = mm(other_ref[...], w[s, :, lead:])
        other_keys.append(y[:, third - lead : 2 * third - lead])
        other_values.append(y[:, 2 * third - lead : 3 * third - lead] + bias[:, third:])
    q_ref[...] = jnp.concatenate(queries, axis=1).astype(LOW)
    width = q_ref.shape[1]
    for ref, k, v in ((kv_ref, keys, values), (other_kv_ref, other_keys, other_values)):
        ref[:, :width] = jnp.concatenate(k, axis=1).astype(LOW)
        ref[:, width:] = jnp.concatenate(v, axis=1).astype(LOW)


def attend_kernel(q_ref, ko, ke, vo, ve, xk_ref, xq_ref, att_ref, lse_ref):
    pair = pl.program_id(0)
    k = jnp.concatenate([ko[...], ke[...]], axis=0)
    v_t = flip(jnp.concatenate([vo[...], ve[...]], axis=0))
    q = q_ref[...]
    rows = q.shape[0]
    ones = jnp.ones((16, k.shape[0]), LOW)
    outs = []
    for h in range(2):
        side = slice(HD * h, HD * h + HD)
        kh = jnp.concatenate([k[:, side], xk_ref[...]], axis=1)
        qh = jnp.concatenate([q[:, side], xq_ref[...]], axis=1)
        vt = jnp.concatenate([v_t[side], ones], axis=0)
        got = []
        for start in range(0, rows, QUERIES):
            span = slice(start, start + QUERIES)
            scores = mm_nt(kh, qh[span])
            top = jnp.max(scores, axis=0, keepdims=True)
            raised = jnp.exp2((scores - top) * SCALE2).astype(LOW)
            o = mm(vt, raised)
            denom = o[HD : HD + 1]
            got.append(o[:HD] * (1.0 / denom))
            lse_ref[pl.ds(2 * pair + h, 1), span] = top * SCALE2 + jnp.log2(denom)
        outs.append(jnp.concatenate(got, axis=1))
    att_ref[...] = jnp.concatenate(outs, axis=0).T.astype(LOW)


def attend_back_kernel(
    first, q_ref, g_ref, att_ref, ko, ke, vo, ve, xk_ref, xq_ref, lse_ref,
    dq_ref, sum_ref, dk_ref, dv_ref, away_ref,
):
    pair = pl.program_id(0) + first
    k = jnp.concatenate([ko[...], ke[...]], axis=0)
    v = jnp.concatenate([vo[...], ve[...]], axis=0)
    k_t = flip(k)
    q, g = q_ref[...], g_ref[...]
    rows = q.shape[0]
    product = (g.astype(FULL) * att_ref[...].astype(FULL)).T
    dqs, dks, dvs = [], [], []
    for h in range(2):
        side = slice(HD * h, HD * h + HD)
        kh = jnp.concatenate([k[:, side], xk_ref[...]], axis=1)
        qh = jnp.concatenate([q[:, side], xq_ref[...]], axis=1)
        inner = jnp.sum(product[side], axis=0, keepdims=True)
        lse = lse_ref[pl.ds(2 * pair + h, 1), :]
        vh, gh, qs = v[:, side], g[:, side], q[:, side]
        dk = dv = None
        got = []
        for start in range(0, rows, QUERIES):
            span = slice(start, start + QUERIES)
            probs = jnp.exp2(mm_nt(kh, qh[span]) * SCALE2 - lse[:, span])
            prob_grad = mm_nt(vh, gh[span])
            score_grad = (probs * (prob_grad - inner[:, span])).astype(LOW)
            more_v = mm(probs.astype(LOW), gh[span])
            more_k = mm(score_grad, qs[span])
            dv = more_v if dv is None else dv + more_v
            dk = more_k if dk is None else dk + more_k
            got.append(mm(k_t[side], score_grad))
        dqs.append(jnp.concatenate(got, axis=1))
        dks.append(dk)
        dvs.append(dv)
    dq = jnp.concatenate(dqs, axis=0).T * 0.125
    dq_ref[...] = dq.astype(LOW)
    sum_ref[...] = jnp.broadcast_to(jnp.sum(dq, axis=0, keepdims=True), sum_ref.shape)
    dk = jnp.concatenate(dks, axis=1) * 0.125
    dv = jnp.concatenate(dvs, axis=1)
    dk_ref[...] = dk[:rows]
    dv_ref[...] = dv[:rows]
    away_ref[:, :LANES] = dk[rows:].astype(LOW)
    away_ref[:, LANES:] = dv[rows:].astype(LOW)


def means(value):
    return jnp.mean(value, axis=-1, keepdims=True)


def normalize(summed):
    center = summed - means(summed)
    inv = lax.rsqrt(means(center * center) + EPS)
    return center * inv, inv


def norm_back(grad, gain, unit, inv):
    scaled = grad * gain
    return inv * (scaled - means(scaled) - unit * means(scaled * unit))


def total(value):
    return jnp.sum(value, axis=0, keepdims=True)


def expand_kernel(blocks, table, x_ref, att_ref, small_ref, *rest):
    n = len(blocks.arrays)
    refs = rest[:n]
    normed_ref, unit_ref, inv_ref, low_ref, act_ref, slope_ref, w, attn, sems = rest[n:]
    copies = blocks.copies(table, refs, w, sems)
    parts = len(copies)
    step = pl.program_id(0)
    hidden = x_ref.shape[1]
    width = hidden // parts

    @pl.when(step == 0)
    def _():
        begin(copies)
        for s in range(parts):
            finish(copies[s])
        value = None
        for s in range(parts):
            more = mm_nt(att_ref[:, width * s : width * s + width], w[s, :, hidden : hidden + width])
            value = more if value is None else value + more
        attn[...] = value

        @pl.loop(0, x_ref.shape[0] // ROWS)
        def _(i):
            span = pl.ds(pl.multiple_of(i * ROWS, ROWS), ROWS)
            summed = x_ref[span].astype(FULL) + attn[span] + small_ref[0:1]
            unit, inv = normalize(summed)
            normed = unit * small_ref[1:2] + small_ref[2:3]
            normed_ref[span] = normed
            unit_ref[span] = unit
            inv_ref[span] = jnp.broadcast_to(inv, (ROWS, LANES))
            low_ref[span] = normed.astype(LOW)

    per = hidden // CHUNK
    s, lanes = step // per, pl.ds(pl.multiple_of(step % per * CHUNK, CHUNK), CHUNK)
    bias = small_ref[pl.ds(8 + s, 1), lanes]
    upper = mm(low_ref[...], w[s, :, lanes]) + bias
    below = 0.5 * (1.0 + lax.erf(upper * ROOT_HALF))
    act_ref[...] = (upper * below).astype(LOW)
    slope_ref[...] = (below + upper * jnp.exp(-0.5 * upper * upper) * DENSITY).astype(LOW)


def shrink_kernel(blocks, table, act_ref, normed_ref, small_ref, cot_ref, live_ref, *rest):
    n = len(blocks.arrays)
    refs = rest[:n]
    out_ref, grad_ref, low_ref, vec_ref, w, acc, sems = rest[n:]
    copies = blocks.copies(table, refs, w, sems)
    step = pl.program_id(0)
    hidden = normed_ref.shape[1]
    per = hidden // CHUNK
    s, lanes = step // per, pl.ds(pl.multiple_of(step % per * CHUNK, CHUNK), CHUNK)

    @pl.when(step == 0)
    def _():
        begin(copies)

    for part, group in copies.items():

        @pl.when(step == part * per)
        def _(group=group):
            finish(group)

    more = mm_nt(act_ref[...], w[s, :, lanes])

    @pl.when(step == 0)
    def _():
        acc[...] = more

    @pl.when(step > 0)
    def _():
        acc[...] += more

    @pl.when(step == pl.num_programs(0) - 1)
    def _():
        vec_ref[...] = jnp.zeros_like(vec_ref)

        @pl.loop(0, normed_ref.shape[0] // ROWS)
        def _(i):
            span = pl.ds(pl.multiple_of(i * ROWS, ROWS), ROWS)
            summed = normed_ref[span] + acc[span] + small_ref[3:4]
            unit, inv = normalize(summed)
            out_ref[span] = (unit * small_ref[4:5] + small_ref[5:6]).astype(LOW)
            arriving = cot_ref[span].astype(FULL) * live_ref[span, 0:1]
            grad = norm_back(arriving, small_ref[4:5], unit, inv)
            grad_ref[span] = grad
            low_ref[span] = grad.astype(LOW)
            vec_ref[0:1] += total(grad)
            vec_ref[1:2] += total(arriving * unit)
            vec_ref[2:3] += total(arriving)


class Exits:
    def __init__(self, flat, outers, rows, order, sides=(0, 1)):
        self.flat, self.outers, self.rows, self.order, self.sides = flat, outers, rows, order, sides

    def height(self):
        return 2 * self.outers * self.rows if self.flat else len(self.sides) * self.outers * self.rows

    def shapes(self, slices, width):
        if self.flat:
            return [shape((slices, self.height(), width), LOW)]
        return [shape((self.outers, slices, self.rows, width), LOW)] * len(self.sides)

    def arrange(self, table, source, target):
        if self.flat:
            target[...] = source[...]
            return
        at = 0
        for side in self.sides:
            for n in self.order:
                start = pl.multiple_of(table[side, n], 16)
                target[at : at + self.rows] = source[pl.ds(start, self.rows), :]
                at += self.rows

    def emit(self, value, refs, s, lanes):
        value = value.astype(LOW)
        if self.flat:
            refs[0][s, :, lanes] = value
            return
        at = 0
        for ref in refs:
            for i in range(self.outers):
                ref[i, s, :, lanes] = value[at : at + self.rows]
                at += self.rows


def shrink_grad_kernel(exits, table, low_ref, act_ref, *rest):
    outs, (natural, turned) = rest[:-2], rest[-2:]

    @pl.when(pl.program_id(0) == 0)
    def _():
        natural[...] = flip(low_ref[...])
        exits.arrange(table, natural, turned)

    exits.emit(mm(turned[...], act_ref[...]), outs, 0, slice(None))


def middle_kernel(
    ups, downs, exits, table, low_ref, normed_low_ref, slope_ref, grad_ref, unit_ref, inv_ref,
    small_ref, att_ref, *rest,
):
    n, m = len(ups.arrays), len(downs.arrays)
    up_refs, down_refs, rest = rest[:n], rest[n : n + m], rest[n + m :]
    first_ref, first_low_ref, att_grad_ref, vec_ref, expand_ref = rest[:5]
    outs = rest[5:-7]
    up_w, down_w, up_sems, down_sems, natural, turned, acc = rest[-7:]
    up_copies = ups.copies(table, up_refs, up_w, up_sems)
    down_copies = downs.copies(table, down_refs, down_w, down_sems)
    parts = len(up_copies)
    step = pl.program_id(0)
    hidden = unit_ref.shape[1]
    width = hidden // parts
    per = hidden // CHUNK
    s, lanes = step // per, pl.ds(pl.multiple_of(step % per * CHUNK, CHUNK), CHUNK)

    @pl.when(step == 0)
    def _():
        for part in range(parts):
            begin({0: down_copies[part], 1: up_copies[part]})
        natural[...] = flip(normed_low_ref[...])
        exits.arrange(table, natural, turned)
        expand_ref[...] = jnp.zeros_like(expand_ref)

    for part in range(parts):

        @pl.when(step == part * per)
        def _(part=part):
            finish(down_copies[part])
            finish(up_copies[part])

    upper_grad = mm(low_ref[...], down_w[s, :, lanes]) * slope_ref[...].astype(FULL)
    expand_ref[pl.ds(s, 1), lanes] = total(upper_grad)
    upper_low = upper_grad.astype(LOW)
    exits.emit(mm(turned[...], upper_low), outs, s, lanes)
    more = mm_nt(upper_low, up_w[s, :, lanes])

    @pl.when(step == 0)
    def _():
        acc[...] = more

    @pl.when(step > 0)
    def _():
        acc[...] += more

    @pl.when(step == pl.num_programs(0) - 1)
    def _():
        vec_ref[...] = jnp.zeros_like(vec_ref)

        @pl.loop(0, unit_ref.shape[0] // ROWS)
        def _(i):
            span = pl.ds(pl.multiple_of(i * ROWS, ROWS), ROWS)
            grad = acc[span] + grad_ref[span]
            unit = unit_ref[span]
            first = norm_back(grad, small_ref[1:2], unit, inv_ref[span, 0:1])
            first_ref[span] = first
            first_low_ref[span] = first.astype(LOW)
            vec_ref[0:1] += total(first)
            vec_ref[1:2] += total(grad * unit)
            vec_ref[2:3] += total(grad)

        natural[...] = flip(first_low_ref[...])
        exits.arrange(table, natural, turned)
        grads = []
        for part in range(parts):
            o = up_w[part, :, hidden : hidden + width]
            grads.append(mm(first_low_ref[...], o))
            value = mm(turned[...], att_ref[:, width * part : width * part + width])
            exits.emit(value, outs, part, slice(hidden, hidden + width))
        att_grad_ref[...] = jnp.concatenate(grads, axis=1).astype(LOW)


def combine(dq_ref, dk_ref, dv_ref, add_ref, number):
    rows, wide = dq_ref.shape
    width = wide // number
    added = [add_ref[:, at : at + LANES] for at in range(0, 2 * wide, LANES)]
    dq = dq_ref[...]
    dk = (dk_ref[...] + jnp.concatenate(added[::2], axis=1).astype(FULL)).astype(LOW)
    dv_full = dv_ref[...] + jnp.concatenate(added[1::2], axis=1).astype(FULL)
    dv = dv_full.astype(LOW)
    blank = jnp.zeros((rows, SMALL), LOW)
    spans = [slice(width * i, width * i + width) for i in range(number)]
    return [jnp.concatenate([dq[:, p], dk[:, p], dv[:, p], blank], axis=1) for p in spans], dv_full


def weight_kernel(
    exits, slices, table, x_ref, dq_ref, dqs_ref, dk_ref, dv_ref, add_ref, one_ref, two_ref,
    expand_ref, pick_ref, *rest,
):
    outs = rest[:-5]
    vecs, natural, turned, columns, sorted_columns = rest[-5:]
    natural[...] = flip(x_ref[...])
    exits.arrange(table, natural, turned)
    lows, dv_full = combine(dq_ref, dk_ref, dv_ref, add_ref, len(slices))
    width = dq_ref.shape[1] // len(slices)
    dvs = total(dv_full)
    base = 3 * width // LANES * LANES
    skip = 3 * width - base
    vecs[...] = jnp.zeros_like(vecs)
    vecs[skip : skip + 3] = one_ref[0:3]
    vecs[skip + 3 : skip + 6] = two_ref[0:3]
    for i, s in enumerate(slices):
        side = slice(width * i, width * i + width)
        value = mm(turned[...], lows[i])
        sums = jnp.concatenate([dqs_ref[:, side], jnp.broadcast_to(dvs[:, side], (8, width))], axis=1)
        high = sums.astype(LOW)
        rest_of = (sums - high.astype(FULL)).astype(LOW)
        heads = mm_nt(high, pick_ref[...]) + mm_nt(rest_of, pick_ref[...])
        vecs[skip + 6 : skip + 7] = expand_ref[s : s + 1]
        vecs[skip + 7 : skip + 8] = heads[0:1]
        columns[...] = vecs[...].T
        exits.arrange(table, columns, sorted_columns)
        value = jnp.concatenate([value[:, :base], value[:, base:] + sorted_columns[...]], axis=1)
        exits.emit(value, outs, i, slice(None))


def last_kernel(
    blocks, exits, lots, table, x_ref, first_ref, one_ref, two_ref, expand_ref, pick_ref, *rest
):
    n = len(blocks.arrays)
    gots, rest = rest[: 5 * len(lots)], rest[5 * len(lots) :]
    refs, rest = rest[:n], rest[n:]
    grad_ref, outs = rest[0], rest[1:-7]
    w, vecs, natural, turned, columns, sorted_columns, sems = rest[-7:]
    copies = blocks.copies(table, refs, w, sems)
    begin(copies)
    natural[...] = flip(x_ref[...])
    exits.arrange(table, natural, turned)
    vecs[...] = jnp.zeros_like(vecs)
    grad = first_ref[...]
    for number, lot in enumerate(lots):
        dq_ref, dqs_ref, dk_ref, dv_ref, add_ref = gots[5 * number : 5 * number + 5]
        lows, dv_full = combine(dq_ref, dk_ref, dv_ref, add_ref, len(lot))
        if number < len(lots) - 1:
            for low, s in zip(lows, lot):
                finish(copies[s])
                grad = grad + mm_nt(low, w[s])
            continue
        width = dq_ref.shape[1] // len(lot)
        dvs = total(dv_full)
        base = 3 * width // LANES * LANES
        skip = 3 * width - base
        vecs[skip : skip + 3] = one_ref[0:3]
        vecs[skip + 3 : skip + 6] = two_ref[0:3]
        for i, s in enumerate(lot):
            side = slice(width * i, width * i + width)
            value = mm(turned[...], lows[i])
            sums = jnp.concatenate([dqs_ref[:, side], jnp.broadcast_to(dvs[:, side], (8, width))], axis=1)
            high = sums.astype(LOW)
            rest_of = (sums - high.astype(FULL)).astype(LOW)
            heads = mm_nt(high, pick_ref[...]) + mm_nt(rest_of, pick_ref[...])
            vecs[skip + 6 : skip + 7] = expand_ref[s : s + 1]
            vecs[skip + 7 : skip + 8] = heads[0:1]
            columns[...] = vecs[...].T
            exits.arrange(table, columns, sorted_columns)
            value = jnp.concatenate([value[:, :base], value[:, base:] + sorted_columns[...]], axis=1)
            exits.emit(value, outs, i, slice(None))
            finish(copies[s])
            grad = grad + mm_nt(lows[i], w[s])
    grad_ref[...] = grad.astype(LOW)


class Plan:
    def __init__(self, rows):
        self.parts = lax.axis_size("tensor")
        self.owners = lax.axis_size("fsdp")
        self.place = lax.axis_index("tensor")
        self.owner = lax.axis_index("fsdp")
        self.core = self.owner % 2
        self.outer = self.owner // 2
        self.outers = self.owners // 2
        self.rows = rows
        self.flat = rows % 16 != 0
        self.bits = [1 << n for n in range((self.outers - 1).bit_length())]
        rising = list(range(self.outers))
        falling = [0]
        for bit in self.bits[::-1]:
            falling = falling + [n ^ bit for n in falling]
        self.orders = (rising, falling)
        own = jnp.array([rising, rising], jnp.int32) ^ self.outer
        core = jnp.array([0, 1], jnp.int32)[:, None] ^ self.core
        self.table = ((own * 2 + core) * rows).astype(jnp.int32)

    def swap(self, value, bit):
        return lax.ppermute(value, "fsdp", [(n, n ^ bit) for n in range(self.owners)])

    def turn(self, value, by):
        n = self.parts
        return lax.ppermute(value, "tensor", [(i, (i + by) % n) for i in range(n)])

    def trade(self, turn, back):
        pairs = []
        half = self.parts // 2
        for owner in range(self.owners):
            for place in range(self.parts):
                micro = (place + turn) % 2
                there = (owner - owner % 2 + place // half) * self.parts + 2 * micro + owner % 2
                here = owner * self.parts + place
                pairs.append((there, here) if back else (here, there))
        return pairs

    def blocks_of(self, value):
        return [lax.dynamic_index_in_dim(value, (self.place + turn) % 2, 0, False) for turn in range(2)]

    def collect(self, blocks):
        return [lax.ppermute(v, BOTH, self.trade(turn, False)) for turn, v in enumerate(blocks)]

    def release(self, blocks):
        return [lax.ppermute(v, BOTH, self.trade(turn, True)) for turn, v in enumerate(blocks)]

    def settle(self, first, second):
        even = self.place % 2 == 0
        return jnp.stack([jnp.where(even, first, second), jnp.where(even, second, first)])

    def around(self, shard):
        return [shard] + [self.turn(shard, by) for by in range(1, self.parts)]

    def gather(self, held):
        if self.flat:
            held = held[None]
            for bit in self.bits:
                held = jnp.concatenate([held, self.swap(held, 2 * bit)])
            return [self.natural(held, self.swap(held, 1), self.orders[0])]
        return [held] + [self.swap(held, 2 * n) for n in range(1, self.outers)]

    def pieces(self, arrays, names):
        if self.flat:
            return [(v, names, 0, None) for v in arrays]
        mine = [(v, names, 0, (0, n)) for n, v in enumerate(arrays)]
        return mine + [(self.swap(v, 1), names, 0, (1, n)) for n, v in enumerate(arrays)]

    def natural(self, mine, other, order):
        where = jnp.array([order.index(n) for n in range(self.outers)])
        both = []
        for n in range(self.outers):
            at = where[n ^ self.outer]
            pair = [lax.dynamic_index_in_dim(v, at, 0, False) for v in (mine, other)]
            both.append(jnp.where(self.core == 0, pair[0], pair[1]))
            both.append(jnp.where(self.core == 0, pair[1], pair[0]))
        return jnp.concatenate(both, axis=1)

    def exits(self, sides=(0, 1), halving=False):
        return Exits(self.flat, self.outers, self.rows, self.orders[halving], sides)


class Reduction:
    def __init__(self, plan, names, keep, send=None, halving=False):
        self.plan, self.names = plan, names
        self.halving = halving or send is None
        if send is None:
            keep, send = self.sort(keep, plan.orders[1])
        self.terms = [keep, plan.swap(send, 1)]
        self.left, self.bits = plan.outers, list(plan.bits)

    def sort(self, value, order):
        plan, names = self.plan, self.names
        value = value.reshape(len(names), plan.outers, 2, plan.rows, -1)
        size = (len(names), 1, 1, plan.rows, value.shape[-1])
        return [
            jnp.concatenate(
                [lax.dynamic_slice(value, (0, n ^ plan.outer, core, 0, 0), size)[:, 0] for n in order],
                axis=1,
            ).swapaxes(0, 1)
            for core in (plan.core, 1 - plan.core)
        ]

    def step(self):
        bit, self.bits = self.bits[0], self.bits[1:]
        self.left //= 2
        away = sum(t[self.left : 2 * self.left].astype(FULL) for t in self.terms).astype(LOW)
        self.terms = self.terms + [self.plan.swap(away, 2 * bit)]
        return away

    def ready(self):
        if self.halving:
            return [self.step() for _ in self.bits]
        return [sum(t[n].astype(FULL) for t in self.terms).astype(LOW) for n in range(1, self.plan.outers)]

    def launch(self, away, first=1):
        if not self.halving:
            self.terms += [self.plan.swap(v, 2 * (n + first))[None] for n, v in enumerate(away)]

    def turns(self):
        terms = [sum(t[0, i].astype(FULL) for t in self.terms) for i in range(len(self.names))]
        self.terms = [t for t, by in zip(terms, self.names) if not by]
        return [t.astype(LOW) for t, by in zip(terms, self.names) if by]

    def launch_turns(self, sent, which=None):
        turns = [by for by in self.names if by]
        self.terms += [
            self.plan.turn(t, -by) for t, by in zip(sent, turns) if which is None or by in which
        ]

    def total(self):
        return sum(t.astype(FULL) for t in self.terms)


def shards(
    tokens, lengths, cotangent, query_proj, key_proj, value_proj, output_proj, expand_proj,
    shrink_proj, query_bias, value_bias, expand_bias, output_bias, attn_gain, attn_shift,
    shrink_bias, ffn_gain, ffn_shift,
):
    rows, width = query_proj.shape
    plan = Plan(rows)
    parts = plan.parts
    hidden = expand_proj.shape[1]
    few = query_bias.shape[0]
    block = tokens.shape[2]
    mine = 2 * block
    model = tokens.shape[3]
    three = 3 * width
    table = plan.table
    half = parts // 2
    low_names, high_names, names = list(range(half)), list(range(half, parts)), list(range(parts))

    smalls = [output_bias, attn_gain, attn_shift, shrink_bias, ffn_gain, ffn_shift, expand_bias]
    heads_biases = jnp.pad(jnp.concatenate([query_bias, value_bias]), (0, rows - 2 * few))
    pack_one = jnp.concatenate(
        [query_proj, key_proj, value_proj, jnp.pad(jnp.concatenate(smalls + [heads_biases]).reshape(8, rows).T, ((0, 0), (0, SMALL - 8)))],
        axis=1,
    )
    gap = jnp.zeros((rows, -width % LANES), LOW)
    pack_two = jnp.concatenate([expand_proj, output_proj.T, gap, shrink_proj.T], axis=1)
    wide_one, wide_two, wide_three = pack_one.shape[1], hidden + width, hidden
    edge = pack_two.shape[1] - wide_three
    ones = plan.around(pack_one)
    ones, up_own = hold(ones, pack_two[:, :edge])
    ups = plan.around(up_own)
    one_part = plan.gather(jnp.stack(ones))
    ups, blocks = hold(ups, plan.blocks_of(tokens[:, 0]))
    own_tokens = plan.collect(blocks)
    x = jnp.concatenate(own_tokens)
    other_x = plan.swap(x, 1)
    x, down_own = hold(x, pack_two[:, edge:])
    downs = {by: plan.turn(down_own, by) for by in range(1, parts, 2)}
    one_part, up_held = hold(one_part, jnp.stack(ups))
    up_part = plan.gather(up_held)
    qkv_w = Blocks(plan.pieces(one_part, names), wide_one)
    place = jnp.arange(model)[:, None]
    head = jnp.arange(2 * width)[None, :]
    inside = head % width
    pick = (place == inside // few * rows + inside % few + few * (head // width)).astype(LOW)

    micro, parity = plan.place // 2, plan.place % 2
    seen = jnp.where(parity == plan.core, lengths, plan.swap(lengths, 1))[:, 0]
    length = jnp.where(micro == 0, seen[0], seen[1])

    def slots_of(core):
        return jnp.concatenate(
            [block * (2 * core + (micro + n) % 2) + jnp.arange(block) for n in range(2)]
        )

    row_slots = slots_of(plan.core)
    live_rows = jnp.broadcast_to((row_slots < length).astype(FULL)[:, None], (mine, LANES))
    live = jnp.concatenate([row_slots, slots_of(1 - plan.core)]) < length
    lead = jnp.arange(HD)[None, :] == 0
    extra_k = jnp.where(lead & ~live[:, None], DEAD, 0.0).astype(LOW)
    extra_q = jnp.broadcast_to(lead, (mine, HD)).astype(LOW)

    dot_cost = 2 * mine * model * model
    query, key_value, other, small = pl.pallas_call(
        functools.partial(project_kernel, qkv_w),
        out_shape=[
            shape((mine, model), LOW), shape((mine, 2 * model), LOW), shape((mine, 2 * model), LOW),
            shape((16, model), FULL),
        ],
        in_specs=[IN_SMEM, IN_VMEM, IN_VMEM, IN_VMEM] + [ANYWHERE] * len(qkv_w.arrays),
        out_specs=[IN_VMEM] * 4,
        scratch_shapes=[
            pltpu.VMEM((parts, model, wide_one), LOW),
            pltpu.SemaphoreType.DMA((qkv_w.count(),)),
        ],
        compiler_params=params(),
        cost_estimate=cost(3 * dot_cost, 8 * MIB, 0, 0.05),
        name="project",
    )(table, x, other_x, pick, *qkv_w.arrays)
    query, downs, down_own = hold(query, downs, down_own)
    downs.update({by: plan.turn(down_own, by) for by in range(2, parts, 2)})
    pairs = model // LANES
    heads = 2 * pairs
    pad_heads = -(-heads // 8) * 8
    all_rows = 2 * mine

    def lane_block(offset):
        return pl.BlockSpec((mine, LANES), lambda i: (0, i + offset))

    score_cost = 2 * mine * all_rows * HD
    attended, log_total = pl.pallas_call(
        attend_kernel,
        out_shape=[shape((mine, model), LOW), shape((pad_heads, mine), FULL)],
        grid=(pairs,),
        in_specs=[
            lane_block(0), lane_block(0), lane_block(0), lane_block(pairs), lane_block(pairs),
            fixed((all_rows, HD)), fixed((mine, HD)),
        ],
        out_specs=[lane_block(0), fixed((pad_heads, mine))],
        compiler_params=params(1),
        cost_estimate=cost(6 * heads * score_cost, 6 * MIB, heads * mine * all_rows, 0.05),
        name="attend",
    )(query, key_value, other, key_value, other, extra_k, extra_q)

    attended, up_part, downs, down_own = hold(attended, up_part, downs, down_own)
    down_part = plan.gather(jnp.stack([down_own] + [downs[n] for n in range(1, parts)]))
    up_pieces = plan.pieces(up_part, names)
    there, blocks = hold([p[0] for p in up_pieces], plan.blocks_of(cotangent[:, 0]))
    up_w = Blocks([(a, *p[1:]) for a, p in zip(there, up_pieces)], edge)
    own_cot = plan.collect(blocks)
    chunks = parts * hidden // CHUNK
    per = hidden // CHUNK
    chunk_block = pl.BlockSpec((mine, CHUNK), lambda i: (0, i))
    full_rows = fixed((mine, model))
    normed, unit, inv, normed_low, active, slope = pl.pallas_call(
        functools.partial(expand_kernel, up_w),
        out_shape=[
            shape((mine, model), FULL), shape((mine, model), FULL), shape((mine, LANES), FULL),
            shape((mine, model), LOW), shape((mine, parts * hidden), LOW), shape((mine, parts * hidden), LOW),
        ],
        grid=(chunks,),
        in_specs=[IN_SMEM, full_rows, full_rows, fixed((16, model))] + [ANYWHERE] * len(up_w.arrays),
        out_specs=[full_rows, full_rows, fixed((mine, LANES)), full_rows, chunk_block, chunk_block],
        scratch_shapes=[
            pltpu.VMEM((parts, model, edge), LOW),
            pltpu.VMEM((mine, model), FULL),
            pltpu.SemaphoreType.DMA((up_w.count(),)),
        ],
        compiler_params=params(1),
        cost_estimate=cost(8 * dot_cost, 20 * MIB),
        name="expand",
    )(table, x, attended, small, *up_w.arrays)
    active, own_cot, down_part = hold(active, own_cot, down_part)
    cot = jnp.concatenate(own_cot)
    down_w = Blocks(plan.pieces(down_part, names), wide_three)
    gate = pace(table, *down_part[:1])
    layer_rows, second_grad, second_low, vec_two = pl.pallas_call(
        functools.partial(shrink_kernel, down_w),
        out_shape=[
            shape((mine, model), LOW), shape((mine, model), FULL), shape((mine, model), LOW), shape((8, model), FULL),
        ],
        grid=(chunks,),
        in_specs=[
            IN_SMEM, chunk_block, full_rows, fixed((16, model)), full_rows, fixed((mine, LANES)),
        ] + [ANYWHERE] * len(down_w.arrays),
        out_specs=[full_rows, full_rows, full_rows, fixed((8, model))],
        scratch_shapes=[
            pltpu.VMEM((parts, model, wide_three), LOW),
            pltpu.VMEM((mine, model), FULL),
            pltpu.SemaphoreType.DMA((down_w.count(),)),
        ],
        compiler_params=params(1),
        cost_estimate=cost(5 * dot_cost, 16 * MIB),
        name="shrink",
    )(gate, active, normed, small, cot, live_rows, *down_w.arrays)
    def shrink_grad(sides, ready):
        exits = plan.exits(sides)
        if plan.flat:
            grad_block = [pl.BlockSpec((1, model, CHUNK), lambda i: (i // per, 0, i % per))]
        else:
            grad_block = [
                pl.BlockSpec((plan.outers, 1, rows, CHUNK), lambda i: (0, i // per, 0, i % per))
            ] * len(sides)
        return pl.pallas_call(
            functools.partial(shrink_grad_kernel, exits),
            out_shape=exits.shapes(parts, hidden),
            grid=(chunks,),
            in_specs=[IN_SMEM, full_rows, chunk_block],
            out_specs=grad_block,
            scratch_shapes=[pltpu.VMEM((model, mine), LOW), pltpu.VMEM((exits.height(), mine), LOW)],
            compiler_params=params(1),
            cost_estimate=cost(4 * dot_cost // (3 - len(sides)), 9 * MIB),
            name="shrink_grad",
        )(table, ready, active)

    if plan.flat:
        three_red = Reduction(plan, names, *shrink_grad((0, 1), second_low))
    else:
        (send,) = shrink_grad((1,), second_low)
        second_low, send = hold(second_low, send)
        (keep,) = shrink_grad((0,), second_low)
        three_red = Reduction(plan, names, keep, send)
    second_low, away, layer_rows = hold(second_low, three_red.ready(), layer_rows)
    three_red.launch(away)
    layer_got = plan.release([layer_rows[:block], layer_rows[block:]])

    exits = plan.exits()
    grad_shapes = exits.shapes(parts, wide_two)
    first_grad, first_low, attended_grad, vec_one, expand_sums, *blocks = pl.pallas_call(
        functools.partial(middle_kernel, up_w, down_w, exits),
        out_shape=[
            shape((mine, model), FULL), shape((mine, model), LOW), shape((mine, model), LOW),
            shape((8, model), FULL), shape((8, model), FULL),
        ] + grad_shapes,
        grid=(chunks,),
        in_specs=[
            IN_SMEM, full_rows, full_rows, chunk_block, full_rows, full_rows, fixed((mine, LANES)),
            fixed((16, model)), full_rows,
        ] + [ANYWHERE] * (len(up_w.arrays) + len(down_w.arrays)),
        out_specs=[full_rows, full_rows, full_rows, fixed((8, model)), fixed((8, model))]
        + [fixed(g.shape) for g in grad_shapes],
        scratch_shapes=[
            pltpu.VMEM((parts, model, edge), LOW),
            pltpu.VMEM((parts, model, wide_three), LOW),
            pltpu.SemaphoreType.DMA((up_w.count(),)),
            pltpu.SemaphoreType.DMA((down_w.count(),)),
            pltpu.VMEM((model, mine), LOW),
            pltpu.VMEM((model, mine), LOW),
            pltpu.VMEM((mine, model), FULL),
        ],
        compiler_params=params(1),
        cost_estimate=cost(14 * dot_cost, 30 * MIB),
        name="middle",
    )(
        table, second_low, normed_low, slope, second_grad, unit, inv, small, attended,
        *up_w.arrays, *down_w.arrays,
    )
    two_red = Reduction(plan, names, *blocks)
    gate = pace(table, first_low, *three_red.terms[2:], *layer_got)
    gate, attended_grad, two_red.terms, three_red.terms, layer_got = hold(
        gate, attended_grad, two_red.terms, three_red.terms, layer_got
    )
    attended_grad, away, sent = hold(attended_grad, two_red.ready(), three_red.turns())
    two_red.launch(away[:-1])
    three_red.launch_turns(sent)

    few_pairs = pairs // 2

    def attend_back(lot, grad, weight):
        first = lot[0] * width // LANES
        wide = len(lot) * width

        def from_block(offset):
            return pl.BlockSpec((mine, LANES), lambda i: (0, i + first + offset))

        lot_block = pl.BlockSpec((mine, LANES), lambda i: (0, i))
        return pl.pallas_call(
            functools.partial(attend_back_kernel, first),
            out_shape=[
                shape((mine, wide), LOW), shape((8, wide), FULL), shape((mine, wide), FULL),
                shape((mine, wide), FULL), shape((mine, 2 * wide), LOW),
            ],
            grid=(few_pairs,),
            in_specs=[
                from_block(0), from_block(0), from_block(0), from_block(0), from_block(0),
                from_block(pairs), from_block(pairs), fixed((all_rows, HD)), fixed((mine, HD)),
                fixed((pad_heads, mine)),
            ],
            out_specs=[
                lot_block, pl.BlockSpec((8, LANES), lambda i: (0, i)), lot_block, lot_block,
                pl.BlockSpec((mine, 2 * LANES), lambda i: (0, i)),
            ],
            compiler_params=params(1),
            cost_estimate=cost(10 * heads * score_cost, 8 * MIB, heads * mine * all_rows // 2, weight),
            name="attend_back",
        )(
            query, grad, attended, key_value, other, key_value, other, extra_k, extra_q, log_total,
        )

    def weight_step(lot, got):
        exits = plan.exits()
        grad_shapes = exits.shapes(len(lot), wide_one)
        return pl.pallas_call(
            functools.partial(weight_kernel, exits, lot),
            out_shape=grad_shapes,
            in_specs=[IN_SMEM] + [IN_VMEM] * 10,
            out_specs=[IN_VMEM] * len(grad_shapes),
            scratch_shapes=[
                pltpu.VMEM((LANES, model), FULL),
                pltpu.VMEM((model, mine), LOW),
                pltpu.VMEM((model, mine), LOW),
                pltpu.VMEM((model, LANES), FULL),
                pltpu.VMEM((model, LANES), FULL),
            ],
            compiler_params=params(),
            cost_estimate=cost(2 * dot_cost, 9 * MIB, 0, 0.05),
            name="weight_grad",
        )(table, x, *got, vec_one, vec_two, expand_sums, pick)

    def last_step(gate, lots, gots):
        exits = plan.exits()
        grad_shapes = exits.shapes(len(lots[-1]), wide_one)
        return pl.pallas_call(
            functools.partial(last_kernel, qkv_w, exits, lots),
            out_shape=[shape((mine, model), LOW)] + grad_shapes,
            in_specs=[IN_SMEM] + [IN_VMEM] * (6 + 5 * len(lots)) + [ANYWHERE] * len(qkv_w.arrays),
            out_specs=[IN_VMEM] * (1 + len(grad_shapes)),
            scratch_shapes=[
                pltpu.VMEM((parts, model, wide_one), LOW),
                pltpu.VMEM((LANES, model), FULL),
                pltpu.VMEM((model, mine), LOW),
                pltpu.VMEM((model, mine), LOW),
                pltpu.VMEM((model, LANES), FULL),
                pltpu.VMEM((model, LANES), FULL),
                pltpu.SemaphoreType.DMA((qkv_w.count(),)),
            ],
            compiler_params=params(),
            cost_estimate=cost(6 * dot_cost, 20 * MIB),
            name="input_grad",
        )(
            gate, x, first_grad, vec_one, vec_two, expand_sums, pick, *[v for g in gots for v in g],
            *qkv_w.arrays,
        )

    def cross(got):
        return *got[:-1], plan.swap(got[-1], 1)

    high = attend_back(high_names, attended_grad, 20)
    high, attended_grad, far, three_red.terms = hold(high, attended_grad, away[-1:], three_red.terms)
    two_red.launch(far, plan.outers - 1)
    high = cross(high)
    low = cross(attend_back(low_names, attended_grad, 20))
    blocks = weight_step(high_names, high)
    high_red = Reduction(plan, high_names, *blocks)
    gate = pace(gate, blocks[0], low[0], *two_red.terms[2:])
    gate, two_red.terms, high_red.terms = hold(gate, two_red.terms, high_red.terms)
    gate, away, sent = hold(gate, high_red.ready(), two_red.turns())
    high_red.launch(away[:-1])
    two_red.launch_turns(sent)
    input_grad, *blocks = last_step(gate, (high_names, low_names), (high, low))
    input_grad, blocks, two_red.terms, high_red.terms, far = hold(
        input_grad, blocks, two_red.terms, high_red.terms, away[-1:]
    )
    low_red = Reduction(plan, low_names, *blocks)
    high_red.launch(far, plan.outers - 1)
    input_got = plan.release([input_grad[:block], input_grad[block:]])
    gate = pace(gate, blocks[0])
    gate, low_red.terms = hold(gate, low_red.terms)
    low_red.launch(low_red.ready())
    high_red.launch_turns(high_red.turns())
    sent, two_red.terms, three_red.terms, layer_got = hold(
        low_red.turns(), two_red.terms, three_red.terms, layer_got
    )
    low_red.launch_turns(sent)
    sums_two = two_red.total()
    input_got, layer_out, *done = hold(
        input_got, plan.settle(*layer_got), sums_two[:, hidden:].T, sums_two[:, :hidden], three_red.total().T
    )
    input_rows = plan.settle(*input_got).astype(FULL)
    sums_one = high_red.total() + low_red.total()
    sums_one += jnp.minimum(gate[0, 0], 0).astype(FULL)
    quarter = rows // parts
    own = lax.dynamic_slice_in_dim(sums_one[:, three : three + 6], plan.place * quarter, quarter, 0)
    return (
        layer_out[:, None],
        input_rows[:, None],
        sums_one[:, :width],
        sums_one[:, width : 2 * width],
        sums_one[:, 2 * width : three],
        *done,
        sums_one[:few, three + 7],
        sums_one[few : 2 * few, three + 7],
        sums_one[:, three + 6],
        own[:, 0],
        own[:, 1],
        own[:, 2],
        own[:, 3],
        own[:, 4],
        own[:, 5],
    )


def solution(mesh):
    rows = P(None, "fsdp", "tensor", None)
    split = P("fsdp", "tensor")
    turned = P("tensor", "fsdp")
    heads = P(("tensor", "fsdp"))
    model = P("fsdp")
    spread = P(("fsdp", "tensor"))
    return jax.shard_map(
        shards,
        mesh=mesh,
        in_specs=(rows, P(None, "fsdp"), rows, split, split, split, turned, split, turned)
        + (heads,) * 3
        + (model,) * 6,
        out_specs=(rows, rows, split, split, split, turned, split, turned)
        + (heads,) * 3
        + (spread,) * 6,
        check_vma=False,
    )
```
